32 devices in a mesh: blk: 8 (over y, x, core), expert: 4 (over z).
Axes of the slice: x: 2, y: 2, z: 4, core: 2. Of those that a mesh axis runs over, the one named last changes fastest.
Arguments:
- residual: bfloat16 [2048, 4096], P('blk', 'expert'), may hold values from -3 to 3
- queries: bfloat16 [2048, 2048], P('blk', 'expert'), may hold values from -8 to 8
- key_cache: bfloat16 [2048, 1024], P('blk', 'expert'), may hold values from -8 to 8
- value_cache: bfloat16 [2048, 1024], P('blk', 'expert'), may hold values from -6 to 6
- segments: int32 [2048], replicated, may hold values from 0 to 3, never falling along the last dimension, each value on 1 to 1536 neighbouring positions
- routes: int32 [2048, 2], P('blk'), may hold values from 0 to 3, all different within a row; in each aligned block of 256 rows (0 to 255, 256 to 511, ...) at most 144 rows name the same one
- w_out: bfloat16 [2048, 4096], P('expert'), may hold values from -0.125 to 0.125
- norm_gain: float32 [4096], replicated, may hold values from 0.5 to 1.5
- w_router: bfloat16 [4096, 4], replicated, may hold values from -0.09375 to 0.09375
- w_gate: bfloat16 [4, 4096, 14336], P('expert', None, 'blk'), may hold values from -0.09375 to 0.09375
- w_up: bfloat16 [4, 4096, 14336], P('expert', None, 'blk'), may hold values from -0.09375 to 0.09375
- w_down: bfloat16 [4, 14336, 4096], P('expert', 'blk'), may hold values from -0.046875 to 0.046875
Outputs:
- layer_out: bfloat16 [2048, 4096], P(('blk', 'expert'))
The draws below stay inside these ranges and needn't reach their ends.
Inputs may be any that keep to these rules, and one draw needn't show every extreme that they name: `segments`: segment ids never fall; one document holds exactly 1536 tokens and none holds more. `routes`: A token's 2 experts differ. In each aligned block of 256 rows (the tokens of one index of blk) no expert is named by more than 144 rows, a bound that some block reaches.
All inputs are finite; a program needn't handle non-finite values.
Results may differ from the reference program's by a relative error of at most 0.019.
Values may be sent and summed in bfloat16 or wider, within the bound.
A program may use at most 192 MiB of HBM per device.

```python
import math
import jax
import jax.numpy as jnp
import numpy as np
from jax import lax

D = 4096
H = 16
KVH = 8
HD = 128
FF = 14336
TOP = 2
S_BLK = 256
SEGS = 4
EXPERTS = 4
TOKENS = 2048
LONGEST = 1536
CAP = 144
N_BLK = 8


def draw_queries(key, part):
    values_out = 1.5 * jax.random.normal(jax.random.fold_in(key, 22), (TOKENS, H * HD), jnp.float32)
    return jnp.clip(values_out, -8.0, 8.0).astype(jnp.bfloat16)


def draw_key_cache(key, part):
    values_out = 1.2 * jax.random.normal(jax.random.fold_in(key, 33), (TOKENS, KVH * HD), jnp.float32)
    return jnp.clip(values_out, -8.0, 8.0).astype(jnp.bfloat16)


def block_levels(stream_key, dims, shards, least, largest):
    def one(dim, blocks):
        steps = jax.random.uniform(jax.random.fold_in(jax.random.fold_in(stream_key, 6), dim), (blocks,), jnp.float32, least / len(shards), largest / len(shards))
        return jnp.repeat(jnp.exp(steps), dims[dim] // blocks).reshape((-1,) + (1,) * (len(dims) - dim - 1))

    loudness = one(*shards[0])
    for cut in shards[1:]:
        loudness = loudness * one(*cut)
    return loudness


def profile(number_of, total, bound, lean):
    loads = [(1 << 20) // math.isqrt(standing ** lean) + 1 for standing in range(2, number_of + 1)]
    rest, given = total - bound - (number_of - 1), [1] * (number_of - 1)
    while rest > 0:
        movable = [i for i in range(number_of - 1) if given[i] < bound]
        pool, left = sum([loads[i] for i in movable]), rest
        for i in movable:
            addition = min(bound - given[i], max(1, left * loads[i] // pool), rest)
            given[i] = given[i] + addition
            rest = rest - addition
    return np.array([bound] + given)


def uneven(rng, count, total, most, slope):
    if count == 2:
        one = jax.random.randint(rng, (), max(1, total - most), min(most, total - 1) + 1)
        return jnp.stack([one, total - one])
    sizes = jnp.asarray(profile(count, total, most, slope), jnp.int32)
    couples = (count - 1) // 2
    donor, sink = sizes[1:1 + 2 * couples:2], sizes[2:2 + 2 * couples:2]
    room = jnp.minimum(donor - 1, most - sink)
    passed = jax.random.randint(jax.random.fold_in(rng, 1), (couples,), 0, 1 << 20) % (room + 1)
    sizes = sizes.at[1:1 + 2 * couples:2].set(donor - passed).at[2:2 + 2 * couples:2].set(sink + passed)
    return sizes[jax.random.permutation(jax.random.fold_in(rng, 2), count)]


def deal_out(own_key, own, number, rows, count, top, most, lean):
    sequence = jax.random.permutation(own_key, count)
    packed, ordinary = load_shares(count, rows * top, most, lean, True), load_shares(count, rows * top, most, lean, False)
    places = jnp.arange(count)

    def named(tallies, turn):
        used = int((tallies > 0).sum())
        fixed = max(1, used // 4)
        moved = fixed + (places - fixed + turn * (used - fixed)) % max(1, count - fixed)
        return jnp.zeros((count,), jnp.int32).at[sequence[jnp.where(places < fixed, places, moved)]].set(jnp.asarray(tallies, jnp.int32))

    tallies = jnp.where(number % 4 == 0, named(packed, number // 4), named(ordinary, number - number // 4 - 1))
    mixed = jax.random.permutation(jax.random.fold_in(own, 3), count)
    source_of, sink = mixed[0:count // 2 * 2:2], mixed[1:count // 2 * 2:2]
    margin = jnp.minimum(tallies[source_of] - 1, most - tallies[sink]) // 2
    margin = jnp.where((source_of == sequence[0]) | (sink == sequence[0]) | (tallies[sink] == 0), 0, jnp.maximum(margin, 0))
    moved = jax.random.randint(jax.random.fold_in(own, 4), (count // 2,), 0, 1 << 20) % (margin + 1)
    tallies = tallies.at[source_of].add(-moved).at[sink].add(moved)
    members = jnp.searchsorted(jnp.cumsum(tallies), jnp.arange(rows * top), side="right").astype(jnp.int32)
    grid = members.reshape(top, rows).T
    grid = grid[jax.random.permutation(jax.random.fold_in(own, 1), rows)]
    turn = jax.random.randint(jax.random.fold_in(own, 2), (rows, 1), 0, top)
    return jnp.take_along_axis(grid, (jnp.arange(top)[None, :] + turn) % top, axis=1)


def load_shares(number_of, total, most, lean, full):
    loads = [(1 << 20) // math.isqrt(grade ** lean) + 1 for grade in range(1, number_of + 1)]
    largest = most if full else min(most, max(-(-total // number_of), total * loads[0] // sum(loads)))
    least = 1 if total - largest >= number_of - 1 else 0
    counts, surplus = [largest] + [least] * (number_of - 1), total - largest - least * (number_of - 1)
    while surplus > 0:
        candidates = [i for i in range(1, number_of) if counts[i] < largest] or [i for i in range(1, number_of) if counts[i] < most]
        pool, budget = sum([loads[i] for i in candidates]), surplus
        for i in candidates:
            addition = min(most - counts[i], max(1, budget * loads[i] // pool), surplus)
            counts[i] = counts[i] + addition
            surplus = surplus - addition
    return np.array(counts)


def bell_draw(rng, extent, spread, reach, pieces=(), held_as=jnp.bfloat16):
    result = jax.random.normal(rng, extent, jnp.float32) * spread
    if len(pieces) > 0:
        result = block_levels(rng, extent, pieces, -0.22, 0.18) * result
    return jnp.clip(result, min=-reach, max=reach).astype(held_as)


def setup_inputs(seed: int = 0) -> dict:
    keys = jax.random.split(jax.random.key(seed), 13)
    residual = bell_draw(keys[0], (TOKENS, D), 0.5, 3.0, ((0, 8), (1, 4)))
    queries = draw_queries(jax.random.fold_in(keys[12], 71), 0)
    key_cache = draw_key_cache(jax.random.fold_in(keys[12], 71), 0)
    value_cache = bell_draw(keys[3], (TOKENS, KVH * HD), 1.0, 6.0, ((0, 8), (1, 4)))
    segments = jnp.searchsorted(jnp.cumsum(uneven(keys[4], SEGS, TOKENS, LONGEST, 2)), jnp.arange(TOKENS), side="right").astype(jnp.int32)
    routes_keys = jax.random.split(jax.random.fold_in(keys[5], 1), TOKENS // S_BLK)
    routes_turns = jax.random.permutation(jax.random.fold_in(keys[5], 3), TOKENS // S_BLK)
    routes = jax.vmap(lambda own, number: deal_out(jax.random.fold_in(keys[5], 2), own, number, S_BLK, EXPERTS, TOP, CAP, 1))(routes_keys, routes_turns).reshape((TOKENS, TOP))
    w_out = bell_draw(keys[6], (H * HD, D), (H * HD) ** -0.5, 0.125, ((0, 4),))
    norm_gain = jnp.clip(1.0 + 0.1 * jax.random.normal(keys[7], (D,), jnp.float32), 0.5, 1.5)
    w_router = bell_draw(keys[8], (D, EXPERTS), D ** -0.5, 0.09375)
    w_gate = bell_draw(keys[9], (EXPERTS, D, FF), D ** -0.5, 0.09375, ((0, 4), (2, 8)))
    w_up = bell_draw(keys[10], (EXPERTS, D, FF), D ** -0.5, 0.09375, ((0, 4), (2, 8)))
    w_down = bell_draw(keys[11], (EXPERTS, FF, D), FF ** -0.5, 0.046875, ((0, 4), (1, 8)))
    return dict(residual=residual, queries=queries, key_cache=key_cache, value_cache=value_cache, segments=segments, routes=routes, w_out=w_out, norm_gain=norm_gain, w_router=w_router, w_gate=w_gate, w_up=w_up, w_down=w_down)


def attend_head(operands, allowed):
    q_group, k_group, v_group = operands
    score_scale = 1.0 / math.sqrt(HD)
    scores = jnp.einsum('tgd,sd->gts', q_group.astype(jnp.float32), k_group.astype(jnp.float32)) * score_scale
    masked = jnp.where(allowed[None, :, :], scores, -1e+30)
    row_max = lax.optimization_barrier(jnp.max(masked, axis=-1, keepdims=True))
    weights = jnp.where(allowed[None, :, :], jnp.exp(masked - row_max), 0.0)
    denominator = lax.optimization_barrier(jnp.sum(weights, axis=-1))
    weight_low = weights.astype(jnp.bfloat16)
    summed = jnp.einsum('gts,sd->tgd', weight_low.astype(jnp.float32), v_group.astype(jnp.float32))
    return (summed / jnp.transpose(denominator)[:, :, None]).astype(jnp.bfloat16)

def reference(residual, queries, key_cache, value_cache, segments, routes, w_out, norm_gain, w_router, w_gate, w_up, w_down):
    q_per_kv = H // KVH
    position = jnp.arange(TOKENS, dtype=jnp.int32)
    allowed = (segments[:, None] == segments[None, :]) & (position[None, :] <= position[:, None])
    q_four = jnp.transpose(queries.reshape(TOKENS, KVH, q_per_kv, HD), (1, 0, 2, 3))
    k_three = jnp.transpose(key_cache.reshape(TOKENS, KVH, HD), (1, 0, 2))
    v_three = jnp.transpose(value_cache.reshape(TOKENS, KVH, HD), (1, 0, 2))
    attended = lax.map(partial_attend(allowed), (q_four, k_three, v_three))
    attended = jnp.transpose(attended, (1, 0, 2, 3)).reshape(TOKENS, H * HD)
    stream = residual.astype(jnp.float32) + jnp.dot(attended, w_out, preferred_element_type=jnp.float32)
    normed = (stream * lax.rsqrt(lax.optimization_barrier(jnp.mean(stream * stream, axis=-1, keepdims=True)) + 1e-05) * norm_gain).astype(jnp.bfloat16)
    gate_score = jax.nn.sigmoid(jnp.dot(normed, w_router, preferred_element_type=jnp.float32))
    chosen = jnp.take_along_axis(gate_score, routes, axis=1)
    mixing = chosen / lax.optimization_barrier(jnp.sum(chosen, axis=-1, keepdims=True))
    ff_part = FF // N_BLK
    slot_count = N_BLK * CAP
    slot_base = (jnp.arange(N_BLK, dtype=jnp.int32) * CAP)[:, None]
    mixture = jnp.zeros((TOKENS, D), jnp.float32)
    for expert_id in range(EXPERTS):
        chosen_here = routes == expert_id
        routed = jnp.any(chosen_here, axis=-1)
        share_w = lax.optimization_barrier(jnp.sum(jnp.where(chosen_here, mixing, 0.0), axis=-1))
        slot_index = (jnp.cumsum(routed.reshape(N_BLK, S_BLK).astype(jnp.int32), axis=1) - 1 + slot_base).reshape(TOKENS)
        target = jnp.where(routed, slot_index, slot_count).astype(jnp.int32)
        token_slot = jnp.zeros((slot_count,), jnp.int32).at[target].set(position, mode='drop')
        gathered = normed[token_slot]
        gate = jnp.dot(gathered, w_gate[expert_id], preferred_element_type=jnp.float32)
        up_proj = jnp.dot(gathered, w_up[expert_id], preferred_element_type=jnp.float32)
        hidden = (jax.nn.silu(gate) * up_proj).astype(jnp.bfloat16)
        partials = jnp.einsum('rnf,nfd->nrd', hidden.reshape(slot_count, N_BLK, ff_part).astype(jnp.float32), w_down[expert_id].reshape(N_BLK, ff_part, D).astype(jnp.float32))
        rounded = lax.optimization_barrier(partials.astype(jnp.bfloat16)).astype(jnp.float32)
        expert_out = lax.optimization_barrier(jnp.sum(rounded, axis=0))
        picked = jnp.clip(slot_index, 0, slot_count - 1).astype(jnp.int32)
        mixture = mixture + share_w[:, None] * expert_out[picked]
    return (stream + mixture).astype(jnp.bfloat16)

def partial_attend(allowed):

    def attend_one(operands):
        return attend_head(operands, allowed)
    return attend_one
```

```python
import functools
import math

import jax
import jax.numpy as jnp
from jax import lax
from jax.experimental import pallas as pl
from jax.experimental.pallas import tpu as pltpu
from jax.sharding import PartitionSpec as P

H = 16
KVH = 8
HD = 128
TOP = 2

MESH = pl.DeviceIdType.MESH


def remote(src, dst, send_sem, recv_sem, target, axis="blk"):
    return pltpu.make_async_remote_copy(
        src_ref=src,
        dst_ref=dst,
        send_sem=send_sem,
        recv_sem=recv_sem,
        device_id={axis: target},
        device_id_type=MESH,
    )


def enter(chips, chip, core, experts=1):
    barrier = pltpu.get_barrier_semaphore()
    if chips > 0:
        pl.semaphore_signal(
            barrier, inc=1, device_id={"blk": chip * 2 + 1 - core}, device_id_type=MESH
        )
    for j in range(1, chips):
        other = (chip + j) % chips
        pl.semaphore_signal(barrier, inc=1, device_id={"blk": other * 2 + core}, device_id_type=MESH)
    for k in range(1, experts):
        other = (lax.axis_index("expert") + k) % experts
        pl.semaphore_signal(barrier, inc=1, device_id={"expert": other}, device_id_type=MESH)
    pl.semaphore_wait(barrier, chips + experts - 1)


def gather_kernel(
    chips, experts, k_ref, v_ref, w_ref, ko_ref, vo_ref, wo_ref,
    send, recv, fsend, frecv, local, wsend, wrecv,
):
    me = lax.axis_index("blk")
    chip, core = me // 2, me % 2
    sibling = chip * 2 + 1 - core
    pairs = ((k_ref, ko_ref), (v_ref, vo_ref))
    group = lax.axis_index("expert")
    enter(chips, chip, core, experts)
    out = []
    part, cols = wo_ref.shape[1], wo_ref.shape[2]
    mine = pl.ds(pl.multiple_of(me * part, part), part)

    def piece(k):
        target = (group + k) % experts
        return w_ref.at[mine, pl.ds(pl.multiple_of(target * cols, 128), cols)]

    def lend(k):
        return remote(
            piece(k), wo_ref.at[group], wsend.at[k], wrecv.at[k], (group + k) % experts, "expert"
        )

    for k in range(1, experts):
        lend(k).start()
    for j in range(1, chips):
        for i, (src, dst) in enumerate(pairs):
            out.append(
                remote(src, dst.at[me], send.at[i, j], recv.at[i, j], (chip + j) % chips * 2 + core)
            )
            out[-1].start()
    for i, (src, dst) in enumerate(pairs):
        out.append(remote(src, dst.at[me], fsend.at[i, 0], frecv.at[i, 0], sibling))
        out[-1].start()
    own = [pltpu.make_async_copy(src, dst.at[me], local.at[i]) for i, (src, dst) in enumerate(pairs)]
    own.append(pltpu.make_async_copy(piece(0), wo_ref.at[group], local.at[2]))
    for copy in own:
        copy.start()
    for j in range(1, chips):
        origin = (chip + chips - j) % chips * 2 + core
        for i, (src, dst) in enumerate(pairs):
            remote(src, dst.at[origin], send.at[i, j], recv.at[i, j], sibling).wait_recv()
            out.append(
                remote(dst.at[origin], dst.at[origin], fsend.at[i, j], frecv.at[i, j], sibling)
            )
            out[-1].start()
    for j in range(chips):
        origin = (chip + chips - j) % chips * 2 + 1 - core
        for i, (src, dst) in enumerate(pairs):
            remote(src, dst.at[origin], fsend.at[i, j], frecv.at[i, j], sibling).wait_recv()
    for copy in own:
        copy.wait()
    for k in range(1, experts):
        origin = (group + experts - k) % experts
        remote(
            piece(k), wo_ref.at[origin], wsend.at[k], wrecv.at[k], (group + k) % experts, "expert"
        ).wait_recv()
        lend(k).wait_send()
    for copy in out:
        copy.wait_send()


def gather_blocks(keys, values, w_out):
    blocks, experts = lax.axis_size("blk"), lax.axis_size("expert")
    chips = blocks // 2
    vmem = pl.BlockSpec(memory_space=pltpu.VMEM)
    shape = jax.ShapeDtypeStruct((blocks,) + keys.shape, keys.dtype)
    wshape = jax.ShapeDtypeStruct(
        (experts, w_out.shape[0] // blocks, w_out.shape[1] // experts), w_out.dtype
    )
    dma = pltpu.SemaphoreType.DMA
    k_all, v_all, w_part = pl.pallas_call(
        functools.partial(gather_kernel, chips, experts),
        out_shape=(shape, shape, wshape),
        in_specs=[vmem, vmem, pl.BlockSpec(memory_space=pl.ANY)],
        out_specs=(vmem, vmem, vmem),
        scratch_shapes=[dma((2, chips)), dma((2, chips)), dma((2, chips)), dma((2, chips)), dma((3,))]
        + [dma((experts,)), dma((experts,))],
        compiler_params=pltpu.CompilerParams(collective_id=0, has_side_effects=True),
    )(keys, values, w_out)
    rows = blocks * keys.shape[0]
    return k_all.reshape(rows, keys.shape[1]), v_all.reshape(rows, keys.shape[1]), w_part


def heads_kernel(experts, x_ref, o_ref, send, recv, local):
    group = lax.axis_index("expert")
    cols = x_ref.shape[1]

    def place(g):
        return o_ref.at[:, pl.ds(pl.multiple_of(g * cols, 128), cols)]

    def push(k, slot):
        return remote(
            x_ref, place(slot), send.at[k], recv.at[k], (group + k) % experts, "expert"
        )

    enter(0, 0, 0, experts)
    for k in range(experts - 1, 0, -1):
        push(k, group).start()
    own = pltpu.make_async_copy(x_ref, place(group), local)
    own.start()
    own.wait()
    for k in range(1, experts):
        push(k, (group + experts - k) % experts).wait_recv()
        push(k, group).wait_send()


def gather_heads(attended):
    experts = lax.axis_size("expert")
    vmem = pl.BlockSpec(memory_space=pltpu.VMEM)
    dma = pltpu.SemaphoreType.DMA
    rows, cols = attended.shape
    return pl.pallas_call(
        functools.partial(heads_kernel, experts),
        out_shape=jax.ShapeDtypeStruct((rows, cols * experts), attended.dtype),
        in_specs=[vmem],
        out_specs=vmem,
        scratch_shapes=[dma((experts,)), dma((experts,)), dma],
        compiler_params=pltpu.CompilerParams(collective_id=2, has_side_effects=True),
    )(attended)


def mix_kernel(
    experts, att_ref, w_ref, res_ref, gain_ref, router_ref, place_ref, stream_ref, buf_ref, logit_ref,
    squares, logits, chosen, s_send, s_recv, l_send, l_recv, d_send, d_recv,
):
    group = lax.axis_index("expert")
    rows, cols = res_ref.shape

    def target(k):
        return (group + k) % experts

    def share_squares(k):
        return remote(
            squares.at[0], squares.at[k], s_send.at[k], s_recv.at[k], target(k), "expert"
        )

    def share_logits(k):
        return remote(logits.at[0], logits.at[k], l_send.at[k], l_recv.at[k], target(k), "expert")

    def slot(g):
        return pl.ds(pl.multiple_of(g * cols, 128), cols)

    def dispatch(k, g):
        return remote(
            chosen.at[k], buf_ref.at[:, slot(g)], d_send.at[k], d_recv.at[k], target(k), "expert"
        )

    stream = res_ref[...].astype(jnp.float32) + jnp.dot(
        att_ref[...], w_ref[...], preferred_element_type=jnp.float32
    )
    stream_ref[...] = stream
    total = jnp.sum(stream * stream, axis=-1, keepdims=True)
    squares[0] = jnp.transpose(jnp.broadcast_to(total, (rows, 128)))[:8, :]
    enter(0, 0, 0, experts)
    for k in range(1, experts):
        share_squares(k).start()
    for k in range(1, experts):
        share_squares(k).wait_recv()
    total = squares[0]
    for k in range(1, experts):
        total = total + squares[k]
    total = jnp.transpose(jnp.broadcast_to(total[:1, :], (128, rows)))[:, :1]
    scale = lax.rsqrt(total * (1.0 / (cols * experts)) + 1e-05)
    normed = (stream_ref[...] * scale * gain_ref[...]).astype(jnp.bfloat16)
    for k in range(experts - 1, 0, -1):
        chosen[k] = jnp.dot(
            place_ref[target(k)], normed, preferred_element_type=jnp.float32
        ).astype(jnp.bfloat16)
        dispatch(k, group).start()
    logits[0] = lax.dot_general(
        router_ref[...], normed, (((1,), (1,)), ((), ())), preferred_element_type=jnp.float32
    )
    for k in range(1, experts):
        share_logits(k).start()
    buf_ref[:, slot(group)] = jnp.dot(
        place_ref[group], normed, preferred_element_type=jnp.float32
    ).astype(jnp.bfloat16)
    for k in range(1, experts):
        share_logits(k).wait_recv()
    total = logits[0]
    for k in range(1, experts):
        total = total + logits[k]
    logit_ref[...] = total
    for k in range(1, experts):
        dispatch(k, target(experts - k)).wait_recv()
    for k in range(1, experts):
        share_squares(k).wait_send()
        share_logits(k).wait_send()
        dispatch(k, group).wait_send()


def mix_columns(attended, w_cols, residual, gain, router, placing):
    experts = lax.axis_size("expert")
    rows, cols = residual.shape
    capacity = placing.shape[1]
    vmem = pl.BlockSpec(memory_space=pltpu.VMEM)
    dma = pltpu.SemaphoreType.DMA
    shape = jax.ShapeDtypeStruct
    return pl.pallas_call(
        functools.partial(mix_kernel, experts),
        out_shape=(
            shape((rows, cols), jnp.float32),
            shape((capacity, cols * experts), jnp.bfloat16),
            shape((router.shape[0], rows), jnp.float32),
        ),
        in_specs=[vmem] * 6,
        out_specs=(vmem, vmem, vmem),
        scratch_shapes=[
            pltpu.VMEM((experts, 8, rows), jnp.float32),
            pltpu.VMEM((experts, router.shape[0], rows), jnp.float32),
            pltpu.VMEM((experts, capacity, cols), jnp.bfloat16),
        ]
        + [dma((experts,)) for _ in range(6)],
        compiler_params=pltpu.CompilerParams(
            collective_id=3, has_side_effects=True, vmem_limit_bytes=40 * 1024 * 1024
        ),
    )(attended, w_cols, residual, gain, router, placing)


def combine_kernel(
    experts, eo_ref, stream_ref, place_ref, share_ref, o_ref,
    low, arrived, final, e_send, e_recv, f_send, f_recv, local,
):
    group = lax.axis_index("expert")
    rows, cols = stream_ref.shape
    own_rows = rows // experts

    def target(k):
        return (group + k) % experts

    def slot(g):
        return pl.ds(pl.multiple_of(g * cols, 128), cols)

    def strip(g):
        return pl.ds(pl.multiple_of(g * own_rows, own_rows), own_rows)

    def give(k, g):
        return remote(
            low.at[:, slot(target(k))], arrived.at[g], e_send.at[k], e_recv.at[k], target(k), "expert"
        )

    def finish(k, g):
        return remote(
            final.at[strip(target(k)), :], o_ref.at[:, slot(g)], f_send.at[k], f_recv.at[k],
            target(k), "expert",
        )

    low[...] = eo_ref[...].astype(jnp.bfloat16)
    enter(0, 0, 0, experts)
    for k in range(experts - 1, 0, -1):
        give(k, group).start()
    own = pltpu.make_async_copy(low.at[:, slot(group)], arrived.at[group], local.at[0])
    own.start()
    own.wait()
    for k in range(1, experts):
        give(k, target(experts - k)).wait_recv()
    total = stream_ref[...]
    for g in range(experts):
        total = total + share_ref[:, g : g + 1] * jnp.dot(
            place_ref[g], arrived[g], preferred_element_type=jnp.float32
        )
    final[...] = total.astype(jnp.bfloat16)
    for k in range(experts - 1, 0, -1):
        finish(k, group).start()
    own = pltpu.make_async_copy(final.at[strip(group), :], o_ref.at[:, slot(group)], local.at[1])
    own.start()
    own.wait()
    for k in range(1, experts):
        finish(k, target(experts - k)).wait_recv()
    for k in range(1, experts):
        give(k, group).wait_send()
        finish(k, group).wait_send()


def combine(expert_out, stream, placing, shares):
    experts = lax.axis_size("expert")
    rows, cols = stream.shape
    capacity = expert_out.shape[0]
    vmem = pl.BlockSpec(memory_space=pltpu.VMEM)
    dma = pltpu.SemaphoreType.DMA
    return pl.pallas_call(
        functools.partial(combine_kernel, experts),
        out_shape=jax.ShapeDtypeStruct((rows // experts, cols * experts), jnp.bfloat16),
        in_specs=[vmem] * 4,
        out_specs=vmem,
        scratch_shapes=[
            pltpu.VMEM((capacity, cols * experts), jnp.bfloat16),
            pltpu.VMEM((experts, capacity, cols), jnp.bfloat16),
            pltpu.VMEM((rows, cols), jnp.bfloat16),
        ]
        + [dma((experts,)) for _ in range(4)]
        + [dma((2,))],
        compiler_params=pltpu.CompilerParams(
            collective_id=4, has_side_effects=True, vmem_limit_bytes=40 * 1024 * 1024
        ),
    )(expert_out, stream, placing, shares)


def expert_kernel(
    chips,
    tiles,
    x_ref,
    wg_ref,
    wu_ref,
    wd_ref,
    o_ref,
    rows_in,
    acc,
    keep,
    leaving,
    sib_in,
    part_in,
    ag_send,
    ag_recv,
    fw_send,
    fw_recv,
    sib_send,
    sib_recv,
    rs_send,
    rs_recv,
    local,
):
    j, f = pl.program_id(0), pl.program_id(1)
    me = lax.axis_index("blk")
    chip, core = me // 2, me % 2
    sibling = chip * 2 + 1 - core
    rows, width = x_ref.shape
    mid = min(2, tiles - 1)

    def push(k):
        return remote(
            rows_in.at[0, 0], rows_in.at[k, 0], ag_send.at[k], ag_recv.at[k], (chip + k) % chips * 2 + core
        )

    def forward(k):
        return remote(rows_in.at[k, 0], rows_in.at[k, 1], fw_send.at[k], fw_recv.at[k], sibling)

    def exchange(k):
        return remote(leaving.at[k % 2], sib_in.at[k], sib_send.at[k], sib_recv.at[k], sibling)

    def deliver(k):
        return remote(
            sib_in.at[k], part_in.at[k], rs_send.at[k], rs_recv.at[k], (chip + chips - k) % chips * 2 + core
        )

    @pl.when((j == 0) & (f == 0))
    def _():
        own = pltpu.make_async_copy(x_ref, rows_in.at[0, 0], local)
        own.start()
        enter(chips, chip, core)
        own.wait()
        forward(0).start()
        for k in range(1, min(3, chips)):
            push(k).start()

    @pl.when((j >= 1) & (f == 0) & (j + 2 < chips))
    def _():
        push(j + 2).start()

    @pl.when(f == 0)
    def _():
        forward(j).wait_recv()

    tokens = rows_in[j].reshape(2 * rows, width)
    gate = jnp.dot(tokens, wg_ref[...], preferred_element_type=jnp.float32)
    up = jnp.dot(tokens, wu_ref[...], preferred_element_type=jnp.float32)
    hidden = (gate / (1.0 + jnp.exp(-gate)) * up).astype(jnp.bfloat16)
    step = 1024

    @pl.when(f == 0)
    def _():
        for c in range(0, width, step):
            acc[:, c : c + step] = jnp.dot(
                hidden, wd_ref[:, c : c + step], preferred_element_type=jnp.float32
            )

    @pl.when(f > 0)
    def _():
        for c in range(0, width, step):
            acc[:, c : c + step] += jnp.dot(
                hidden, wd_ref[:, c : c + step], preferred_element_type=jnp.float32
            )

    @pl.when((f == mid) & (j + 1 < chips))
    def _():
        push(j + 1).wait_recv()
        forward(j + 1).start()

    def settle(k):
        exchange(k).wait_recv()
        sib_in[k] = (keep[...] + sib_in[k].astype(jnp.float32)).astype(jnp.bfloat16)
        deliver(k).start()

    @pl.when((f == 1) & (j == 1))
    def _():
        exchange(0).wait_recv()
        o_ref[...] += sib_in[0].astype(jnp.float32)

    @pl.when((f == 1) & (j >= 2))
    def _():
        settle(j - 1)

    @pl.when(f == tiles - 1)
    def _():
        @pl.when(j >= 2)
        def _():
            exchange(j - 2).wait_send()

        leaving[j % 2] = acc[rows:, :].astype(jnp.bfloat16)
        exchange(j).start()

        @pl.when(j == 0)
        def _():
            o_ref[...] = acc[:rows, :]

        @pl.when(j > 0)
        def _():
            keep[...] = acc[:rows, :]

        @pl.when(j == chips - 1)
        def _():
            settle(chips - 1)
            for k in range(1, chips):
                deliver(k).wait_recv()
                o_ref[...] += part_in[k].astype(jnp.float32)
            for k in range(chips):
                forward(k).wait_send()
                if k >= 1:
                    push(k).wait_send()
                    deliver(k).wait_send()
            for k in range(max(0, chips - 2), chips):
                exchange(k).wait_send()


def expert_layer(x, gate_w, up_w, down_w):
    blocks = lax.axis_size("blk")
    chips = blocks // 2
    rows, width = x.shape
    units = gate_w.shape[1]
    tile = 256 if units % 256 == 0 else 128
    tiles = units // tile
    dma = pltpu.SemaphoreType.DMA
    low, wide = jnp.bfloat16, jnp.float32
    return pl.pallas_call(
        functools.partial(expert_kernel, chips, tiles),
        grid=(chips, tiles),
        out_shape=jax.ShapeDtypeStruct((rows, width), wide),
        in_specs=[
            pl.BlockSpec(memory_space=pl.ANY),
            pl.BlockSpec((width, tile), lambda j, f: (0, f)),
            pl.BlockSpec((width, tile), lambda j, f: (0, f)),
            pl.BlockSpec((tile, width), lambda j, f: (f, 0)),
        ],
        out_specs=pl.BlockSpec((rows, width), lambda j, f: (0, 0)),
        scratch_shapes=[
            pltpu.VMEM((chips, 2, rows, width), low),
            pltpu.VMEM((2 * rows, width), wide),
            pltpu.VMEM((rows, width), wide),
            pltpu.VMEM((2, rows, width), low),
            pltpu.VMEM((chips, rows, width), low),
            pltpu.VMEM((chips, rows, width), low),
        ]
        + [dma((chips,)) for _ in range(8)]
        + [dma],
        compiler_params=pltpu.CompilerParams(
            collective_id=1,
            has_side_effects=True,
            dimension_semantics=("arbitrary", "arbitrary"),
            vmem_limit_bytes=60 * 1024 * 1024,
        ),
    )(x, gate_w, up_w, down_w)


def on_device(
    residual,
    queries,
    key_cache,
    value_cache,
    segments,
    routes,
    w_out,
    norm_gain,
    w_router,
    w_gate,
    w_up,
    w_down,
):
    tok_rows = queries.shape[0]
    kv_heads = key_cache.shape[1] // HD
    q_per_kv = H // KVH
    seq_block = lax.axis_index("blk")
    head_group = lax.axis_index("expert")
    first_row = seq_block * tok_rows
    query_pos = first_row + jnp.arange(tok_rows, dtype=jnp.int32)
    query_seg = lax.dynamic_slice_in_dim(segments, first_row, tok_rows)
    query_four = queries.reshape(tok_rows, kv_heads, q_per_kv, HD)
    score_scale = 1.0 / math.sqrt(HD)
    running = jnp.full((kv_heads, q_per_kv, tok_rows), -1e30, jnp.float32)
    key_rows, value_rows, w_part = gather_blocks(key_cache, value_cache, w_out)
    w_cols = lax.all_gather(w_part, "blk", axis=1, tiled=True)
    w_cols = w_cols.reshape(-1, w_cols.shape[2])
    piece_len = key_rows.shape[0]
    key_pos = jnp.arange(piece_len, dtype=jnp.int32)
    visible = (query_seg[:, None] == segments[None, :]) & (key_pos[None, :] <= query_pos[:, None])
    scores = (
        jnp.einsum(
            "qkgd,skd->kgqs",
            query_four,
            key_rows.reshape(piece_len, kv_heads, HD),
            preferred_element_type=jnp.float32,
        )
        * score_scale
    )
    scores = jnp.where(visible, scores, -1e30)
    newmax = jnp.maximum(running, jnp.max(scores, axis=-1))
    weights = jnp.where(visible, jnp.exp(scores - newmax[..., None]), 0.0)
    totals = jnp.sum(weights, axis=-1)
    weighted_sum = jnp.einsum(
        "kgqs,skd->kgqd",
        weights.astype(jnp.bfloat16),
        value_rows.reshape(piece_len, kv_heads, HD),
        preferred_element_type=jnp.float32,
    )
    running, totals, weighted_sum = (newmax, totals, weighted_sum)
    attended = (
        jnp.transpose(weighted_sum / totals[..., None], (2, 0, 1, 3))
        .reshape(tok_rows, kv_heads * q_per_kv * HD)
        .astype(jnp.bfloat16)
    )
    feat_width = residual.shape[1]
    experts = w_router.shape[1]
    first_col = head_group * feat_width
    capacity = tok_rows * TOP * 9 // (8 * experts)
    capacity = -(-capacity // 16) * 16
    ids = jnp.arange(experts, dtype=jnp.int32)
    picked = routes[:, :, None] == ids[None, None, :]
    routed = jnp.any(picked, axis=1).T
    earlier = jnp.arange(tok_rows)[:, None] <= jnp.arange(tok_rows)[None, :]
    counted = jnp.dot(
        routed.astype(jnp.bfloat16), earlier.astype(jnp.bfloat16), preferred_element_type=jnp.float32
    )
    slot_index = jnp.where(routed, counted.astype(jnp.int32) - 1, -1)
    slots = jnp.arange(capacity, dtype=jnp.int32)
    placing = (slot_index[:, None, :] == slots[None, :, None]).astype(jnp.bfloat16)
    placing_back = (slot_index[:, :, None] == slots[None, None, :]).astype(jnp.bfloat16)
    router = lax.dynamic_slice_in_dim(w_router, first_col, feat_width, 0).T
    router = jnp.pad(router, ((0, -experts % 16), (0, 0)))
    gain = lax.dynamic_slice_in_dim(norm_gain, first_col, feat_width)[None, :]
    attended = gather_heads(attended)
    stream, buffer, logits = mix_columns(attended, w_cols, residual, gain, router, placing)
    gate_score = jax.nn.sigmoid(logits[:experts, :].T)
    chosen = jnp.where(routed.T, gate_score, 0.0)
    shares = chosen / jnp.sum(chosen, axis=-1, keepdims=True)
    shares = jnp.pad(shares, ((0, 0), (0, -experts % 128)))
    expert_out = expert_layer(buffer, w_gate[0], w_up[0], w_down[0])
    return combine(expert_out, stream, placing_back, shares)


def solution(mesh):
    return jax.shard_map(
        on_device,
        mesh=mesh,
        in_specs=(
            P("blk", "expert"),
            P("blk", "expert"),
            P("blk", "expert"),
            P("blk", "expert"),
            P(),
            P("blk", None),
            P("expert", None),
            P(),
            P(),
            P("expert", None, "blk"),
            P("expert", None, "blk"),
            P("expert", "blk", None),
        ),
        out_specs=P(("blk", "expert"), None),
        check_vma=False,
    )
```

```python
import functools
import math

import jax
import jax.numpy as jnp
from jax import lax
from jax.experimental import pallas as pl
from jax.experimental.pallas import tpu as pltpu
from jax.sharding import PartitionSpec as P

H = 16
KVH = 8
HD = 128
TOP = 2

MESH = pl.DeviceIdType.MESH


def remote(src, dst, send_sem, recv_sem, target, axis="blk"):
    return pltpu.make_async_remote_copy(
        src_ref=src,
        dst_ref=dst,
        send_sem=send_sem,
        recv_sem=recv_sem,
        device_id={axis: target},
        device_id_type=MESH,
    )


def enter(chips, chip, core, experts=1):
    barrier = pltpu.get_barrier_semaphore()
    if chips > 0:
        pl.semaphore_signal(
            barrier, inc=1, device_id={"blk": chip * 2 + 1 - core}, device_id_type=MESH
        )
    for j in range(1, chips):
        other = (chip + j) % chips
        pl.semaphore_signal(barrier, inc=1, device_id={"blk": other * 2 + core}, device_id_type=MESH)
    for k in range(1, experts):
        other = (lax.axis_index("expert") + k) % experts
        pl.semaphore_signal(barrier, inc=1, device_id={"expert": other}, device_id_type=MESH)
    pl.semaphore_wait(barrier, chips + experts - 1)


def gather_kernel(
    chips, experts, k_ref, v_ref, w_ref, ko_ref, vo_ref, wo_ref,
    send, recv, fsend, frecv, local, wsend, wrecv,
):
    me = lax.axis_index("blk")
    chip, core = me // 2, me % 2
    sibling = chip * 2 + 1 - core
    pairs = ((k_ref, ko_ref), (v_ref, vo_ref))
    group = lax.axis_index("expert")
    enter(chips, chip, core, experts)
    out = []
    part, cols = wo_ref.shape[1], wo_ref.shape[2]
    mine = pl.ds(pl.multiple_of(me * part, part), part)

    def piece(k):
        target = (group + k) % experts
        return w_ref.at[mine, pl.ds(pl.multiple_of(target * cols, 128), cols)]

    def lend(k):
        return remote(
            piece(k), wo_ref.at[group], wsend.at[k], wrecv.at[k], (group + k) % experts, "expert"
        )

    for k in range(1, experts):
        lend(k).start()
    for j in range(1, chips):
        for i, (src, dst) in enumerate(pairs):
            out.append(
                remote(src, dst.at[me], send.at[i, j], recv.at[i, j], (chip + j) % chips * 2 + core)
            )
            out[-1].start()
    for i, (src, dst) in enumerate(pairs):
        out.append(remote(src, dst.at[me], fsend.at[i, 0], frecv.at[i, 0], sibling))
        out[-1].start()
    own = [pltpu.make_async_copy(src, dst.at[me], local.at[i]) for i, (src, dst) in enumerate(pairs)]
    own.append(pltpu.make_async_copy(piece(0), wo_ref.at[group], local.at[2]))
    for copy in own:
        copy.start()
    for j in range(1, chips):
        origin = (chip + chips - j) % chips * 2 + core
        for i, (src, dst) in enumerate(pairs):
            remote(src, dst.at[origin], send.at[i, j], recv.at[i, j], sibling).wait_recv()
            out.append(
                remote(dst.at[origin], dst.at[origin], fsend.at[i, j], frecv.at[i, j], sibling)
            )
            out[-1].start()
    for j in range(chips):
        origin = (chip + chips - j) % chips * 2 + 1 - core
        for i, (src, dst) in enumerate(pairs):
            remote(src, dst.at[origin], fsend.at[i, j], frecv.at[i, j], sibling).wait_recv()
    for copy in own:
        copy.wait()
    for k in range(1, experts):
        origin = (group + experts - k) % experts
        remote(
            piece(k), wo_ref.at[origin], wsend.at[k], wrecv.at[k], (group + k) % experts, "expert"
        ).wait_recv()
        lend(k).wait_send()
    for copy in out:
        copy.wait_send()


def gather_blocks(keys, values, w_out):
    blocks, experts = lax.axis_size("blk"), lax.axis_size("expert")
    chips = blocks // 2
    vmem = pl.BlockSpec(memory_space=pltpu.VMEM)
    shape = jax.ShapeDtypeStruct((blocks,) + keys.shape, keys.dtype)
    wshape = jax.ShapeDtypeStruct(
        (experts, w_out.shape[0] // blocks, w_out.shape[1] // experts), w_out.dtype
    )
    dma = pltpu.SemaphoreType.DMA
    k_all, v_all, w_part = pl.pallas_call(
        functools.partial(gather_kernel, chips, experts),
        out_shape=(shape, shape, wshape),
        in_specs=[vmem, vmem, pl.BlockSpec(memory_space=pl.ANY)],
        out_specs=(vmem, vmem, vmem),
        scratch_shapes=[dma((2, chips)), dma((2, chips)), dma((2, chips)), dma((2, chips)), dma((3,))]
        + [dma((experts,)), dma((experts,))],
        compiler_params=pltpu.CompilerParams(collective_id=0, has_side_effects=True),
    )(keys, values, w_out)
    rows = blocks * keys.shape[0]
    return k_all.reshape(rows, keys.shape[1]), v_all.reshape(rows, keys.shape[1]), w_part


def heads_kernel(experts, x_ref, o_ref, send, recv, local):
    group = lax.axis_index("expert")
    cols = x_ref.shape[1]

    def place(g):
        return o_ref.at[:, pl.ds(pl.multiple_of(g * cols, 128), cols)]

    def push(k, slot):
        return remote(
            x_ref, place(slot), send.at[k], recv.at[k], (group + k) % experts, "expert"
        )

    enter(0, 0, 0, experts)
    for k in range(experts - 1, 0, -1):
        push(k, group).start()
    own = pltpu.make_async_copy(x_ref, place(group), local)
    own.start()
    own.wait()
    for k in range(1, experts):
        push(k, (group + experts - k) % experts).wait_recv()
        push(k, group).wait_send()


def gather_heads(attended):
    experts = lax.axis_size("expert")
    vmem = pl.BlockSpec(memory_space=pltpu.VMEM)
    dma = pltpu.SemaphoreType.DMA
    rows, cols = attended.shape
    return pl.pallas_call(
        functools.partial(heads_kernel, experts),
        out_shape=jax.ShapeDtypeStruct((rows, cols * experts), attended.dtype),
        in_specs=[vmem],
        out_specs=vmem,
        scratch_shapes=[dma((experts,)), dma((experts,)), dma],
        compiler_params=pltpu.CompilerParams(collective_id=2, has_side_effects=True),
    )(attended)


def mix_kernel(
    experts, att_ref, w_ref, res_ref, gain_ref, router_ref, place_ref, stream_ref, buf_ref, logit_ref,
    squares, logits, chosen, s_send, s_recv, l_send, l_recv, d_send, d_recv,
):
    group = lax.axis_index("expert")
    rows, cols = res_ref.shape

    def target(k):
        return (group + k) % experts

    def share_squares(k):
        return remote(
            squares.at[0], squares.at[k], s_send.at[k], s_recv.at[k], target(k), "expert"
        )

    def share_logits(k):
        return remote(logits.at[0], logits.at[k], l_send.at[k], l_recv.at[k], target(k), "expert")

    def slot(g):
        return pl.ds(pl.multiple_of(g * cols, 128), cols)

    def dispatch(k, g):
        return remote(
            chosen.at[k], buf_ref.at[:, slot(g)], d_send.at[k], d_recv.at[k], target(k), "expert"
        )

    stream = res_ref[...].astype(jnp.float32) + jnp.dot(
        att_ref[...], w_ref[...], preferred_element_type=jnp.float32
    )
    stream_ref[...] = stream
    total = jnp.sum(stream * stream, axis=-1, keepdims=True)
    squares[0] = jnp.transpose(jnp.broadcast_to(total, (rows, 128)))[:8, :]
    enter(0, 0, 0, experts)
    for k in range(1, experts):
        share_squares(k).start()
    for k in range(1, experts):
        share_squares(k).wait_recv()
    total = squares[0]
    for k in range(1, experts):
        total = total + squares[k]
    total = jnp.transpose(jnp.broadcast_to(total[:1, :], (128, rows)))[:, :1]
    scale = lax.rsqrt(total * (1.0 / (cols * experts)) + 1e-05)
    normed = (stream_ref[...] * scale * gain_ref[...]).astype(jnp.bfloat16)
    for k in range(experts - 1, 0, -1):
        chosen[k] = jnp.dot(
            place_ref[target(k)], normed, preferred_element_type=jnp.float32
        ).astype(jnp.bfloat16)
        dispatch(k, group).start()
    logits[0] = lax.dot_general(
        router_ref[...], normed, (((1,), (1,)), ((), ())), preferred_element_type=jnp.float32
    )
    for k in range(1, experts):
        share_logits(k).start()
    buf_ref[:, slot(group)] = jnp.dot(
        place_ref[group], normed, preferred_element_type=jnp.float32
    ).astype(jnp.bfloat16)
    for k in range(1, experts):
        share_logits(k).wait_recv()
    total = logits[0]
    for k in range(1, experts):
        total = total + logits[k]
    logit_ref[...] = total
    for k in range(1, experts):
        dispatch(k, target(experts - k)).wait_recv()
    for k in range(1, experts):
        share_squares(k).wait_send()
        share_logits(k).wait_send()
        dispatch(k, group).wait_send()


def mix_columns(attended, w_cols, residual, gain, router, placing):
    experts = lax.axis_size("expert")
    rows, cols = residual.shape
    capacity = placing.shape[1]
    vmem = pl.BlockSpec(memory_space=pltpu.VMEM)
    dma = pltpu.SemaphoreType.DMA
    shape = jax.ShapeDtypeStruct
    return pl.pallas_call(
        functools.partial(mix_kernel, experts),
        out_shape=(
            shape((rows, cols), jnp.float32),
            shape((capacity, cols * experts), jnp.bfloat16),
            shape((router.shape[0], rows), jnp.float32),
        ),
        in_specs=[vmem] * 6,
        out_specs=(vmem, vmem, vmem),
        scratch_shapes=[
            pltpu.VMEM((experts, 8, rows), jnp.float32),
            pltpu.VMEM((experts, router.shape[0], rows), jnp.float32),
            pltpu.VMEM((experts, capacity, cols), jnp.bfloat16),
        ]
        + [dma((experts,)) for _ in range(6)],
        compiler_params=pltpu.CompilerParams(
            collective_id=3, has_side_effects=True, vmem_limit_bytes=40 * 1024 * 1024
        ),
    )(attended, w_cols, residual, gain, router, placing)


def flip(index, bit):
    return index + bit * (1 - 2 * ((index // bit) % 2))


def across(index, bits):
    for bit in bits:
        index = flip(index, bit)
    return index


def log2(n):
    return n.bit_length() - 1


def parts_of(mask):
    return [1 << b for b in range(mask.bit_length()) if mask >> b & 1]


def span(order):
    found = [0]
    for bit in order:
        found += [f | bit for f in found]
    return found


def expert_kernel(
    chips, experts, x_ref, wg_ref, wu_ref, wd_ref, stream_ref, place_ref, share_ref, o_ref,
    rows_in, weights, hidden, leaving, sib_in, keep, part_in, own_out, strips, strip_in, scatter,
    local, w_sem, d_sem, ag_send, ag_recv, fw_send, fw_recv, sib_send, sib_recv,
    rs_send, rs_recv, z_send, z_recv,
):
    me, group = lax.axis_index("blk"), lax.axis_index("expert")
    chip, core = me // 2, me % 2
    sibling = chip * 2 + 1 - core
    rows, width = x_ref.shape
    units = wg_ref.shape[1]
    tile = weights.shape[2]
    tiles = units // tile
    slots = 2 * tiles
    steps, zsteps = log2(chips), log2(experts)
    bits = [1 << b for b in range(steps)]
    zbits = [1 << b for b in range(zsteps)]
    parts = 2
    orders = [bits[p % steps :] + bits[: p % steps] for p in range(parts)]
    half = width // parts
    tw = leaving.shape[2]
    pw = tw // parts
    total = width // tw
    per_tile = tw // tile
    piece = tw // experts
    subs = width // tile
    slab = width // experts
    own_rows = o_ref.shape[0]
    low = jnp.bfloat16

    def peer(bit):
        return flip(chip, bit) * 2 + core

    barrier = pltpu.get_barrier_semaphore()
    pl.semaphore_signal(barrier, inc=1, device_id={"blk": sibling}, device_id_type=MESH)
    for bit in bits:
        pl.semaphore_signal(barrier, inc=1, device_id={"blk": peer(bit)}, device_id_type=MESH)
    for bit in zbits:
        pl.semaphore_signal(barrier, inc=1, device_id={"expert": flip(group, bit)}, device_id_type=MESH)

    def load(f, side):
        src = (wg_ref, wu_ref)[side]
        return pltpu.make_async_copy(
            src.at[:, pl.ds(pl.multiple_of(f * tile, 128), tile)], weights.at[2 * f + side], w_sem.at[2 * f + side]
        )

    def load_down(m, i):
        column = (m % per_tile) * (tile // piece) + i
        column = column * slab + (m // per_tile) * piece
        slot = m % slots
        return pltpu.make_async_copy(
            wd_ref.at[:, pl.ds(pl.multiple_of(column, 128), piece)],
            weights.at[slot, pl.ds(0, units), pl.ds(i * piece, piece)],
            d_sem.at[slot, i],
        )

    def cols(p):
        return pl.ds(p * half, half)

    def spread(p, bit, r):
        return remote(
            rows_in.at[r, 0, :, cols(p)], rows_in.at[r ^ bit, 0, :, cols(p)],
            ag_send.at[p, r ^ bit], ag_recv.at[p, r ^ bit], peer(bit),
        )

    def arrived(p, r):
        spread(p, orders[p][0], r ^ orders[p][0]).wait_recv()

    def forward(p, r):
        return remote(
            rows_in.at[r, 0, :, cols(p)], rows_in.at[r, 1, :, cols(p)],
            fw_send.at[p, r], fw_recv.at[p, r], sibling,
        )

    own = pltpu.make_async_copy(x_ref, rows_in.at[0, 0], local)
    own.start()

    @pl.loop(0, tiles)
    def _(f):
        load(f, 0).start()
        load(f, 1).start()

    own.wait()
    pl.semaphore_wait(barrier, 1 + steps + zsteps)
    for p in range(parts):
        spread(p, orders[p][0], 0).start()
    for p in range(parts):
        forward(p, 0).start()

    def up_tiles(r, begin, end, first=False, last=False):
        @pl.loop(begin, end)
        def _(f):
            if first:
                load(f, 0).wait()
                load(f, 1).wait()
            tokens = rows_in[r].reshape(2 * rows, width)
            gate = jnp.dot(tokens, weights[2 * f], preferred_element_type=jnp.float32)
            up = jnp.dot(tokens, weights[2 * f + 1], preferred_element_type=jnp.float32)
            act = (gate / (1.0 + jnp.exp(-gate)) * up).astype(low)
            at = pl.ds(pl.multiple_of(f * tile, 128), tile)
            hidden[0, r * rows : (r + 1) * rows, at] = act[:rows]
            hidden[1, r * rows : (r + 1) * rows, at] = act[rows:]
            if last:
                for side in range(2):
                    m = 2 * f + side

                    @pl.when(m < subs)
                    def _():
                        for i in range(tile // piece):
                            load_down(m, i).start()

    def ready(r):
        for p in range(parts):
            forward(p, r).wait_recv()

    ready(0)
    up_tiles(0, 0, tiles, first=True)
    got = [{0} for _ in range(parts)]

    def absorb(p, r):
        if r not in got[p]:
            arrived(p, r)
            forward(p, r).start()
            got[p].add(r)

    for t in range(1, steps):
        for p in range(parts):
            for r in span(orders[p][:t]):
                absorb(p, r)
        for k in range(1 << t):
            for p in range(parts):
                spread(p, orders[p][t], span(orders[p][:t])[k]).start()
    rest = sorted(range(1, chips), key=lambda r: (len(parts_of(r)), r))
    for i, r in enumerate(rest):
        for p in range(parts):
            absorb(p, r)
        ready(r)
        middle = tiles // 2
        up_tiles(r, 0, middle, last=i + 1 == len(rest))
        for later in rest[i + 1 : i + 2]:
            for p in range(parts):
                absorb(p, later)
        up_tiles(r, middle, tiles, last=i + 1 == len(rest))

    moves = []
    for t in range(steps):
        step = []
        for p in range(parts):
            for i, left in enumerate(span(orders[p][t + 1 :])):
                step.append((p, left | orders[p][t], left, i))
        moves.append(step)
    base = [sum(len(s) for s in moves[:t]) for t in range(steps)]
    zmoves = [[(left | zbits[u], left) for left in span(zbits[u + 1 :])] for u in range(zsteps)]
    zbase = [sum(len(s) for s in zmoves[:u]) for u in range(zsteps)]

    def exchange(n):
        return remote(leaving.at[n % 2], sib_in.at[n], sib_send.at[n], sib_recv.at[n], sibling)

    def block(r):
        return pl.ds(r * rows, rows)

    def deliver(n, t, k):
        p, sent, _, _ = moves[t][k]
        at = base[t] + k
        return remote(
            sib_in.at[n, block(sent), pl.ds(p * pw, pw)], part_in.at[n, at],
            rs_send.at[n, at], rs_recv.at[n, at], peer(orders[p][t]),
        )

    def hand(n, u, k):
        sent, _ = zmoves[u][k]
        at = zbase[u] + k
        return remote(
            strips.at[n, sent - 1], strip_in.at[n, at], z_send.at[n, at], z_recv.at[n, at],
            flip(group, zbits[u]), "expert",
        )

    def down(c, n, i):
        slot = (n * per_tile + i) % slots
        return jnp.dot(hidden[c], weights[slot, :units, :], preferred_element_type=jnp.float32)

    def leave(n):
        for i in range(per_tile):
            for j in range(tile // piece):
                load_down(n * per_tile + i, j).wait()

        @pl.when(n >= 2)
        def _():
            exchange(n - 2).wait_send()

        for i in range(per_tile):
            leaving[n % 2, :, i * tile : (i + 1) * tile] = down(1, n, i).astype(low)
        exchange(n).start()

    def stay(n):
        for i in range(per_tile):
            keep[:, i * tile : (i + 1) * tile] = down(0, n, i)
        for i in range(per_tile):
            m = n * per_tile + i + slots

            @pl.when(m < subs)
            def _():
                for j in range(tile // piece):
                    load_down(m, j).start()

    def join(n):
        exchange(n).wait_recv()
        sib_in[n] = (keep[...] + sib_in[n].astype(jnp.float32)).astype(low)
        for k in range(len(moves[0])):
            deliver(n, 0, k).start()

    def gather_step(n, t):
        for k, (p, _, left, _) in enumerate(moves[t]):
            deliver(n, t, k).wait_recv()
            at = (block(left), pl.ds(p * pw, pw))
            mine = sib_in[n, at[0], at[1]].astype(jnp.float32)
            sib_in[n, at[0], at[1]] = (mine + part_in[n, base[t] + k].astype(jnp.float32)).astype(low)
        if t + 1 < steps:
            for k in range(len(moves[t + 1])):
                deliver(n, t + 1, k).start()
        else:
            mix = share_ref[...] * jnp.dot(place_ref[...], sib_in[n, :rows, :], preferred_element_type=jnp.float32)
            column = pl.ds(pl.multiple_of(n * piece, 128), piece)
            scatter[...] = mix
            mine = pl.ds(pl.multiple_of(group * piece, 128), piece)
            scatter[:, mine] += stream_ref[:, column]
            for q in range(experts):
                start = across(group, parts_of(q)) * own_rows
                strip = scatter[pl.ds(pl.multiple_of(start, own_rows), own_rows), :]
                if q == 0:
                    own_out[n] = strip
                else:
                    strips[n, q - 1] = strip.astype(low)
            for k in range(len(zmoves[0])):
                hand(n, 0, k).start()

    def combine_step(n, u):
        for k, (_, left) in enumerate(zmoves[u]):
            hand(n, u, k).wait_recv()
            theirs = strip_in[n, zbase[u] + k].astype(jnp.float32)
            if left == 0:
                own_out[n] += theirs
            else:
                strips[n, left - 1] = (strips[n, left - 1].astype(jnp.float32) + theirs).astype(low)
        if u + 1 < zsteps:
            for k in range(len(zmoves[u + 1])):
                hand(n, u + 1, k).start()
        else:
            column = n * piece
            for g in range(experts):
                at = pl.ds(pl.multiple_of(g * slab + column, 128), piece)
                o_ref[:, at] = own_out[n, :, g * piece : (g + 1) * piece].astype(o_ref.dtype)

    lag = 1 + steps + zsteps

    @pl.loop(0, total + lag)
    def _(n):
        @pl.when(n < total)
        def _():
            leave(n)

        @pl.when((n >= 1) & (n - 1 < total))
        def _():
            join(n - 1)

        @pl.when(n < total)
        def _():
            stay(n)

        for t in range(steps):
            @pl.when((n >= 2 + t) & (n - 2 - t < total))
            def _():
                gather_step(n - 2 - t, t)

        for u in range(zsteps):
            @pl.when((n >= 2 + steps + u) & (n - 2 - steps - u < total))
            def _():
                combine_step(n - 2 - steps - u, u)

    for n in range(max(0, total - 2), total):
        exchange(n).wait_send()
    for p in range(parts):
        for r in range(chips):
            forward(p, r).wait_send()
            if r > 0:
                spread(p, orders[p][0], r ^ orders[p][0]).wait_send()

    @pl.loop(0, total)
    def _(n):
        for t in range(steps):
            for k in range(len(moves[t])):
                deliver(n, t, k).wait_send()
        for u in range(zsteps):
            for k in range(len(zmoves[u])):
                hand(n, u, k).wait_send()


def expert_layer(x, gate_w, up_w, down_w, stream, place, share):
    chips, experts = lax.axis_size("blk") // 2, lax.axis_size("expert")
    rows, width = x.shape
    units = gate_w.shape[1]
    tile = 256 if units % 256 == 0 else 128
    tokens = stream.shape[0]
    tw = 128 * experts
    total = width // tw
    dma = pltpu.SemaphoreType.DMA
    low, wide = jnp.bfloat16, jnp.float32
    vmem = pl.BlockSpec(memory_space=pltpu.VMEM)
    anywhere = pl.BlockSpec(memory_space=pl.ANY)
    own_rows = tokens // experts
    slots = 2 * (units // tile)
    moved = 2 * (chips - 1)
    return pl.pallas_call(
        functools.partial(expert_kernel, chips, experts),
        out_shape=jax.ShapeDtypeStruct((own_rows, width), low),
        in_specs=[anywhere] * 4 + [vmem] * 3,
        out_specs=vmem,
        scratch_shapes=[
            pltpu.VMEM((chips, 2, rows, width), low),
            pltpu.VMEM((slots, width, tile), low),
            pltpu.VMEM((2, chips * rows, units), low),
            pltpu.VMEM((2, chips * rows, tw), low),
            pltpu.VMEM((total, chips * rows, tw), low),
            pltpu.VMEM((chips * rows, tw), wide),
            pltpu.VMEM((total, moved, rows, tw // 2), low),
            pltpu.VMEM((total, own_rows, tw), wide),
            pltpu.VMEM((total, experts - 1, own_rows, tw), low),
            pltpu.VMEM((total, experts - 1, own_rows, tw), low),
            pltpu.VMEM((tokens, tw), wide),
            dma,
            dma((slots,)),
            dma((slots, tile // 128)),
            dma((2, chips)),
            dma((2, chips)),
            dma((2, chips)),
            dma((2, chips)),
            dma((total,)),
            dma((total,)),
            dma((total, moved)),
            dma((total, moved)),
            dma((total, experts - 1)),
            dma((total, experts - 1)),
        ],
        compiler_params=pltpu.CompilerParams(
            collective_id=1, has_side_effects=True, vmem_limit_bytes=61 * 1024 * 1024
        ),
    )(x, gate_w, up_w, down_w, stream, place, share)


def on_device(
    residual,
    queries,
    key_cache,
    value_cache,
    segments,
    routes,
    w_out,
    norm_gain,
    w_router,
    w_gate,
    w_up,
    w_down,
):
    tok_rows = queries.shape[0]
    kv_heads = key_cache.shape[1] // HD
    q_per_kv = H // KVH
    seq_block = lax.axis_index("blk")
    head_group = lax.axis_index("expert")
    first_row = seq_block * tok_rows
    query_pos = first_row + jnp.arange(tok_rows, dtype=jnp.int32)
    query_seg = lax.dynamic_slice_in_dim(segments, first_row, tok_rows)
    query_four = queries.reshape(tok_rows, kv_heads, q_per_kv, HD)
    score_scale = 1.0 / math.sqrt(HD)
    running = jnp.full((kv_heads, q_per_kv, tok_rows), -1e30, jnp.float32)
    key_rows, value_rows, w_part = gather_blocks(key_cache, value_cache, w_out)
    w_cols = lax.all_gather(w_part, "blk", axis=1, tiled=True)
    w_cols = w_cols.reshape(-1, w_cols.shape[2])
    piece_len = key_rows.shape[0]
    key_pos = jnp.arange(piece_len, dtype=jnp.int32)
    visible = (query_seg[:, None] == segments[None, :]) & (key_pos[None, :] <= query_pos[:, None])
    scores = (
        jnp.einsum(
            "qkgd,skd->kgqs",
            query_four,
            key_rows.reshape(piece_len, kv_heads, HD),
            preferred_element_type=jnp.float32,
        )
        * score_scale
    )
    scores = jnp.where(visible, scores, -1e30)
    newmax = jnp.maximum(running, jnp.max(scores, axis=-1))
    weights = jnp.where(visible, jnp.exp(scores - newmax[..., None]), 0.0)
    totals = jnp.sum(weights, axis=-1)
    weighted_sum = jnp.einsum(
        "kgqs,skd->kgqd",
        weights.astype(jnp.bfloat16),
        value_rows.reshape(piece_len, kv_heads, HD),
        preferred_element_type=jnp.float32,
    )
    running, totals, weighted_sum = (newmax, totals, weighted_sum)
    attended = (
        jnp.transpose(weighted_sum / totals[..., None], (2, 0, 1, 3))
        .reshape(tok_rows, kv_heads * q_per_kv * HD)
        .astype(jnp.bfloat16)
    )
    feat_width = residual.shape[1]
    experts = w_router.shape[1]
    first_col = head_group * feat_width
    capacity = tok_rows * TOP * 9 // (8 * experts)
    capacity = -(-capacity // 16) * 16
    ids = jnp.arange(experts, dtype=jnp.int32)
    picked = routes[:, :, None] == ids[None, None, :]
    routed = jnp.any(picked, axis=1).T
    earlier = jnp.arange(tok_rows)[:, None] <= jnp.arange(tok_rows)[None, :]
    counted = jnp.dot(
        routed.astype(jnp.bfloat16), earlier.astype(jnp.bfloat16), preferred_element_type=jnp.float32
    )
    slot_index = jnp.where(routed, counted.astype(jnp.int32) - 1, -1)
    slots = jnp.arange(capacity, dtype=jnp.int32)
    placing = (slot_index[:, None, :] == slots[None, :, None]).astype(jnp.bfloat16)
    placing_back = (slot_index[:, :, None] == slots[None, None, :]).astype(jnp.bfloat16)
    router = lax.dynamic_slice_in_dim(w_router, first_col, feat_width, 0).T
    router = jnp.pad(router, ((0, -experts % 16), (0, 0)))
    gain = lax.dynamic_slice_in_dim(norm_gain, first_col, feat_width)[None, :]
    attended = gather_heads(attended)
    stream, buffer, logits = mix_columns(attended, w_cols, residual, gain, router, placing)
    gate_score = jax.nn.sigmoid(logits[:experts, :].T)
    chosen = jnp.where(routed.T, gate_score, 0.0)
    shares = chosen / jnp.sum(chosen, axis=-1, keepdims=True)
    share = lax.dynamic_slice_in_dim(shares, head_group, 1, 1)
    place = lax.dynamic_index_in_dim(placing_back, head_group, 0, keepdims=False)
    return expert_layer(buffer, w_gate[0], w_up[0], w_down[0], stream, place, share)


def solution(mesh):
    return jax.shard_map(
        on_device,
        mesh=mesh,
        in_specs=(
            P("blk", "expert"),
            P("blk", "expert"),
            P("blk", "expert"),
            P("blk", "expert"),
            P(),
            P("blk", None),
            P("expert", None),
            P(),
            P(),
            P("expert", None, "blk"),
            P("expert", None, "blk"),
            P("expert", "blk", None),
        ),
        out_specs=P(("blk", "expert"), None),
        check_vma=False,
    )
```

```python
import functools
import math

import jax
import jax.numpy as jnp
from jax import lax
from jax.experimental import pallas as pl
from jax.experimental.pallas import tpu as pltpu
from jax.sharding import PartitionSpec as P

HD = 128
TOP = 2

MESH = pl.DeviceIdType.MESH


def remote(src, dst, send_sem, recv_sem, target, axis="blk"):
    return pltpu.make_async_remote_copy(
        src_ref=src,
        dst_ref=dst,
        send_sem=send_sem,
        recv_sem=recv_sem,
        device_id={axis: target},
        device_id_type=MESH,
    )


def flip(index, bit):
    return index + bit * (1 - 2 * ((index // bit) % 2))


def across(index, bits):
    for bit in bits:
        index = flip(index, bit)
    return index


def log2(n):
    return n.bit_length() - 1


def parts_of(mask):
    return [1 << b for b in range(mask.bit_length()) if mask >> b & 1]


def span(order):
    found = [0]
    for bit in order:
        found += [f | bit for f in found]
    return found


def front_kernel(
    chips, experts, given, q_ref, k_ref, v_ref, seg_ref, rt_ref, w_ref, res_ref, gain_ref, router_ref,
    stream_ref, buf_ref, logit_ref, mine_ref,
    kv_in, w_in, att_in, stacked, top, total_w, acc, place, squares, logits, chosen, local,
    kv_send, kv_recv, kf_send, kf_recv, wz_send, wz_recv, w_send, w_recv, wf_send, wf_recv,
    a_send, a_recv, s_send, s_recv, l_send, l_recv, d_send, d_recv,
):
    me, group = lax.axis_index("blk"), lax.axis_index("expert")
    chip, core = me // 2, me % 2
    sibling = chip * 2 + 1 - core
    steps, zsteps = log2(chips), log2(experts)
    bits = [1 << b for b in range(steps)]
    zorder = [1 << b for b in range(zsteps)][::-1]
    parts = 2
    orders = [bits[p % steps :] + bits[: p % steps] for p in range(parts)]
    rows, cols = res_ref.shape
    kv_heads = k_ref.shape[1] // HD
    pack = q_ref.shape[1] // k_ref.shape[1]
    depth = q_ref.shape[1]
    wide, low = jnp.float32, jnp.bfloat16
    kv = (k_ref, v_ref)

    def peer(bit):
        return flip(chip, bit) * 2 + core

    def target(k):
        return (group + k) % experts

    barrier = pltpu.get_barrier_semaphore()
    pl.semaphore_signal(barrier, inc=1, device_id={"blk": sibling}, device_id_type=MESH)
    for bit in bits:
        pl.semaphore_signal(barrier, inc=1, device_id={"blk": peer(bit)}, device_id_type=MESH)
    for k in range(1, experts):
        pl.semaphore_signal(barrier, inc=1, device_id={"expert": target(k)}, device_id_type=MESH)

    def kv_from(p, r):
        return kv[p] if r == 0 else kv_in.at[p, r, 0]

    def kv_spread(p, bit, r):
        return remote(
            kv_from(p, r), kv_in.at[p, r ^ bit, 0], kv_send.at[p, r ^ bit], kv_recv.at[p, r ^ bit], peer(bit)
        )

    def kv_forward(p, r):
        return remote(kv_from(p, r), kv_in.at[p, r, 1], kf_send.at[p, r], kf_recv.at[p, r], sibling)

    piece = cols // (2 * chips)
    half = w_in.shape[1] // parts
    lanes = pl.ds(pl.multiple_of(core * piece, 128), piece)
    w_rows = pl.ds(pl.multiple_of(group * depth, depth), depth)

    def w_piece(k):
        return w_ref.at[:, pl.ds(pl.multiple_of(target(k) * cols + me * piece, 128), piece)]

    def lend(k):
        return remote(
            w_piece(k), w_in.at[0, w_rows, lanes], wz_send.at[k], wz_recv.at[k], target(k), "expert"
        )

    def w_part(p, r):
        return w_in.at[r, pl.ds(p * half, half), lanes]

    def w_spread(p, bit, r):
        return remote(
            w_part(p, r), w_part(p, r ^ bit), w_send.at[p, r ^ bit], w_recv.at[p, r ^ bit], peer(bit)
        )

    def w_forward(p, r):
        return remote(w_part(p, r), w_part(p, r), wf_send.at[p, r], wf_recv.at[p, r], sibling)

    own = [pltpu.make_async_copy(kv[p], kv_in.at[p, 0, 0], local.at[p]) for p in range(2)]
    if given:
        own.append(pltpu.make_async_copy(w_ref, w_in.at[0], local.at[2]))
    else:
        own.append(pltpu.make_async_copy(w_piece(0), w_in.at[0, w_rows, lanes], local.at[2]))
    for copy in own:
        copy.start()
    pl.semaphore_wait(barrier, steps + experts)
    for p in range(parts):
        kv_spread(p, orders[p][0], 0).start()
    for p in range(parts):
        kv_forward(p, 0).start()
    for t in range(1, steps):
        for p in range(parts):
            kv_spread(p, orders[p][t], 0).start()
    if not given:
        for k in range(experts - 1, 0, -1):
            lend(k).start()

    ids = lax.broadcasted_iota(jnp.int32, (16, rows), 0)
    routed = rt_ref[0:1, :] == ids
    for j in range(1, rt_ref.shape[0]):
        routed = routed | (rt_ref[j : j + 1, :] == ids)
    earlier = lax.broadcasted_iota(jnp.int32, (rows, rows), 0) <= lax.broadcasted_iota(jnp.int32, (rows, rows), 1)
    counted = jnp.dot(
        jnp.where(routed, 1.0, 0.0).astype(low), jnp.where(earlier, 1.0, 0.0).astype(low), preferred_element_type=wide
    )
    index = jnp.where(routed, counted.astype(jnp.int32) - 1, -1)
    capacity = place.shape[1]
    slots = lax.broadcasted_iota(jnp.int32, (capacity, rows), 0)
    for e in range(experts):
        place[e] = jnp.where(index[e : e + 1, :] == slots, 1.0, 0.0).astype(low)
    mine_ref[...] = place[group]

    for h in range(kv_heads):
        for g in range(pack):
            at = (h * pack + g) * HD
            stacked[h, g * rows : (g + 1) * rows, :] = q_ref[:, at : at + HD]
    top[...] = jnp.full_like(top, -1e30)
    total_w[...] = jnp.zeros_like(total_w)
    acc[...] = jnp.zeros_like(acc)
    here = seg_ref[:, pl.ds(pl.multiple_of(me * rows, 128), rows)].astype(wide)
    here = jnp.transpose(jnp.broadcast_to(here, (128, rows)))[:, :1]
    row_id = lax.broadcasted_iota(jnp.int32, (rows, rows), 0)
    col_id = lax.broadcasted_iota(jnp.int32, (rows, rows), 1)
    scale = 1.0 / math.sqrt(HD)

    def attend(h, r, c):
        block = across(chip, parts_of(r)) * 2 + (core if c == 0 else 1 - core)

        @pl.when(block <= me)
        def _():
            there = seg_ref[:, pl.ds(pl.multiple_of(block * rows, 128), rows)].astype(wide)
            seen = (here == there) & (col_id + block * rows <= row_id + me * rows)
            seen = jnp.concatenate([seen.astype(jnp.int32)] * pack, axis=0) > 0
            keys = kv_in[0, r, c, :, h * HD : (h + 1) * HD]
            values = kv_in[1, r, c, :, h * HD : (h + 1) * HD]
            score = lax.dot_general(
                stacked[h], keys, (((1,), (1,)), ((), ())), preferred_element_type=wide
            ) * scale
            score = jnp.where(seen, score, -1e30)
            before = top[h]
            after = jnp.maximum(before, jnp.max(score, axis=-1, keepdims=True))
            shrink = jnp.exp(before - after)
            weight = jnp.where(seen, jnp.exp(score - after[:, :1]), 0.0)
            top[h] = after
            total_w[h] = total_w[h] * shrink + jnp.sum(weight, axis=-1, keepdims=True)
            acc[h] = acc[h] * shrink + jnp.dot(weight.astype(low), values, preferred_element_type=wide)

    for copy in own[:2]:
        copy.wait()
    for h in range(kv_heads):
        attend(h, 0, 0)
    for p in range(parts):
        kv_forward(p, 0).wait_recv()
    for h in range(kv_heads):
        attend(h, 0, 1)

    def take(spread, onward, got, p, r):
        if r not in got[p]:
            spread(p, orders[p][0], r ^ orders[p][0]).wait_recv()
            onward(p, r).start()
            got[p].add(r)

    def relay(spread, onward, got, t, skip):
        for p in range(parts):
            for r in span(orders[p][:t]):
                take(spread, onward, got, p, r)
        for k in range(skip, 1 << t):
            for p in range(parts):
                spread(p, orders[p][t], span(orders[p][:t])[k]).start()

    got = [{0} for _ in range(parts)]
    for t in range(1, steps):
        relay(kv_spread, kv_forward, got, t, 1)
    rest = sorted(range(1, chips), key=lambda r: (len(parts_of(r)), r))
    w_got = [{0} for _ in range(parts)]
    for r in rest:
        for p in range(parts):
            take(kv_spread, kv_forward, got, p, r)
    if not given:
        own[2].wait()
        for k in range(1, experts):
            lend(k).wait_recv()
        for p in range(parts):
            w_spread(p, orders[p][0], 0).start()
        for p in range(parts):
            w_forward(p, 0).start()
        for t in range(1, steps):
            for p in range(parts):
                w_spread(p, orders[p][t], 0).start()
    for r in rest:
        for p in range(parts):
            kv_forward(p, r).wait_recv()

    def part(h):
        return pl.ds(h * pack * HD, pack * HD)

    def share_heads(h, bit, q):
        return remote(
            att_in.at[q, :, part(h)], att_in.at[q ^ bit, :, part(h)],
            a_send.at[h, q ^ bit], a_recv.at[h, q ^ bit], flip(group, bit), "expert",
        )

    for h in range(kv_heads):
        for r in rest:
            for c in range(2):
                attend(h, r, c)
        done = (acc[h] / total_w[h]).astype(low)
        for g in range(pack):
            at = (h * pack + g) * HD
            att_in[0, :, at : at + HD] = done[g * rows : (g + 1) * rows, :]
        for bit in zorder:
            share_heads(h, bit, 0).start()

    if given:
        own[2].wait()
    else:
        for t in range(1, steps):
            relay(w_spread, w_forward, w_got, t, 1)
    stream_ref[...] = res_ref[...].astype(wide)
    z_got = {0}
    for t in range(1, zsteps):
        for q in span(zorder[:t]):
            if q not in z_got:
                z_got.add(q)
                for h in range(kv_heads):
                    share_heads(h, zorder[0], q ^ zorder[0]).wait_recv()
                    for bit in zorder[t:]:
                        share_heads(h, bit, q).start()
    if not given:
        for r in rest:
            for p in range(parts):
                take(w_spread, w_forward, w_got, p, r)
        for r in range(chips):
            for p in range(parts):
                w_forward(p, r).wait_recv()

    def project(q):
        g = across(group, parts_of(q))
        from_rows = pl.ds(pl.multiple_of(g * depth, depth), depth)
        if given:
            stream_ref[...] += jnp.dot(att_in[q], w_in[0, from_rows, :], preferred_element_type=wide)
        else:
            for r in range(chips):
                c = across(chip, parts_of(r)) * 2 * piece
                at = pl.ds(pl.multiple_of(c, 2 * piece), 2 * piece)
                stream_ref[:, at] += jnp.dot(att_in[q], w_in[r, from_rows, :], preferred_element_type=wide)

    for q in [0] + zorder + sorted(set(range(1, experts)) - set(zorder)):
        if q not in z_got:
            z_got.add(q)
            for h in range(kv_heads):
                share_heads(h, zorder[0], q ^ zorder[0]).wait_recv()
        project(q)

    def share_squares(k):
        return remote(squares.at[0], squares.at[k], s_send.at[k], s_recv.at[k], target(k), "expert")

    def share_logits(k):
        return remote(logits.at[0], logits.at[k], l_send.at[k], l_recv.at[k], target(k), "expert")

    def slab(g):
        return pl.ds(pl.multiple_of(g * cols, 128), cols)

    def dispatch(k, g):
        return remote(
            chosen.at[k], buf_ref.at[:, slab(g)], d_send.at[k], d_recv.at[k], target(k), "expert"
        )

    stream = stream_ref[...]
    total = jnp.sum(stream * stream, axis=-1, keepdims=True)
    squares[0] = jnp.transpose(jnp.broadcast_to(total, (rows, 128)))[:8, :]
    for k in range(1, experts):
        share_squares(k).start()
    for k in range(1, experts):
        share_squares(k).wait_recv()
    total = squares[0]
    for k in range(1, experts):
        total = total + squares[k]
    total = jnp.transpose(jnp.broadcast_to(total[:1, :], (128, rows)))[:, :1]
    inverse = lax.rsqrt(total * (1.0 / (cols * experts)) + 1e-05)
    normed = (stream_ref[...] * inverse * gain_ref[...]).astype(low)
    for k in range(experts - 1, 0, -1):
        chosen[k] = jnp.dot(place[target(k)], normed, preferred_element_type=wide).astype(low)
        dispatch(k, group).start()
    logits[0] = lax.dot_general(
        router_ref[...], normed, (((1,), (1,)), ((), ())), preferred_element_type=wide
    )
    for k in range(1, experts):
        share_logits(k).start()
    buf_ref[:, slab(group)] = jnp.dot(place[group], normed, preferred_element_type=wide).astype(low)
    for k in range(1, experts):
        share_logits(k).wait_recv()
    total = logits[0]
    for k in range(1, experts):
        total = total + logits[k]
    logit_ref[...] = total
    for p in range(parts):
        for r in range(chips):
            kv_forward(p, r).wait_send()
            if r > 0:
                kv_spread(p, orders[p][0], r ^ orders[p][0]).wait_send()
            if not given:
                w_forward(p, r).wait_send()
                if r > 0:
                    w_spread(p, orders[p][0], r ^ orders[p][0]).wait_send()
    for h in range(kv_heads):
        for q in range(1, experts):
            share_heads(h, zorder[0], q ^ zorder[0]).wait_send()
    for k in range(1, experts):
        dispatch(k, target(experts - k)).wait_recv()
    for k in range(1, experts):
        if not given:
            lend(k).wait_send()
        share_squares(k).wait_send()
        share_logits(k).wait_send()
        dispatch(k, group).wait_send()


def front(queries, keys, values, segments, routes_t, w_out, residual, gain, router, capacity):
    chips, experts = lax.axis_size("blk") // 2, lax.axis_size("expert")
    rows, cols = residual.shape
    depth = queries.shape[1]
    kv_heads = keys.shape[1] // HD
    pack = queries.shape[1] // keys.shape[1]
    low, wide = jnp.bfloat16, jnp.float32
    vmem, dma, shape = pl.BlockSpec(memory_space=pltpu.VMEM), pltpu.SemaphoreType.DMA, jax.ShapeDtypeStruct
    given = cols % (256 * chips) != 0
    if given:
        w_out = lax.all_to_all(w_out, "expert", 1, 0, tiled=True)
    w_shape = (1, depth * experts, cols) if given else (chips, depth * experts, cols // chips)
    return pl.pallas_call(
        functools.partial(front_kernel, chips, experts, given),
        out_shape=(
            shape((rows, cols), wide),
            shape((capacity, cols * experts), low),
            shape((router.shape[0], rows), wide),
            shape((capacity, rows), low),
        ),
        in_specs=[vmem] * 5 + [pl.BlockSpec(memory_space=pl.ANY)] + [vmem] * 3,
        out_specs=(vmem,) * 4,
        scratch_shapes=[
            pltpu.VMEM((2, chips, 2) + keys.shape, low),
            pltpu.VMEM(w_shape, low),
            pltpu.VMEM((experts, rows, depth), low),
            pltpu.VMEM((kv_heads, pack * rows, HD), low),
            pltpu.VMEM((kv_heads, pack * rows, HD), wide),
            pltpu.VMEM((kv_heads, pack * rows, HD), wide),
            pltpu.VMEM((kv_heads, pack * rows, HD), wide),
            pltpu.VMEM((experts, capacity, rows), low),
            pltpu.VMEM((experts, 8, rows), wide),
            pltpu.VMEM((experts, router.shape[0], rows), wide),
            pltpu.VMEM((experts, capacity, cols), low),
            dma((3,)),
        ]
        + [dma((2, chips))] * 4
        + [dma((experts,))] * 2
        + [dma((2, chips))] * 4
        + [dma((kv_heads, experts))] * 2
        + [dma((experts,))] * 6,
        compiler_params=pltpu.CompilerParams(
            collective_id=0, has_side_effects=True, vmem_limit_bytes=48 * 1024 * 1024
        ),
    )(queries, keys, values, segments, routes_t, w_out, residual, gain, router)


def expert_kernel(
    chips, experts, x_ref, wg_ref, wu_ref, wd_ref, stream_ref, place_ref, logit_ref, rt_ref, o_ref,
    rows_in, weights, hidden, leaving, sib_in, keep, part_in, own_out, strips, strip_in, scatter, share,
    local, w_sem, d_sem, ag_send, ag_recv, fw_send, fw_recv, sib_send, sib_recv,
    rs_send, rs_recv, z_send, z_recv,
):
    me, group = lax.axis_index("blk"), lax.axis_index("expert")
    chip, core = me // 2, me % 2
    sibling = chip * 2 + 1 - core
    rows, width = x_ref.shape
    units = wg_ref.shape[1]
    tile = weights.shape[2]
    tiles = units // tile
    slots = 2 * tiles
    steps, zsteps = log2(chips), log2(experts)
    bits = [1 << b for b in range(steps)]
    zbits = [1 << b for b in range(zsteps)]
    parts = 2
    orders = [bits[p % steps :] + bits[: p % steps] for p in range(parts)]
    half = width // parts
    tw = leaving.shape[2]
    pw = tw // parts
    total = width // tw
    per_tile = tw // tile
    piece = tw // experts
    subs = width // tile
    slab = width // experts
    own_rows = o_ref.shape[0]
    low = jnp.bfloat16

    def peer(bit):
        return flip(chip, bit) * 2 + core

    barrier = pltpu.get_barrier_semaphore()
    pl.semaphore_signal(barrier, inc=1, device_id={"blk": sibling}, device_id_type=MESH)
    for bit in bits:
        pl.semaphore_signal(barrier, inc=1, device_id={"blk": peer(bit)}, device_id_type=MESH)
    for bit in zbits:
        pl.semaphore_signal(barrier, inc=1, device_id={"expert": flip(group, bit)}, device_id_type=MESH)

    def load(f, side):
        src = (wg_ref, wu_ref)[side]
        return pltpu.make_async_copy(
            src.at[:, pl.ds(pl.multiple_of(f * tile, 128), tile)], weights.at[2 * f + side], w_sem.at[2 * f + side]
        )

    def load_down(m, i):
        column = (m % per_tile) * (tile // piece) + i
        column = column * slab + (m // per_tile) * piece
        slot = m % slots
        return pltpu.make_async_copy(
            wd_ref.at[:, pl.ds(pl.multiple_of(column, 128), piece)],
            weights.at[slot, pl.ds(0, units), pl.ds(i * piece, piece)],
            d_sem.at[slot, i],
        )

    def cols(p):
        return pl.ds(p * half, half)

    def spread(p, bit, r):
        return remote(
            rows_in.at[r, 0, :, cols(p)], rows_in.at[r ^ bit, 0, :, cols(p)],
            ag_send.at[p, r ^ bit], ag_recv.at[p, r ^ bit], peer(bit),
        )

    def arrived(p, r):
        spread(p, orders[p][0], r ^ orders[p][0]).wait_recv()

    def forward(p, r):
        return remote(
            rows_in.at[r, 0, :, cols(p)], rows_in.at[r, 1, :, cols(p)],
            fw_send.at[p, r], fw_recv.at[p, r], sibling,
        )

    own = pltpu.make_async_copy(x_ref, rows_in.at[0, 0], local)
    own.start()

    @pl.loop(0, tiles)
    def _(f):
        load(f, 0).start()
        load(f, 1).start()

    own.wait()
    pl.semaphore_wait(barrier, 1 + steps + zsteps)
    for p in range(parts):
        spread(p, orders[p][0], 0).start()
    for p in range(parts):
        forward(p, 0).start()

    def up_tiles(r, begin, end, first=False, last=False):
        @pl.loop(begin, end)
        def _(f):
            if first:
                load(f, 0).wait()
                load(f, 1).wait()
            tokens = rows_in[r].reshape(2 * rows, width)
            gate = jnp.dot(tokens, weights[2 * f], preferred_element_type=jnp.float32)
            up = jnp.dot(tokens, weights[2 * f + 1], preferred_element_type=jnp.float32)
            act = (gate / (1.0 + jnp.exp(-gate)) * up).astype(low)
            at = pl.ds(pl.multiple_of(f * tile, 128), tile)
            hidden[0, r * rows : (r + 1) * rows, at] = act[:rows]
            hidden[1, r * rows : (r + 1) * rows, at] = act[rows:]
            if last:
                for side in range(2):
                    m = 2 * f + side

                    @pl.when(m < subs)
                    def _():
                        for i in range(tile // piece):
                            load_down(m, i).start()

    def ready(r):
        for p in range(parts):
            forward(p, r).wait_recv()

    tokens_here = rt_ref.shape[1]
    ids = lax.broadcasted_iota(jnp.int32, (logit_ref.shape[0], tokens_here), 0)
    routed = rt_ref[0:1, :] == ids
    for j in range(1, rt_ref.shape[0]):
        routed = routed | (rt_ref[j : j + 1, :] == ids)
    score = jnp.where(routed, 1.0 / (1.0 + jnp.exp(-logit_ref[...])), 0.0)
    fraction = jnp.sum(jnp.where(ids == group, score, 0.0), axis=0, keepdims=True) / jnp.sum(
        score, axis=0, keepdims=True
    )
    share[...] = jnp.transpose(jnp.broadcast_to(fraction, (128, tokens_here)))

    ready(0)
    up_tiles(0, 0, tiles, first=True)
    got = [{0} for _ in range(parts)]

    def absorb(p, r):
        if r not in got[p]:
            arrived(p, r)
            forward(p, r).start()
            got[p].add(r)

    for t in range(1, steps):
        for p in range(parts):
            for r in span(orders[p][:t]):
                absorb(p, r)
        for k in range(1 << t):
            for p in range(parts):
                spread(p, orders[p][t], span(orders[p][:t])[k]).start()
    rest = sorted(range(1, chips), key=lambda r: (len(parts_of(r)), r))
    for i, r in enumerate(rest):
        for p in range(parts):
            absorb(p, r)
        ready(r)
        middle = tiles // 2
        up_tiles(r, 0, middle, last=i + 1 == len(rest))
        for later in rest[i + 1 : i + 2]:
            for p in range(parts):
                absorb(p, later)
        up_tiles(r, middle, tiles, last=i + 1 == len(rest))

    moves = []
    for t in range(steps):
        step = []
        for p in range(parts):
            for i, left in enumerate(span(orders[p][t + 1 :])):
                step.append((p, left | orders[p][t], left, i))
        moves.append(step)
    base = [sum(len(s) for s in moves[:t]) for t in range(steps)]
    zmoves = [[(left | zbits[u], left) for left in span(zbits[u + 1 :])] for u in range(zsteps)]
    zbase = [sum(len(s) for s in zmoves[:u]) for u in range(zsteps)]

    def exchange(n):
        return remote(leaving.at[n % 2], sib_in.at[n], sib_send.at[n], sib_recv.at[n], sibling)

    def block(r):
        return pl.ds(r * rows, rows)

    def deliver(n, t, k):
        p, sent, _, _ = moves[t][k]
        at = base[t] + k
        return remote(
            sib_in.at[n, block(sent), pl.ds(p * pw, pw)], part_in.at[n, at],
            rs_send.at[n, at], rs_recv.at[n, at], peer(orders[p][t]),
        )

    def hand(n, u, k):
        sent, _ = zmoves[u][k]
        at = zbase[u] + k
        return remote(
            strips.at[n, sent - 1], strip_in.at[n, at], z_send.at[n, at], z_recv.at[n, at],
            flip(group, zbits[u]), "expert",
        )

    def down(c, n, i):
        slot = (n * per_tile + i) % slots
        return jnp.dot(hidden[c], weights[slot, :units, :], preferred_element_type=jnp.float32)

    def leave(n):
        for i in range(per_tile):
            for j in range(tile // piece):
                load_down(n * per_tile + i, j).wait()

        @pl.when(n >= 2)
        def _():
            exchange(n - 2).wait_send()

        for i in range(per_tile):
            leaving[n % 2, :, i * tile : (i + 1) * tile] = down(1, n, i).astype(low)
        exchange(n).start()

    def stay(n):
        for i in range(per_tile):
            keep[:, i * tile : (i + 1) * tile] = down(0, n, i)
        for i in range(per_tile):
            m = n * per_tile + i + slots

            @pl.when(m < subs)
            def _():
                for j in range(tile // piece):
                    load_down(m, j).start()

    def join(n):
        exchange(n).wait_recv()
        sib_in[n] = (keep[...] + sib_in[n].astype(jnp.float32)).astype(low)
        for k in range(len(moves[0])):
            deliver(n, 0, k).start()

    def gather_step(n, t):
        for k, (p, _, left, _) in enumerate(moves[t]):
            deliver(n, t, k).wait_recv()
            at = (block(left), pl.ds(p * pw, pw))
            mine = sib_in[n, at[0], at[1]].astype(jnp.float32)
            sib_in[n, at[0], at[1]] = (mine + part_in[n, base[t] + k].astype(jnp.float32)).astype(low)
        if t + 1 < steps:
            for k in range(len(moves[t + 1])):
                deliver(n, t + 1, k).start()
        else:
            mix = share[:, :1] * lax.dot_general(
                place_ref[...], sib_in[n, :rows, :], (((0,), (0,)), ((), ())), preferred_element_type=jnp.float32
            )
            column = pl.ds(pl.multiple_of(n * piece, 128), piece)
            scatter[...] = mix
            mine = pl.ds(pl.multiple_of(group * piece, 128), piece)
            scatter[:, mine] += stream_ref[:, column]
            for q in range(experts):
                start = across(group, parts_of(q)) * own_rows
                strip = scatter[pl.ds(pl.multiple_of(start, own_rows), own_rows), :]
                if q == 0:
                    own_out[n] = strip
                else:
                    strips[n, q - 1] = strip.astype(low)
            for k in range(len(zmoves[0])):
                hand(n, 0, k).start()

    def combine_step(n, u):
        for k, (_, left) in enumerate(zmoves[u]):
            hand(n, u, k).wait_recv()
            theirs = strip_in[n, zbase[u] + k].astype(jnp.float32)
            if left == 0:
                own_out[n] += theirs
            else:
                strips[n, left - 1] = (strips[n, left - 1].astype(jnp.float32) + theirs).astype(low)
        if u + 1 < zsteps:
            for k in range(len(zmoves[u + 1])):
                hand(n, u + 1, k).start()
        else:
            column = n * piece
            for g in range(experts):
                at = pl.ds(pl.multiple_of(g * slab + column, 128), piece)
                o_ref[:, at] = own_out[n, :, g * piece : (g + 1) * piece].astype(o_ref.dtype)

    lag = 1 + steps + zsteps

    @pl.loop(0, total + lag)
    def _(n):
        @pl.when(n < total)
        def _():
            leave(n)

        @pl.when((n >= 1) & (n - 1 < total))
        def _():
            join(n - 1)

        @pl.when(n < total)
        def _():
            stay(n)

        for t in range(steps):
            @pl.when((n >= 2 + t) & (n - 2 - t < total))
            def _():
                gather_step(n - 2 - t, t)

        for u in range(zsteps):
            @pl.when((n >= 2 + steps + u) & (n - 2 - steps - u < total))
            def _():
                combine_step(n - 2 - steps - u, u)

    for n in range(max(0, total - 2), total):
        exchange(n).wait_send()
    for p in range(parts):
        for r in range(chips):
            forward(p, r).wait_send()
            if r > 0:
                spread(p, orders[p][0], r ^ orders[p][0]).wait_send()

    @pl.loop(0, total)
    def _(n):
        for t in range(steps):
            for k in range(len(moves[t])):
                deliver(n, t, k).wait_send()
        for u in range(zsteps):
            for k in range(len(zmoves[u])):
                hand(n, u, k).wait_send()


def expert_layer(x, gate_w, up_w, down_w, stream, place, logits, routes_t):
    chips, experts = lax.axis_size("blk") // 2, lax.axis_size("expert")
    rows, width = x.shape
    units = gate_w.shape[1]
    tile = 256 if units % 256 == 0 else 128
    tokens = stream.shape[0]
    tw = 128 * experts
    total = width // tw
    dma = pltpu.SemaphoreType.DMA
    low, wide = jnp.bfloat16, jnp.float32
    vmem = pl.BlockSpec(memory_space=pltpu.VMEM)
    anywhere = pl.BlockSpec(memory_space=pl.ANY)
    own_rows = tokens // experts
    slots = 2 * (units // tile)
    moved = 2 * (chips - 1)
    return pl.pallas_call(
        functools.partial(expert_kernel, chips, experts),
        out_shape=jax.ShapeDtypeStruct((own_rows, width), low),
        in_specs=[anywhere] * 4 + [vmem] * 4,
        out_specs=vmem,
        scratch_shapes=[
            pltpu.VMEM((chips, 2, rows, width), low),
            pltpu.VMEM((slots, width, tile), low),
            pltpu.VMEM((2, chips * rows, units), low),
            pltpu.VMEM((2, chips * rows, tw), low),
            pltpu.VMEM((total, chips * rows, tw), low),
            pltpu.VMEM((chips * rows, tw), wide),
            pltpu.VMEM((total, moved, rows, tw // 2), low),
            pltpu.VMEM((total, own_rows, tw), wide),
            pltpu.VMEM((total, experts - 1, own_rows, tw), low),
            pltpu.VMEM((total, experts - 1, own_rows, tw), low),
            pltpu.VMEM((tokens, tw), wide),
            pltpu.VMEM((tokens, 128), wide),
            dma,
            dma((slots,)),
            dma((slots, tile // 128)),
            dma((2, chips)),
            dma((2, chips)),
            dma((2, chips)),
            dma((2, chips)),
            dma((total,)),
            dma((total,)),
            dma((total, moved)),
            dma((total, moved)),
            dma((total, experts - 1)),
            dma((total, experts - 1)),
        ],
        compiler_params=pltpu.CompilerParams(
            collective_id=1, has_side_effects=True, vmem_limit_bytes=61 * 1024 * 1024
        ),
    )(x, gate_w, up_w, down_w, stream, place, logits, routes_t)


def on_device(
    residual,
    queries,
    key_cache,
    value_cache,
    segments,
    routes,
    w_out,
    norm_gain,
    w_router,
    w_gate,
    w_up,
    w_down,
):
    experts = w_router.shape[1]
    cols = residual.shape[1]
    first_col = lax.axis_index("expert") * cols
    capacity = queries.shape[0] * TOP * 9 // (8 * experts)
    capacity = -(-capacity // 16) * 16
    router = lax.dynamic_slice_in_dim(w_router, first_col, cols, 0).T
    router = jnp.pad(router, ((0, -experts % 16), (0, 0)))
    gain = lax.dynamic_slice_in_dim(norm_gain, first_col, cols)[None, :]
    routes_t = routes.T
    stream, buffer, logits, place = front(
        queries, key_cache, value_cache, segments[None, :], routes_t, w_out, residual, gain, router, capacity
    )
    return expert_layer(buffer, w_gate[0], w_up[0], w_down[0], stream, place, logits, routes_t)


def solution(mesh):
    return jax.shard_map(
        on_device,
        mesh=mesh,
        in_specs=(
            P("blk", "expert"),
            P("blk", "expert"),
            P("blk", "expert"),
            P("blk", "expert"),
            P(),
            P("blk", None),
            P("expert", None),
            P(),
            P(),
            P("expert", None, "blk"),
            P("expert", None, "blk"),
            P("expert", "blk", None),
        ),
        out_specs=P(("blk", "expert"), None),
        check_vma=False,
    )
```

```python
import functools
import math

import jax
import jax.numpy as jnp
from jax import lax
from jax.experimental import pallas as pl
from jax.experimental.pallas import tpu as pltpu
from jax.sharding import PartitionSpec as P

HD = 128
TOP = 2

MESH = pl.DeviceIdType.MESH


def remote(src, dst, send_sem, recv_sem, target, axis="blk"):
    return pltpu.make_async_remote_copy(
        src_ref=src,
        dst_ref=dst,
        send_sem=send_sem,
        recv_sem=recv_sem,
        device_id={axis: target},
        device_id_type=MESH,
    )


def flip(index, bit):
    return index + bit * (1 - 2 * ((index // bit) % 2))


def across(index, bits):
    for bit in bits:
        index = flip(index, bit)
    return index


def log2(n):
    return n.bit_length() - 1


def parts_of(mask):
    return [1 << b for b in range(mask.bit_length()) if mask >> b & 1]


def span(order):
    found = [0]
    for bit in order:
        found += [f | bit for f in found]
    return found


def front_kernel(
    chips, experts, given, q_ref, k_ref, v_ref, seg_ref, rt_ref, w_ref, res_ref, gain_ref, router_ref,
    stream_ref, chosen_ref, logit_ref, mine_ref,
    kv_in, w_in, att_in, stacked, top, total_w, acc, place, squares, res_in, seg_in, rt_in, gain_in, router_in,
    local, q_local,
    kv_send, kv_recv, kf_send, kf_recv, wz_send, wz_recv, w_send, w_recv, wf_send, wf_recv,
    a_send, a_recv, s_send, s_recv,
):
    me, group = lax.axis_index("blk"), lax.axis_index("expert")
    chip, core = me // 2, me % 2
    sibling = chip * 2 + 1 - core
    steps, zsteps = log2(chips), log2(experts)
    bits = [1 << b for b in range(steps)]
    zorder = [1 << b for b in range(zsteps)][::-1]
    parts = 2
    orders = [bits[p % steps :] + bits[: p % steps] for p in range(parts)]
    rows, cols = res_ref.shape
    kv_heads = k_ref.shape[1] // HD
    pack = q_ref.shape[1] // k_ref.shape[1]
    depth = q_ref.shape[1]
    wide, low = jnp.float32, jnp.bfloat16
    kv = (k_ref, v_ref)

    def peer(bit):
        return flip(chip, bit) * 2 + core

    def target(k):
        return (group + k) % experts

    barrier = pltpu.get_barrier_semaphore()
    pl.semaphore_signal(barrier, inc=1, device_id={"blk": sibling}, device_id_type=MESH)
    for bit in bits:
        pl.semaphore_signal(barrier, inc=1, device_id={"blk": peer(bit)}, device_id_type=MESH)
    for k in range(1, experts):
        pl.semaphore_signal(barrier, inc=1, device_id={"expert": target(k)}, device_id_type=MESH)

    def kv_from(p, r):
        return kv[p] if r == 0 else kv_in.at[p, r, 0]

    def kv_spread(p, bit, r):
        return remote(
            kv_from(p, r), kv_in.at[p, r ^ bit, 0], kv_send.at[p, r ^ bit], kv_recv.at[p, r ^ bit], peer(bit)
        )

    def kv_forward(p, r):
        return remote(kv_from(p, r), kv_in.at[p, r, 1], kf_send.at[p, r], kf_recv.at[p, r], sibling)

    piece = cols // (2 * chips)
    half = w_in.shape[1] // parts
    lanes = pl.ds(pl.multiple_of(core * piece, 128), piece)
    w_rows = pl.ds(pl.multiple_of(group * depth, depth), depth)

    def w_piece(k):
        return w_ref.at[:, pl.ds(pl.multiple_of(target(k) * cols + me * piece, 128), piece)]

    def lend(k):
        return remote(
            w_piece(k), w_in.at[0, w_rows, lanes], wz_send.at[k], wz_recv.at[k], target(k), "expert"
        )

    def w_part(p, r):
        return w_in.at[r, pl.ds(p * half, half), lanes]

    def w_spread(p, bit, r):
        return remote(
            w_part(p, r), w_part(p, r ^ bit), w_send.at[p, r ^ bit], w_recv.at[p, r ^ bit], peer(bit)
        )

    def w_forward(p, r):
        return remote(w_part(p, r), w_part(p, r), wf_send.at[p, r], wf_recv.at[p, r], sibling)

    own = [pltpu.make_async_copy(kv[p], kv_in.at[p, 0, 0], local.at[p]) for p in range(2)]
    if given:
        own.append(pltpu.make_async_copy(w_ref, w_in.at[0], local.at[2]))
    else:
        own.append(pltpu.make_async_copy(w_piece(0), w_in.at[0, w_rows, lanes], local.at[2]))
    early = [
        pltpu.make_async_copy(seg_ref, seg_in, local.at[3]),
        pltpu.make_async_copy(rt_ref, rt_in, local.at[4]),
    ]
    late = [
        pltpu.make_async_copy(res_ref, res_in, local.at[5]),
        pltpu.make_async_copy(gain_ref.at[:, pl.ds(pl.multiple_of(group * cols, 128), cols)], gain_in, local.at[6]),
        pltpu.make_async_copy(router_ref, router_in, local.at[7]),
    ]
    for h in range(kv_heads):
        for g in range(pack):
            early.append(
                pltpu.make_async_copy(
                    q_ref.at[:, pl.ds((h * pack + g) * HD, HD)],
                    stacked.at[h, pl.ds(g * rows, rows), :],
                    q_local.at[h, g],
                )
            )
    for copy in own + early + late:
        copy.start()
    pl.semaphore_wait(barrier, steps + experts)
    for p in range(parts):
        kv_spread(p, orders[p][0], 0).start()
    for p in range(parts):
        kv_forward(p, 0).start()
    for t in range(1, steps):
        for p in range(parts):
            kv_spread(p, orders[p][t], 0).start()
    if not given:
        for k in range(experts - 1, 0, -1):
            lend(k).start()

    for copy in early:
        copy.wait()

    ids = lax.broadcasted_iota(jnp.int32, (16, rows), 0)
    routed = rt_in[0:1, :] == ids
    for j in range(1, rt_in.shape[0]):
        routed = routed | (rt_in[j : j + 1, :] == ids)
    earlier = lax.broadcasted_iota(jnp.int32, (rows, rows), 0) <= lax.broadcasted_iota(jnp.int32, (rows, rows), 1)
    counted = jnp.dot(
        jnp.where(routed, 1.0, 0.0).astype(low), jnp.where(earlier, 1.0, 0.0).astype(low), preferred_element_type=wide
    )
    index = jnp.where(routed, counted.astype(jnp.int32) - 1, -1)
    capacity = place.shape[1]
    slots = lax.broadcasted_iota(jnp.int32, (capacity, rows), 0)
    for e in range(experts):
        place[e] = jnp.where(index[e : e + 1, :] == slots, 1.0, 0.0).astype(low)
    mine_ref[...] = place[group]

    top[...] = jnp.full_like(top, -1e30)
    total_w[...] = jnp.zeros_like(total_w)
    acc[...] = jnp.zeros_like(acc)
    here = seg_in[:, pl.ds(pl.multiple_of(me * rows, 128), rows)].astype(wide)
    here = jnp.transpose(jnp.broadcast_to(here, (128, rows)))[:, :1]
    row_id = lax.broadcasted_iota(jnp.int32, (rows, rows), 0)
    col_id = lax.broadcasted_iota(jnp.int32, (rows, rows), 1)
    scale = 1.0 / math.sqrt(HD)

    def attend(h, r, c):
        block = across(chip, parts_of(r)) * 2 + (core if c == 0 else 1 - core)

        @pl.when(block <= me)
        def _():
            there = seg_in[:, pl.ds(pl.multiple_of(block * rows, 128), rows)].astype(wide)
            seen = (here == there) & (col_id + block * rows <= row_id + me * rows)
            seen = jnp.concatenate([seen.astype(jnp.int32)] * pack, axis=0) > 0
            keys = kv_in[0, r, c, :, h * HD : (h + 1) * HD]
            values = kv_in[1, r, c, :, h * HD : (h + 1) * HD]
            score = lax.dot_general(
                stacked[h], keys, (((1,), (1,)), ((), ())), preferred_element_type=wide
            ) * scale
            score = jnp.where(seen, score, -1e30)
            before = top[h]
            after = jnp.maximum(before, jnp.max(score, axis=-1, keepdims=True))
            shrink = jnp.exp(before - after)
            weight = jnp.where(seen, jnp.exp(score - after[:, :1]), 0.0)
            top[h] = after
            total_w[h] = total_w[h] * shrink + jnp.sum(weight, axis=-1, keepdims=True)
            acc[h] = acc[h] * shrink + jnp.dot(weight.astype(low), values, preferred_element_type=wide)

    for copy in own[:2]:
        copy.wait()
    for h in range(kv_heads):
        attend(h, 0, 0)
    for p in range(parts):
        kv_forward(p, 0).wait_recv()
    for h in range(kv_heads):
        attend(h, 0, 1)

    def take(spread, onward, got, p, r):
        if r not in got[p]:
            spread(p, orders[p][0], r ^ orders[p][0]).wait_recv()
            onward(p, r).start()
            got[p].add(r)

    def relay(spread, onward, got, t, skip):
        for p in range(parts):
            for r in span(orders[p][:t]):
                take(spread, onward, got, p, r)
        for k in range(skip, 1 << t):
            for p in range(parts):
                spread(p, orders[p][t], span(orders[p][:t])[k]).start()

    got = [{0} for _ in range(parts)]
    for t in range(1, steps):
        relay(kv_spread, kv_forward, got, t, 1)
    rest = sorted(range(1, chips), key=lambda r: (len(parts_of(r)), r))
    w_got = [{0} for _ in range(parts)]
    for r in rest:
        for p in range(parts):
            take(kv_spread, kv_forward, got, p, r)
    if not given:
        own[2].wait()
        for k in range(1, experts):
            lend(k).wait_recv()
        for p in range(parts):
            w_spread(p, orders[p][0], 0).start()
        for p in range(parts):
            w_forward(p, 0).start()
        for t in range(1, steps):
            for p in range(parts):
                w_spread(p, orders[p][t], 0).start()
    for r in rest:
        for p in range(parts):
            kv_forward(p, r).wait_recv()

    def part(h):
        return pl.ds(h * pack * HD, pack * HD)

    def share_heads(h, bit, q):
        return remote(
            att_in.at[q, :, part(h)], att_in.at[q ^ bit, :, part(h)],
            a_send.at[h, q ^ bit], a_recv.at[h, q ^ bit], flip(group, bit), "expert",
        )

    for h in range(kv_heads):
        for r in rest:
            for c in range(2):
                attend(h, r, c)
        done = (acc[h] / total_w[h]).astype(low)
        for g in range(pack):
            at = (h * pack + g) * HD
            att_in[0, :, at : at + HD] = done[g * rows : (g + 1) * rows, :]
        for bit in zorder:
            share_heads(h, bit, 0).start()

    if given:
        own[2].wait()
    else:
        for t in range(1, steps):
            relay(w_spread, w_forward, w_got, t, 1)
    for copy in late:
        copy.wait()
    stream_ref[...] = res_in[...].astype(wide)
    z_got = {0}
    for t in range(1, zsteps):
        for q in span(zorder[:t]):
            if q not in z_got:
                z_got.add(q)
                for h in range(kv_heads):
                    share_heads(h, zorder[0], q ^ zorder[0]).wait_recv()
                    for bit in zorder[t:]:
                        share_heads(h, bit, q).start()
    if not given:
        for r in rest:
            for p in range(parts):
                take(w_spread, w_forward, w_got, p, r)
        for r in range(chips):
            for p in range(parts):
                w_forward(p, r).wait_recv()

    def project(q):
        g = across(group, parts_of(q))
        from_rows = pl.ds(pl.multiple_of(g * depth, depth), depth)
        if given:
            stream_ref[...] += jnp.dot(att_in[q], w_in[0, from_rows, :], preferred_element_type=wide)
        else:
            for r in range(chips):
                c = across(chip, parts_of(r)) * 2 * piece
                at = pl.ds(pl.multiple_of(c, 2 * piece), 2 * piece)
                stream_ref[:, at] += jnp.dot(att_in[q], w_in[r, from_rows, :], preferred_element_type=wide)

    for q in [0] + zorder + sorted(set(range(1, experts)) - set(zorder)):
        if q not in z_got:
            z_got.add(q)
            for h in range(kv_heads):
                share_heads(h, zorder[0], q ^ zorder[0]).wait_recv()
        project(q)

    def share_squares(k):
        return remote(squares.at[0], squares.at[k], s_send.at[k], s_recv.at[k], target(k), "expert")

    stream = stream_ref[...]
    total = jnp.sum(stream * stream, axis=-1, keepdims=True)
    squares[0] = jnp.transpose(jnp.broadcast_to(total, (rows, 128)))[:8, :]
    for k in range(1, experts):
        share_squares(k).start()
    for k in range(1, experts):
        share_squares(k).wait_recv()
    total = squares[0]
    for k in range(1, experts):
        total = total + squares[k]
    total = jnp.transpose(jnp.broadcast_to(total[:1, :], (128, rows)))[:, :1]
    inverse = lax.rsqrt(total * (1.0 / (cols * experts)) + 1e-05)
    normed = (stream_ref[...] * inverse * gain_in[...]).astype(low)
    for k in range(experts):
        chosen_ref[k] = jnp.dot(place[target(k)], normed, preferred_element_type=wide).astype(low)
    logit_ref[...] = lax.dot_general(
        router_in[...], normed, (((1,), (1,)), ((), ())), preferred_element_type=wide
    )
    for p in range(parts):
        for r in range(chips):
            kv_forward(p, r).wait_send()
            if r > 0:
                kv_spread(p, orders[p][0], r ^ orders[p][0]).wait_send()
            if not given:
                w_forward(p, r).wait_send()
                if r > 0:
                    w_spread(p, orders[p][0], r ^ orders[p][0]).wait_send()
    for h in range(kv_heads):
        for q in range(1, experts):
            share_heads(h, zorder[0], q ^ zorder[0]).wait_send()
    for k in range(1, experts):
        if not given:
            lend(k).wait_send()
        share_squares(k).wait_send()


def front(queries, keys, values, segments, routes_t, w_out, residual, gain, router, capacity):
    chips, experts = lax.axis_size("blk") // 2, lax.axis_size("expert")
    rows, cols = residual.shape
    depth = queries.shape[1]
    kv_heads = keys.shape[1] // HD
    pack = queries.shape[1] // keys.shape[1]
    low, wide = jnp.bfloat16, jnp.float32
    vmem, dma, shape = pl.BlockSpec(memory_space=pltpu.VMEM), pltpu.SemaphoreType.DMA, jax.ShapeDtypeStruct
    given = cols % (256 * chips) != 0
    if given:
        w_out = lax.all_to_all(w_out, "expert", 1, 0, tiled=True)
    w_shape = (1, depth * experts, cols) if given else (chips, depth * experts, cols // chips)
    return pl.pallas_call(
        functools.partial(front_kernel, chips, experts, given),
        out_shape=(
            shape((rows, cols), wide),
            shape((experts, capacity, cols), low),
            shape((router.shape[0], rows), wide),
            shape((capacity, rows), low),
        ),
        in_specs=[pl.BlockSpec(memory_space=pl.ANY)] * 9,
        out_specs=(vmem,) * 4,
        scratch_shapes=[
            pltpu.VMEM((2, chips, 2) + keys.shape, low),
            pltpu.VMEM(w_shape, low),
            pltpu.VMEM((experts, rows, depth), low),
            pltpu.VMEM((kv_heads, pack * rows, HD), low),
            pltpu.VMEM((kv_heads, pack * rows, HD), wide),
            pltpu.VMEM((kv_heads, pack * rows, HD), wide),
            pltpu.VMEM((kv_heads, pack * rows, HD), wide),
            pltpu.VMEM((experts, capacity, rows), low),
            pltpu.VMEM((experts, 8, rows), wide),
            pltpu.VMEM((rows, cols), low),
            pltpu.VMEM(segments.shape, jnp.int32),
            pltpu.VMEM(routes_t.shape, jnp.int32),
            pltpu.VMEM((1, cols), wide),
            pltpu.VMEM(router.shape, low),
            dma((8,)),
            dma((kv_heads, pack)),
        ]
        + [dma((2, chips))] * 4
        + [dma((experts,))] * 2
        + [dma((2, chips))] * 4
        + [dma((kv_heads, experts))] * 2
        + [dma((experts,))] * 2,
        compiler_params=pltpu.CompilerParams(
            collective_id=0, has_side_effects=True, vmem_limit_bytes=48 * 1024 * 1024
        ),
    )(queries, keys, values, segments, routes_t, w_out, residual, gain, router)


def expert_kernel(
    chips, experts, x_ref, wg_ref, wu_ref, wd_ref, stream_any, place_any, logit_any, rt_any, o_ref,
    rows_in, weights, hidden, leaving, sib_in, keep, part_in, own_out, strips, strip_in, scatter, share,
    stream_ref, place_ref, logit_ref, rt_ref,
    w_sem, d_sem, ag_send, ag_recv, fw_send, fw_recv, sib_send, sib_recv,
    rs_send, rs_recv, z_send, z_recv, x_send, x_recv, l_send, l_recv, small,
):
    me, group = lax.axis_index("blk"), lax.axis_index("expert")
    chip, core = me // 2, me % 2
    sibling = chip * 2 + 1 - core
    rows, width = x_ref.shape[1], x_ref.shape[2] * experts
    units = wg_ref.shape[1]
    tile = weights.shape[2]
    tiles = units // tile
    slots = 2 * tiles
    steps, zsteps = log2(chips), log2(experts)
    bits = [1 << b for b in range(steps)]
    zbits = [1 << b for b in range(zsteps)]
    parts = 2
    groups = 4
    orders = [bits[p % steps :] + bits[: p % steps] for p in range(parts)]
    tw = leaving.shape[2]
    pw = tw // parts
    total = width // tw
    per_tile = tw // tile
    piece = tw // experts
    subs = width // tile
    slab = width // experts
    own_rows = o_ref.shape[0]
    low = jnp.bfloat16

    def peer(bit):
        return flip(chip, bit) * 2 + core

    barrier = pltpu.get_barrier_semaphore()
    pl.semaphore_signal(barrier, inc=1, device_id={"blk": sibling}, device_id_type=MESH)
    for bit in bits:
        pl.semaphore_signal(barrier, inc=1, device_id={"blk": peer(bit)}, device_id_type=MESH)
    for e in range(1, experts):
        pl.semaphore_signal(barrier, inc=1, device_id={"expert": (group + e) % experts}, device_id_type=MESH)

    def load(f, side):
        src = (wg_ref, wu_ref)[side]
        return pltpu.make_async_copy(
            src.at[:, pl.ds(pl.multiple_of(f * tile, 128), tile)], weights.at[2 * f + side], w_sem.at[2 * f + side]
        )

    def load_down(m, i):
        column = (m % per_tile) * (tile // piece) + i
        column = column * slab + (m // per_tile) * piece
        slot = m % slots
        return pltpu.make_async_copy(
            wd_ref.at[:, pl.ds(pl.multiple_of(column, 128), piece)],
            weights.at[slot, pl.ds(0, units), pl.ds(i * piece, piece)],
            d_sem.at[slot, i],
        )

    cuts = [0]
    for p in range(groups):
        cuts.append(cuts[-1] + 16 * ((rows // 16 + groups - 1 - p) // groups))
    everything, early, late = list(range(groups)), [0, 1], [2, 3]
    by_distance = sorted(range(1, chips), key=lambda r: (len(parts_of(r)), r))
    near = [r for r in by_distance if len(parts_of(r)) == 1]
    units_of_work = [[(0, early)], [(r, early) for r in near], [(r, late) for r in [0] + near]]
    units_of_work += [[(r, everything)] for r in by_distance if r not in near]
    place_of, begins, count = {}, [], 0
    for work in units_of_work:
        begins.append(count)
        for r, which in work:
            for c in range(2):
                for p in which:
                    place_of[r, c, p] = count
                    count += cuts[p + 1] - cuts[p]
    begins.append(count)

    def lot(r, c, p):
        return rows_in.at[pl.ds(place_of[r, c, p], cuts[p + 1] - cuts[p]), :]

    def slab_of(g):
        return pl.ds(pl.multiple_of(g * slab, 128), slab)

    def dispatch(k, p, g):
        take_rows = pl.ds(cuts[p], cuts[p + 1] - cuts[p])
        put_rows = pl.ds(place_of[0, 0, p], cuts[p + 1] - cuts[p])
        source, goal = x_ref.at[k, take_rows, :], rows_in.at[put_rows, slab_of(g)]
        if k == 0:
            return pltpu.make_async_copy(source, goal, x_send.at[0, p])
        return remote(source, goal, x_send.at[k, p], x_recv.at[k, p], (group + k) % experts, "expert")

    def share_logits(k):
        if k == 0:
            return pltpu.make_async_copy(logit_any, logit_ref.at[0], l_send.at[0])
        return remote(logit_any, logit_ref.at[k], l_send.at[k], l_recv.at[k], (group + k) % experts, "expert")

    def order(p):
        return bits[p % steps :] + bits[: p % steps]

    def spread(p, bit, r):
        return remote(
            lot(r, 0, p), lot(r ^ bit, 0, p), ag_send.at[p, r ^ bit], ag_recv.at[p, r ^ bit], peer(bit)
        )

    def forward(p, r):
        return remote(lot(r, 0, p), lot(r, 1, p), fw_send.at[p, r], fw_recv.at[p, r], sibling)

    got = set()

    def take(p, r):
        if (p, r) in got:
            return
        got.add((p, r))
        if r == 0:
            dispatch(0, p, group).wait()
            for e in range(1, experts):
                dispatch(e, p, (group + experts - e) % experts).wait_recv()
            onward = order(p)
        else:
            bit = order(p)[0]
            spread(p, bit, r ^ bit).wait_recv()
            onward = order(p)[max(order(p).index(b) for b in parts_of(r)) + 1 :]
        for bit in onward:
            spread(p, bit, r).start()
        forward(p, r).start()

    def begin_dispatch(p):
        for e in range(experts - 1, -1, -1):
            dispatch(e, p, group).start()

    smalls = [
        pltpu.make_async_copy(stream_any, stream_ref, small.at[0]),
        pltpu.make_async_copy(place_any, place_ref, small.at[1]),
        pltpu.make_async_copy(rt_any, rt_ref, small.at[2]),
    ]
    pl.semaphore_wait(barrier, steps + experts)
    begin_dispatch(0)
    begin_dispatch(1)
    for e in range(experts):
        share_logits(e).start()
    for copy in smalls:
        copy.start()

    @pl.loop(0, tiles)
    def _(f):
        load(f, 0).start()
        load(f, 1).start()

    take(0, 0)
    begin_dispatch(2)
    take(1, 0)
    begin_dispatch(3)

    for copy in smalls:
        copy.wait()
    share_logits(0).wait()
    for e in range(1, experts):
        share_logits(e).wait_recv()
    logit = logit_ref[0]
    for e in range(1, experts):
        logit = logit + logit_ref[e]
    tokens_here = rt_ref.shape[1]
    ids = lax.broadcasted_iota(jnp.int32, logit.shape, 0)
    routed = rt_ref[0:1, :] == ids
    for j in range(1, rt_ref.shape[0]):
        routed = routed | (rt_ref[j : j + 1, :] == ids)
    score = jnp.where(routed, 1.0 / (1.0 + jnp.exp(-logit)), 0.0)
    fraction = jnp.sum(jnp.where(ids == group, score, 0.0), axis=0, keepdims=True) / jnp.sum(
        score, axis=0, keepdims=True
    )
    share[...] = jnp.transpose(jnp.broadcast_to(fraction, (128, tokens_here)))

    def up_tiles(u, begin, end):
        size = begins[u + 1] - begins[u]

        def body(f):
            if u == 0:
                load(f, 0).wait()
                load(f, 1).wait()
            tokens = rows_in[begins[u] : begins[u + 1], :]
            gate = jnp.dot(tokens, weights[2 * f], preferred_element_type=jnp.float32)
            up = jnp.dot(tokens, weights[2 * f + 1], preferred_element_type=jnp.float32)
            act = (gate / (1.0 + jnp.exp(-gate)) * up).astype(low)
            at = pl.ds(pl.multiple_of(f * tile, 128), tile)
            for r, which in units_of_work[u]:
                for c in range(2):
                    start = place_of[r, c, which[0]] - begins[u]
                    length = cuts[which[-1] + 1] - cuts[which[0]]
                    to = r * rows + cuts[which[0]]
                    hidden[c, to : to + length, at] = act[start : start + length]
            if u == len(units_of_work) - 1:
                for side in range(2):
                    m = 2 * f + side

                    @pl.when(m < subs)
                    def _():
                        for i in range(tile // piece):
                            load_down(m, i).start()

        pl.loop(begin, end, unroll=1)(body)

    middle = tiles // 2
    for u, work in enumerate(units_of_work):
        for r, which in work:
            for p in which:
                take(p, r)
        for r, which in work:
            for p in which:
                forward(p, r).wait_recv()
        up_tiles(u, 0, middle)
        if u <= 1:
            take(2 + u, 0)
        elif u + 1 < len(units_of_work):
            for r, which in units_of_work[u + 1]:
                for p in which:
                    take(p, r)
        up_tiles(u, middle, tiles)

    moves = []
    for t in range(steps):
        step = []
        for p in range(parts):
            for i, left in enumerate(span(orders[p][t + 1 :])):
                step.append((p, left | orders[p][t], left, i))
        moves.append(step)
    base = [sum(len(s) for s in moves[:t]) for t in range(steps)]
    zmoves = [[(left | zbits[u], left) for left in span(zbits[u + 1 :])] for u in range(zsteps)]
    zbase = [sum(len(s) for s in zmoves[:u]) for u in range(zsteps)]

    def exchange(n):
        return remote(leaving.at[n % 2], sib_in.at[n], sib_send.at[n], sib_recv.at[n], sibling)

    def block(r):
        return pl.ds(r * rows, rows)

    def deliver(n, t, k):
        p, sent, _, _ = moves[t][k]
        at = base[t] + k
        return remote(
            sib_in.at[n, block(sent), pl.ds(p * pw, pw)], part_in.at[n, at],
            rs_send.at[n, at], rs_recv.at[n, at], peer(orders[p][t]),
        )

    def hand(n, u, k):
        sent, _ = zmoves[u][k]
        at = zbase[u] + k
        return remote(
            strips.at[n, sent - 1], strip_in.at[n, at], z_send.at[n, at], z_recv.at[n, at],
            flip(group, zbits[u]), "expert",
        )

    def down(c, n, i):
        slot = (n * per_tile + i) % slots
        return jnp.dot(hidden[c], weights[slot, :units, :], preferred_element_type=jnp.float32)

    def leave(n):
        for i in range(per_tile):
            for j in range(tile // piece):
                load_down(n * per_tile + i, j).wait()

        @pl.when(n >= 2)
        def _():
            exchange(n - 2).wait_send()

        for i in range(per_tile):
            leaving[n % 2, :, i * tile : (i + 1) * tile] = down(1, n, i).astype(low)
        exchange(n).start()

    def stay(n):
        for i in range(per_tile):
            keep[:, i * tile : (i + 1) * tile] = down(0, n, i)
        for i in range(per_tile):
            m = n * per_tile + i + slots

            @pl.when(m < subs)
            def _():
                for j in range(tile // piece):
                    load_down(m, j).start()

    def join(n):
        exchange(n).wait_recv()
        sib_in[n] = (keep[...] + sib_in[n].astype(jnp.float32)).astype(low)
        for k in range(len(moves[0])):
            deliver(n, 0, k).start()

    def gather_step(n, t):
        for k, (p, _, left, _) in enumerate(moves[t]):
            deliver(n, t, k).wait_recv()
            at = (block(left), pl.ds(p * pw, pw))
            mine = sib_in[n, at[0], at[1]].astype(jnp.float32)
            sib_in[n, at[0], at[1]] = (mine + part_in[n, base[t] + k].astype(jnp.float32)).astype(low)
        if t + 1 < steps:
            for k in range(len(moves[t + 1])):
                deliver(n, t + 1, k).start()
        else:
            mix = share[:, :1] * lax.dot_general(
                place_ref[...], sib_in[n, :rows, :], (((0,), (0,)), ((), ())), preferred_element_type=jnp.float32
            )
            column = pl.ds(pl.multiple_of(n * piece, 128), piece)
            scatter[...] = mix
            mine = pl.ds(pl.multiple_of(group * piece, 128), piece)
            scatter[:, mine] += stream_ref[:, column]
            for q in range(experts):
                start = across(group, parts_of(q)) * own_rows
                strip = scatter[pl.ds(pl.multiple_of(start, own_rows), own_rows), :]
                if q == 0:
                    own_out[n] = strip
                else:
                    strips[n, q - 1] = strip.astype(low)
            for k in range(len(zmoves[0])):
                hand(n, 0, k).start()

    def combine_step(n, u):
        for k, (_, left) in enumerate(zmoves[u]):
            hand(n, u, k).wait_recv()
            theirs = strip_in[n, zbase[u] + k].astype(jnp.float32)
            if left == 0:
                own_out[n] += theirs
            else:
                strips[n, left - 1] = (strips[n, left - 1].astype(jnp.float32) + theirs).astype(low)
        if u + 1 < zsteps:
            for k in range(len(zmoves[u + 1])):
                hand(n, u + 1, k).start()
        else:
            column = n * piece
            for g in range(experts):
                at = pl.ds(pl.multiple_of(g * slab + column, 128), piece)
                o_ref[:, at] = own_out[n, :, g * piece : (g + 1) * piece].astype(o_ref.dtype)

    lag = 1 + steps + zsteps

    @pl.loop(0, total + lag)
    def _(n):
        @pl.when(n < total)
        def _():
            leave(n)

        @pl.when((n >= 1) & (n - 1 < total))
        def _():
            join(n - 1)

        @pl.when(n < total)
        def _():
            stay(n)

        for t in range(steps):
            @pl.when((n >= 2 + t) & (n - 2 - t < total))
            def _():
                gather_step(n - 2 - t, t)

        for u in range(zsteps):
            @pl.when((n >= 2 + steps + u) & (n - 2 - steps - u < total))
            def _():
                combine_step(n - 2 - steps - u, u)

    for n in range(max(0, total - 2), total):
        exchange(n).wait_send()
    for e in range(1, experts):
        share_logits(e).wait_send()
        for p in range(groups):
            dispatch(e, p, group).wait_send()
    for p in range(groups):
        for r in range(chips):
            forward(p, r).wait_send()
            if r > 0:
                spread(p, order(p)[0], r ^ order(p)[0]).wait_send()

    @pl.loop(0, total)
    def _(n):
        for t in range(steps):
            for k in range(len(moves[t])):
                deliver(n, t, k).wait_send()
        for u in range(zsteps):
            for k in range(len(zmoves[u])):
                hand(n, u, k).wait_send()


def expert_layer(x, gate_w, up_w, down_w, stream, place, logits, routes_t):
    chips, experts = lax.axis_size("blk") // 2, lax.axis_size("expert")
    rows, width = x.shape[1], x.shape[2] * experts
    units = gate_w.shape[1]
    tile = 256 if units % 256 == 0 else 128
    tokens = stream.shape[0]
    tw = 128 * experts
    total = width // tw
    dma = pltpu.SemaphoreType.DMA
    low, wide = jnp.bfloat16, jnp.float32
    vmem = pl.BlockSpec(memory_space=pltpu.VMEM)
    anywhere = pl.BlockSpec(memory_space=pl.ANY)
    own_rows = tokens // experts
    slots = 2 * (units // tile)
    moved = 2 * (chips - 1)
    return pl.pallas_call(
        functools.partial(expert_kernel, chips, experts),
        out_shape=jax.ShapeDtypeStruct((own_rows, width), low),
        in_specs=[anywhere] * 8,
        out_specs=vmem,
        scratch_shapes=[
            pltpu.VMEM((2 * chips * rows, width), low),
            pltpu.VMEM((slots, width, tile), low),
            pltpu.VMEM((2, chips * rows, units), low),
            pltpu.VMEM((2, chips * rows, tw), low),
            pltpu.VMEM((total, chips * rows, tw), low),
            pltpu.VMEM((chips * rows, tw), wide),
            pltpu.VMEM((total, moved, rows, tw // 2), low),
            pltpu.VMEM((total, own_rows, tw), wide),
            pltpu.VMEM((total, experts - 1, own_rows, tw), low),
            pltpu.VMEM((total, experts - 1, own_rows, tw), low),
            pltpu.VMEM((tokens, tw), wide),
            pltpu.VMEM((tokens, 128), wide),
            pltpu.VMEM(stream.shape, wide),
            pltpu.VMEM(place.shape, low),
            pltpu.VMEM((experts,) + logits.shape, wide),
            pltpu.VMEM(routes_t.shape, jnp.int32),
            dma((slots,)),
            dma((slots, tile // 128)),
            dma((4, chips)),
            dma((4, chips)),
            dma((4, chips)),
            dma((4, chips)),
            dma((total,)),
            dma((total,)),
            dma((total, moved)),
            dma((total, moved)),
            dma((total, experts - 1)),
            dma((total, experts - 1)),
            dma((experts, 4)),
            dma((experts, 4)),
            dma((experts,)),
            dma((experts,)),
            dma((3,)),
        ],
        compiler_params=pltpu.CompilerParams(
            collective_id=1, has_side_effects=True, vmem_limit_bytes=61 * 1024 * 1024
        ),
    )(x, gate_w, up_w, down_w, stream, place, logits, routes_t)


def on_device(
    residual,
    queries,
    key_cache,
    value_cache,
    segments,
    routes,
    w_out,
    norm_gain,
    w_router,
    w_gate,
    w_up,
    w_down,
):
    experts = w_router.shape[1]
    cols = residual.shape[1]
    first_col = lax.axis_index("expert") * cols
    capacity = queries.shape[0] * TOP * 9 // (8 * experts)
    capacity = -(-capacity // 16) * 16
    router = lax.dynamic_slice_in_dim(w_router, first_col, cols, 0).T
    router = jnp.pad(router, ((0, -experts % 16), (0, 0)))
    routes_t = routes.T
    stream, chosen, logits, place = front(
        queries, key_cache, value_cache, segments[None, :], routes_t, w_out, residual, norm_gain[None, :], router, capacity
    )
    return expert_layer(chosen, w_gate[0], w_up[0], w_down[0], stream, place, logits, routes_t)


def solution(mesh):
    return jax.shard_map(
        on_device,
        mesh=mesh,
        in_specs=(
            P("blk", "expert"),
            P("blk", "expert"),
            P("blk", "expert"),
            P("blk", "expert"),
            P(),
            P("blk", None),
            P("expert", None),
            P(),
            P(),
            P("expert", None, "blk"),
            P("expert", None, "blk"),
            P("expert", "blk", None),
        ),
        out_specs=P(("blk", "expert"), None),
        check_vma=False,
    )
```

```python
import functools
import math

import jax
import jax.numpy as jnp
from jax import lax
from jax.experimental import pallas as pl
from jax.experimental.pallas import tpu as pltpu
from jax.sharding import PartitionSpec as P

HD = 128
TOP = 2

MESH = pl.DeviceIdType.MESH


def remote(src, dst, send_sem, recv_sem, target, axis="blk"):
    return pltpu.make_async_remote_copy(
        src_ref=src,
        dst_ref=dst,
        send_sem=send_sem,
        recv_sem=recv_sem,
        device_id={axis: target},
        device_id_type=MESH,
    )


def flip(index, bit):
    return index + bit * (1 - 2 * ((index // bit) % 2))


def across(index, bits):
    for bit in bits:
        index = flip(index, bit)
    return index


def log2(n):
    return n.bit_length() - 1


def parts_of(mask):
    return [1 << b for b in range(mask.bit_length()) if mask >> b & 1]


def span(order):
    found = [0]
    for bit in order:
        found += [f | bit for f in found]
    return found


def front_kernel(
    chips, experts, given, q_ref, k_ref, v_ref, seg_ref, rt_ref, w_ref, res_ref, gain_ref, router_ref,
    stream_any, chosen_any, logit_ref, mine_ref,
    stream_ref, chosen_ref, kv_in, w_in, att_in, stacked, top, total_w, acc, place, squares, res_in, seg_in, rt_in, gain_in, router_in,
    local, q_local, out_local,
    kv_send, kv_recv, kf_send, kf_recv, wz_send, wz_recv, w_send, w_recv, wf_send, wf_recv,
    a_send, a_recv, s_send, s_recv,
):
    me, group = lax.axis_index("blk"), lax.axis_index("expert")
    chip, core = me // 2, me % 2
    sibling = chip * 2 + 1 - core
    steps, zsteps = log2(chips), log2(experts)
    bits = [1 << b for b in range(steps)]
    zorder = [1 << b for b in range(zsteps)][::-1]
    parts = 2
    orders = [bits[p % steps :] + bits[: p % steps] for p in range(parts)]
    rows, cols = res_ref.shape
    kv_heads = k_ref.shape[1] // HD
    pack = q_ref.shape[1] // k_ref.shape[1]
    depth = q_ref.shape[1]
    wide, low = jnp.float32, jnp.bfloat16
    kv = (k_ref, v_ref)

    def peer(bit):
        return flip(chip, bit) * 2 + core

    def target(k):
        return (group + k) % experts

    barrier = pltpu.get_barrier_semaphore()
    pl.semaphore_signal(barrier, inc=1, device_id={"blk": sibling}, device_id_type=MESH)
    for bit in bits:
        pl.semaphore_signal(barrier, inc=1, device_id={"blk": peer(bit)}, device_id_type=MESH)
    for k in range(1, experts):
        pl.semaphore_signal(barrier, inc=1, device_id={"expert": target(k)}, device_id_type=MESH)

    def kv_from(p, r):
        return kv[p] if r == 0 else kv_in.at[p, r, 0]

    def kv_spread(p, bit, r):
        return remote(
            kv_from(p, r), kv_in.at[p, r ^ bit, 0], kv_send.at[p, r ^ bit], kv_recv.at[p, r ^ bit], peer(bit)
        )

    def kv_forward(p, r):
        return remote(kv_from(p, r), kv_in.at[p, r, 1], kf_send.at[p, r], kf_recv.at[p, r], sibling)

    piece = cols // (2 * chips)
    half = w_in.shape[1] // parts
    lanes = pl.ds(pl.multiple_of(core * piece, 128), piece)
    w_rows = pl.ds(pl.multiple_of(group * depth, depth), depth)

    def w_piece(k):
        return w_ref.at[:, pl.ds(pl.multiple_of(target(k) * cols + me * piece, 128), piece)]

    def lend(k):
        return remote(
            w_piece(k), w_in.at[0, w_rows, lanes], wz_send.at[k], wz_recv.at[k], target(k), "expert"
        )

    def w_part(p, r):
        return w_in.at[r, pl.ds(p * half, half), lanes]

    def w_spread(p, bit, r):
        return remote(
            w_part(p, r), w_part(p, r ^ bit), w_send.at[p, r ^ bit], w_recv.at[p, r ^ bit], peer(bit)
        )

    def w_forward(p, r):
        return remote(w_part(p, r), w_part(p, r), wf_send.at[p, r], wf_recv.at[p, r], sibling)

    own = [pltpu.make_async_copy(kv[p], kv_in.at[p, 0, 0], local.at[p]) for p in range(2)]
    if given:
        own.append(pltpu.make_async_copy(w_ref, w_in.at[0], local.at[2]))
    else:
        own.append(pltpu.make_async_copy(w_piece(0), w_in.at[0, w_rows, lanes], local.at[2]))
    early = [
        pltpu.make_async_copy(seg_ref, seg_in, local.at[3]),
        pltpu.make_async_copy(rt_ref, rt_in, local.at[4]),
    ]
    late = [
        pltpu.make_async_copy(res_ref, res_in, local.at[5]),
        pltpu.make_async_copy(gain_ref.at[:, pl.ds(pl.multiple_of(group * cols, 128), cols)], gain_in, local.at[6]),
        pltpu.make_async_copy(router_ref, router_in, local.at[7]),
    ]
    for h in range(kv_heads):
        for g in range(pack):
            early.append(
                pltpu.make_async_copy(
                    q_ref.at[:, pl.ds((h * pack + g) * HD, HD)],
                    stacked.at[h, pl.ds(g * rows, rows), :],
                    q_local.at[h, g],
                )
            )
    for copy in own + early + late:
        copy.start()
    pl.semaphore_wait(barrier, steps + experts)
    for p in range(parts):
        kv_spread(p, orders[p][0], 0).start()
    for p in range(parts):
        kv_forward(p, 0).start()
    for t in range(1, steps):
        for p in range(parts):
            kv_spread(p, orders[p][t], 0).start()
    if not given:
        for k in range(experts - 1, 0, -1):
            lend(k).start()

    for copy in early:
        copy.wait()

    ids = lax.broadcasted_iota(jnp.int32, (16, rows), 0)
    routed = rt_in[0:1, :] == ids
    for j in range(1, rt_in.shape[0]):
        routed = routed | (rt_in[j : j + 1, :] == ids)
    earlier = lax.broadcasted_iota(jnp.int32, (rows, rows), 0) <= lax.broadcasted_iota(jnp.int32, (rows, rows), 1)
    counted = jnp.dot(
        jnp.where(routed, 1.0, 0.0).astype(low), jnp.where(earlier, 1.0, 0.0).astype(low), preferred_element_type=wide
    )
    index = jnp.where(routed, counted.astype(jnp.int32) - 1, -1)
    capacity = place.shape[1]
    slots = lax.broadcasted_iota(jnp.int32, (capacity, rows), 0)
    for e in range(experts):
        place[e] = jnp.where(index[e : e + 1, :] == slots, 1.0, 0.0).astype(low)
    mine_ref[...] = place[group]

    top[...] = jnp.full_like(top, -1e30)
    total_w[...] = jnp.zeros_like(total_w)
    acc[...] = jnp.zeros_like(acc)
    here = seg_in[:, pl.ds(pl.multiple_of(me * rows, 128), rows)].astype(wide)
    here = jnp.transpose(jnp.broadcast_to(here, (128, rows)))[:, :1]
    row_id = lax.broadcasted_iota(jnp.int32, (rows, rows), 0)
    col_id = lax.broadcasted_iota(jnp.int32, (rows, rows), 1)
    scale = 1.0 / math.sqrt(HD)

    def attend(h, r, c):
        block = across(chip, parts_of(r)) * 2 + (core if c == 0 else 1 - core)

        @pl.when(block <= me)
        def _():
            there = seg_in[:, pl.ds(pl.multiple_of(block * rows, 128), rows)].astype(wide)
            seen = (here == there) & (col_id + block * rows <= row_id + me * rows)
            seen = jnp.concatenate([seen.astype(jnp.int32)] * pack, axis=0) > 0
            keys = kv_in[0, r, c, :, h * HD : (h + 1) * HD]
            values = kv_in[1, r, c, :, h * HD : (h + 1) * HD]
            score = lax.dot_general(
                stacked[h], keys, (((1,), (1,)), ((), ())), preferred_element_type=wide
            ) * scale
            score = jnp.where(seen, score, -1e30)
            before = top[h]
            after = jnp.maximum(before, jnp.max(score, axis=-1, keepdims=True))
            shrink = jnp.exp(before - after)
            weight = jnp.where(seen, jnp.exp(score - after[:, :1]), 0.0)
            top[h] = after
            total_w[h] = total_w[h] * shrink + jnp.sum(weight, axis=-1, keepdims=True)
            acc[h] = acc[h] * shrink + jnp.dot(weight.astype(low), values, preferred_element_type=wide)

    for copy in own[:2]:
        copy.wait()
    for h in range(kv_heads):
        attend(h, 0, 0)
    for p in range(parts):
        kv_forward(p, 0).wait_recv()
    for h in range(kv_heads):
        attend(h, 0, 1)

    def take(spread, onward, got, p, r):
        if r not in got[p]:
            spread(p, orders[p][0], r ^ orders[p][0]).wait_recv()
            onward(p, r).start()
            got[p].add(r)

    def relay(spread, onward, got, t, skip):
        for p in range(parts):
            for r in span(orders[p][:t]):
                take(spread, onward, got, p, r)
        for k in range(skip, 1 << t):
            for p in range(parts):
                spread(p, orders[p][t], span(orders[p][:t])[k]).start()

    got = [{0} for _ in range(parts)]
    for t in range(1, steps):
        relay(kv_spread, kv_forward, got, t, 1)
    rest = sorted(range(1, chips), key=lambda r: (len(parts_of(r)), r))
    w_got = [{0} for _ in range(parts)]
    for r in rest:
        for p in range(parts):
            take(kv_spread, kv_forward, got, p, r)
    if not given:
        own[2].wait()
        for k in range(1, experts):
            lend(k).wait_recv()
        for p in range(parts):
            w_spread(p, orders[p][0], 0).start()
        for p in range(parts):
            w_forward(p, 0).start()
        for t in range(1, steps):
            for p in range(parts):
                w_spread(p, orders[p][t], 0).start()
    for r in rest:
        for p in range(parts):
            kv_forward(p, r).wait_recv()

    def part(h):
        return pl.ds(h * pack * HD, pack * HD)

    def share_heads(h, bit, q):
        return remote(
            att_in.at[q, :, part(h)], att_in.at[q ^ bit, :, part(h)],
            a_send.at[h, q ^ bit], a_recv.at[h, q ^ bit], flip(group, bit), "expert",
        )

    for h in range(kv_heads):
        for r in rest:
            for c in range(2):
                attend(h, r, c)
        done = (acc[h] / total_w[h]).astype(low)
        for g in range(pack):
            at = (h * pack + g) * HD
            att_in[0, :, at : at + HD] = done[g * rows : (g + 1) * rows, :]
        for bit in zorder:
            share_heads(h, bit, 0).start()

    if given:
        own[2].wait()
    else:
        for t in range(1, steps):
            relay(w_spread, w_forward, w_got, t, 1)
    for copy in late:
        copy.wait()
    stream_ref[...] = res_in[...].astype(wide)
    z_got = {0}
    for t in range(1, zsteps):
        for q in span(zorder[:t]):
            if q not in z_got:
                z_got.add(q)
                for h in range(kv_heads):
                    share_heads(h, zorder[0], q ^ zorder[0]).wait_recv()
                    for bit in zorder[t:]:
                        share_heads(h, bit, q).start()
    if not given:
        for r in rest:
            for p in range(parts):
                take(w_spread, w_forward, w_got, p, r)
        for r in range(chips):
            for p in range(parts):
                w_forward(p, r).wait_recv()

    def project(q):
        g = across(group, parts_of(q))
        from_rows = pl.ds(pl.multiple_of(g * depth, depth), depth)
        if given:
            stream_ref[...] += jnp.dot(att_in[q], w_in[0, from_rows, :], preferred_element_type=wide)
        else:
            for r in range(chips):
                c = across(chip, parts_of(r)) * 2 * piece
                at = pl.ds(pl.multiple_of(c, 2 * piece), 2 * piece)
                stream_ref[:, at] += jnp.dot(att_in[q], w_in[r, from_rows, :], preferred_element_type=wide)

    for q in [0] + zorder + sorted(set(range(1, experts)) - set(zorder)):
        if q not in z_got:
            z_got.add(q)
            for h in range(kv_heads):
                share_heads(h, zorder[0], q ^ zorder[0]).wait_recv()
        project(q)

    def share_squares(k):
        return remote(squares.at[0], squares.at[k], s_send.at[k], s_recv.at[k], target(k), "expert")

    leaving = [pltpu.make_async_copy(stream_ref, stream_any, out_local.at[experts])]
    leaving[0].start()
    stream = stream_ref[...]
    total = jnp.sum(stream * stream, axis=-1, keepdims=True)
    squares[0] = jnp.transpose(jnp.broadcast_to(total, (rows, 128)))[:8, :]
    for k in range(1, experts):
        share_squares(k).start()
    for k in range(1, experts):
        share_squares(k).wait_recv()
    total = squares[0]
    for k in range(1, experts):
        total = total + squares[k]
    total = jnp.transpose(jnp.broadcast_to(total[:1, :], (128, rows)))[:, :1]
    inverse = lax.rsqrt(total * (1.0 / (cols * experts)) + 1e-05)
    normed = (stream_ref[...] * inverse * gain_in[...]).astype(low)
    for k in range(experts):
        chosen_ref[k] = jnp.dot(place[target(k)], normed, preferred_element_type=wide).astype(low)
        leaving.append(pltpu.make_async_copy(chosen_ref.at[k], chosen_any.at[k], out_local.at[k]))
        leaving[-1].start()
    logit_ref[...] = lax.dot_general(
        router_in[...], normed, (((1,), (1,)), ((), ())), preferred_element_type=wide
    )
    for p in range(parts):
        for r in range(chips):
            kv_forward(p, r).wait_send()
            if r > 0:
                kv_spread(p, orders[p][0], r ^ orders[p][0]).wait_send()
            if not given:
                w_forward(p, r).wait_send()
                if r > 0:
                    w_spread(p, orders[p][0], r ^ orders[p][0]).wait_send()
    for h in range(kv_heads):
        for q in range(1, experts):
            share_heads(h, zorder[0], q ^ zorder[0]).wait_send()
    for k in range(1, experts):
        if not given:
            lend(k).wait_send()
        share_squares(k).wait_send()
    for copy in leaving:
        copy.wait()


def front(queries, keys, values, segments, routes_t, w_out, residual, gain, router, capacity):
    chips, experts = lax.axis_size("blk") // 2, lax.axis_size("expert")
    rows, cols = residual.shape
    depth = queries.shape[1]
    kv_heads = keys.shape[1] // HD
    pack = queries.shape[1] // keys.shape[1]
    low, wide = jnp.bfloat16, jnp.float32
    vmem, dma, shape = pl.BlockSpec(memory_space=pltpu.VMEM), pltpu.SemaphoreType.DMA, jax.ShapeDtypeStruct
    given = cols % (256 * chips) != 0
    if given:
        w_out = lax.all_to_all(w_out, "expert", 1, 0, tiled=True)
    w_shape = (1, depth * experts, cols) if given else (chips, depth * experts, cols // chips)
    return pl.pallas_call(
        functools.partial(front_kernel, chips, experts, given),
        out_shape=(
            shape((rows, cols), wide),
            shape((experts, capacity, cols), low),
            shape((router.shape[0], rows), wide),
            shape((capacity, rows), low),
        ),
        in_specs=[pl.BlockSpec(memory_space=pl.ANY)] * 9,
        out_specs=(pl.BlockSpec(memory_space=pl.ANY),) * 2 + (vmem,) * 2,
        scratch_shapes=[
            pltpu.VMEM((rows, cols), wide),
            pltpu.VMEM((experts, capacity, cols), low),
            pltpu.VMEM((2, chips, 2) + keys.shape, low),
            pltpu.VMEM(w_shape, low),
            pltpu.VMEM((experts, rows, depth), low),
            pltpu.VMEM((kv_heads, pack * rows, HD), low),
            pltpu.VMEM((kv_heads, pack * rows, HD), wide),
            pltpu.VMEM((kv_heads, pack * rows, HD), wide),
            pltpu.VMEM((kv_heads, pack * rows, HD), wide),
            pltpu.VMEM((experts, capacity, rows), low),
            pltpu.VMEM((experts, 8, rows), wide),
            pltpu.VMEM((rows, cols), low),
            pltpu.VMEM(segments.shape, jnp.int32),
            pltpu.VMEM(routes_t.shape, jnp.int32),
            pltpu.VMEM((1, cols), wide),
            pltpu.VMEM(router.shape, low),
            dma((8,)),
            dma((kv_heads, pack)),
            dma((experts + 1,)),
        ]
        + [dma((2, chips))] * 4
        + [dma((experts,))] * 2
        + [dma((2, chips))] * 4
        + [dma((kv_heads, experts))] * 2
        + [dma((experts,))] * 2,
        compiler_params=pltpu.CompilerParams(
            collective_id=0, has_side_effects=True, vmem_limit_bytes=61 * 1024 * 1024
        ),
    )(queries, keys, values, segments, routes_t, w_out, residual, gain, router)


def expert_kernel(
    chips, experts, x_ref, wg_ref, wu_ref, wd_ref, stream_any, place_any, logit_any, rt_any, o_ref,
    rows_in, weights, hidden, leaving, sib_in, keep, part_in, own_out, strips, strip_in, scatter, share,
    stream_ref, place_ref, logit_ref, rt_ref,
    w_sem, d_sem, ag_send, ag_recv, fw_send, fw_recv, sib_send, sib_recv,
    rs_send, rs_recv, z_send, z_recv, x_send, x_recv, l_send, l_recv, small,
):
    me, group = lax.axis_index("blk"), lax.axis_index("expert")
    chip, core = me // 2, me % 2
    sibling = chip * 2 + 1 - core
    rows, width = x_ref.shape[1], x_ref.shape[2] * experts
    units = wg_ref.shape[1]
    tile = weights.shape[2]
    tiles = units // tile
    slots = 2 * tiles
    steps, zsteps = log2(chips), log2(experts)
    bits = [1 << b for b in range(steps)]
    zbits = [1 << b for b in range(zsteps)]
    parts = 2
    groups = 4
    orders = [bits[p % steps :] + bits[: p % steps] for p in range(parts)]
    tw = leaving.shape[2]
    pw = tw // parts
    total = width // tw
    per_tile = tw // tile
    piece = tw // experts
    subs = width // tile
    slab = width // experts
    own_rows = o_ref.shape[0]
    low = jnp.bfloat16

    def peer(bit):
        return flip(chip, bit) * 2 + core

    barrier = pltpu.get_barrier_semaphore()
    pl.semaphore_signal(barrier, inc=1, device_id={"blk": sibling}, device_id_type=MESH)
    for bit in bits:
        pl.semaphore_signal(barrier, inc=1, device_id={"blk": peer(bit)}, device_id_type=MESH)
    for e in range(1, experts):
        pl.semaphore_signal(barrier, inc=1, device_id={"expert": (group + e) % experts}, device_id_type=MESH)

    def load(f, side):
        src = (wg_ref, wu_ref)[side]
        return pltpu.make_async_copy(
            src.at[:, pl.ds(pl.multiple_of(f * tile, 128), tile)], weights.at[2 * f + side], w_sem.at[2 * f + side]
        )

    def load_down(m, i):
        column = (m % per_tile) * (tile // piece) + i
        column = column * slab + (m // per_tile) * piece
        slot = m % slots
        return pltpu.make_async_copy(
            wd_ref.at[:, pl.ds(pl.multiple_of(column, 128), piece)],
            weights.at[slot, pl.ds(0, units), pl.ds(i * piece, piece)],
            d_sem.at[slot, i],
        )

    cuts = [0]
    for p in range(groups):
        cuts.append(cuts[-1] + 16 * ((rows // 16 + groups - 1 - p) // groups))
    early, late = [0, 1], [2, 3]
    by_distance = sorted(range(1, chips), key=lambda r: (len(parts_of(r)), r))
    near = [r for r in by_distance if len(parts_of(r)) == 1]
    far = [r for r in by_distance if r not in near]
    units_of_work = [
        [(0, early)],
        [(r, early) for r in near],
        [(r, early) for r in far] + [(0, late)],
        [(r, late) for r in near],
        [(r, late) for r in far],
    ]
    units_of_work = [work for work in units_of_work if work]
    place_of, begins, count = {}, [], 0
    for work in units_of_work:
        begins.append(count)
        for r, which in work:
            for c in range(2):
                for p in which:
                    place_of[r, c, p] = count
                    count += cuts[p + 1] - cuts[p]
    begins.append(count)

    def lot(r, c, p):
        return rows_in.at[pl.ds(place_of[r, c, p], cuts[p + 1] - cuts[p]), :]

    def slab_of(g):
        return pl.ds(pl.multiple_of(g * slab, 128), slab)

    def dispatch(k, p, g):
        take_rows = pl.ds(cuts[p], cuts[p + 1] - cuts[p])
        put_rows = pl.ds(place_of[0, 0, p], cuts[p + 1] - cuts[p])
        source, goal = x_ref.at[k, take_rows, :], rows_in.at[put_rows, slab_of(g)]
        if k == 0:
            return pltpu.make_async_copy(source, goal, x_send.at[0, p])
        return remote(source, goal, x_send.at[k, p], x_recv.at[k, p], (group + k) % experts, "expert")

    def share_logits(k):
        if k == 0:
            return pltpu.make_async_copy(logit_any, logit_ref.at[0], l_send.at[0])
        return remote(logit_any, logit_ref.at[k], l_send.at[k], l_recv.at[k], (group + k) % experts, "expert")

    def order(p):
        return bits[p % steps :] + bits[: p % steps]

    def spread(p, bit, r):
        return remote(
            lot(r, 0, p), lot(r ^ bit, 0, p), ag_send.at[p, r ^ bit], ag_recv.at[p, r ^ bit], peer(bit)
        )

    def forward(p, r):
        return remote(lot(r, 0, p), lot(r, 1, p), fw_send.at[p, r], fw_recv.at[p, r], sibling)

    got = set()

    def take(p, r):
        if (p, r) in got:
            return
        got.add((p, r))
        if r == 0:
            dispatch(0, p, group).wait()
            for e in range(1, experts):
                dispatch(e, p, (group + experts - e) % experts).wait_recv()
            onward = order(p)
        else:
            bit = order(p)[0]
            spread(p, bit, r ^ bit).wait_recv()
            onward = order(p)[max(order(p).index(b) for b in parts_of(r)) + 1 :]
        for bit in onward:
            spread(p, bit, r).start()
        forward(p, r).start()

    def begin_dispatch(p):
        for e in range(experts - 1, -1, -1):
            dispatch(e, p, group).start()

    smalls = [
        pltpu.make_async_copy(stream_any, stream_ref, small.at[0]),
        pltpu.make_async_copy(place_any, place_ref, small.at[1]),
        pltpu.make_async_copy(rt_any, rt_ref, small.at[2]),
    ]
    pl.semaphore_wait(barrier, steps + experts)
    begin_dispatch(0)
    begin_dispatch(1)
    for e in range(experts):
        share_logits(e).start()
    for copy in smalls:
        copy.start()

    @pl.loop(0, tiles)
    def _(f):
        load(f, 0).start()
        load(f, 1).start()

    take(0, 0)
    begin_dispatch(2)
    take(1, 0)
    begin_dispatch(3)

    for copy in smalls:
        copy.wait()
    share_logits(0).wait()
    for e in range(1, experts):
        share_logits(e).wait_recv()
    logit = logit_ref[0]
    for e in range(1, experts):
        logit = logit + logit_ref[e]
    tokens_here = rt_ref.shape[1]
    ids = lax.broadcasted_iota(jnp.int32, logit.shape, 0)
    routed = rt_ref[0:1, :] == ids
    for j in range(1, rt_ref.shape[0]):
        routed = routed | (rt_ref[j : j + 1, :] == ids)
    score = jnp.where(routed, 1.0 / (1.0 + jnp.exp(-logit)), 0.0)
    fraction = jnp.sum(jnp.where(ids == group, score, 0.0), axis=0, keepdims=True) / jnp.sum(
        score, axis=0, keepdims=True
    )
    share[...] = jnp.transpose(jnp.broadcast_to(fraction, (128, tokens_here)))

    def up_tiles(u, begin, end):
        size = begins[u + 1] - begins[u]

        def body(f):
            if u == 0:
                load(f, 0).wait()
                load(f, 1).wait()
            tokens = rows_in[begins[u] : begins[u + 1], :]
            gate = jnp.dot(tokens, weights[2 * f], preferred_element_type=jnp.float32)
            up = jnp.dot(tokens, weights[2 * f + 1], preferred_element_type=jnp.float32)
            act = (gate / (1.0 + jnp.exp(-gate)) * up).astype(low)
            at = pl.ds(pl.multiple_of(f * tile, 128), tile)
            for r, which in units_of_work[u]:
                for c in range(2):
                    start = place_of[r, c, which[0]] - begins[u]
                    length = cuts[which[-1] + 1] - cuts[which[0]]
                    to = r * rows + cuts[which[0]]
                    hidden[c, to : to + length, at] = act[start : start + length]
            if u == len(units_of_work) - 1:
                for side in range(2):
                    m = 2 * f + side

                    @pl.when(m < subs)
                    def _():
                        for i in range(tile // piece):
                            load_down(m, i).start()

        pl.loop(begin, end, unroll=1)(body)

    middle = tiles // 2
    for u, work in enumerate(units_of_work):
        for r, which in work:
            for p in which:
                take(p, r)
        for r, which in work:
            for p in which:
                forward(p, r).wait_recv()
        up_tiles(u, 0, middle)
        if u == 1:
            take(2, 0)
            take(3, 0)
        if u == 2:
            for r in near:
                take(2, r)
        up_tiles(u, middle, tiles)

    moves = []
    for t in range(steps):
        step = []
        for p in range(parts):
            for i, left in enumerate(span(orders[p][t + 1 :])):
                step.append((p, left | orders[p][t], left, i))
        moves.append(step)
    base = [sum(len(s) for s in moves[:t]) for t in range(steps)]
    zmoves = [[(left | zbits[u], left) for left in span(zbits[u + 1 :])] for u in range(zsteps)]
    zbase = [sum(len(s) for s in zmoves[:u]) for u in range(zsteps)]

    def exchange(n):
        return remote(leaving.at[n % 2], sib_in.at[n], sib_send.at[n], sib_recv.at[n], sibling)

    def block(r):
        return pl.ds(r * rows, rows)

    def deliver(n, t, k):
        p, sent, _, _ = moves[t][k]
        at = base[t] + k
        return remote(
            sib_in.at[n, block(sent), pl.ds(p * pw, pw)], part_in.at[n, at],
            rs_send.at[n, at], rs_recv.at[n, at], peer(orders[p][t]),
        )

    def hand(n, u, k):
        sent, _ = zmoves[u][k]
        at = zbase[u] + k
        return remote(
            strips.at[n, sent - 1], strip_in.at[n, at], z_send.at[n, at], z_recv.at[n, at],
            flip(group, zbits[u]), "expert",
        )

    def down(c, n, i):
        slot = (n * per_tile + i) % slots
        return jnp.dot(hidden[c], weights[slot, :units, :], preferred_element_type=jnp.float32)

    def leave(n):
        for i in range(per_tile):
            for j in range(tile // piece):
                load_down(n * per_tile + i, j).wait()

        @pl.when(n >= 2)
        def _():
            exchange(n - 2).wait_send()

        for i in range(per_tile):
            leaving[n % 2, :, i * tile : (i + 1) * tile] = down(1, n, i).astype(low)
        exchange(n).start()

    def stay(n):
        for i in range(per_tile):
            keep[:, i * tile : (i + 1) * tile] = down(0, n, i)
        for i in range(per_tile):
            m = n * per_tile + i + slots

            @pl.when(m < subs)
            def _():
                for j in range(tile // piece):
                    load_down(m, j).start()

    def join(n):
        exchange(n).wait_recv()
        sib_in[n] = (keep[...] + sib_in[n].astype(jnp.float32)).astype(low)
        for k in range(len(moves[0])):
            deliver(n, 0, k).start()

    def gather_step(n, t):
        for k, (p, _, left, _) in enumerate(moves[t]):
            deliver(n, t, k).wait_recv()
            at = (block(left), pl.ds(p * pw, pw))
            mine = sib_in[n, at[0], at[1]].astype(jnp.float32)
            sib_in[n, at[0], at[1]] = (mine + part_in[n, base[t] + k].astype(jnp.float32)).astype(low)
        if t + 1 < steps:
            for k in range(len(moves[t + 1])):
                deliver(n, t + 1, k).start()
        else:
            mix = share[:, :1] * lax.dot_general(
                place_ref[...], sib_in[n, :rows, :], (((0,), (0,)), ((), ())), preferred_element_type=jnp.float32
            )
            column = pl.ds(pl.multiple_of(n * piece, 128), piece)
            scatter[...] = mix
            mine = pl.ds(pl.multiple_of(group * piece, 128), piece)
            scatter[:, mine] += stream_ref[:, column]
            for q in range(experts):
                start = across(group, parts_of(q)) * own_rows
                strip = scatter[pl.ds(pl.multiple_of(start, own_rows), own_rows), :]
                if q == 0:
                    own_out[n] = strip
                else:
                    strips[n, q - 1] = strip.astype(low)
            for k in range(len(zmoves[0])):
                hand(n, 0, k).start()

    def combine_step(n, u):
        for k, (_, left) in enumerate(zmoves[u]):
            hand(n, u, k).wait_recv()
            theirs = strip_in[n, zbase[u] + k].astype(jnp.float32)
            if left == 0:
                own_out[n] += theirs
            else:
                strips[n, left - 1] = (strips[n, left - 1].astype(jnp.float32) + theirs).astype(low)
        if u + 1 < zsteps:
            for k in range(len(zmoves[u + 1])):
                hand(n, u + 1, k).start()
        else:
            column = n * piece
            for g in range(experts):
                at = pl.ds(pl.multiple_of(g * slab + column, 128), piece)
                o_ref[:, at] = own_out[n, :, g * piece : (g + 1) * piece].astype(o_ref.dtype)

    lag = 1 + steps + zsteps

    @pl.loop(0, total + lag)
    def _(n):
        @pl.when(n < total)
        def _():
            leave(n)

        @pl.when((n >= 1) & (n - 1 < total))
        def _():
            join(n - 1)

        @pl.when(n < total)
        def _():
            stay(n)

        for t in range(steps):
            @pl.when((n >= 2 + t) & (n - 2 - t < total))
            def _():
                gather_step(n - 2 - t, t)

        for u in range(zsteps):
            @pl.when((n >= 2 + steps + u) & (n - 2 - steps - u < total))
            def _():
                combine_step(n - 2 - steps - u, u)

    for n in range(max(0, total - 2), total):
        exchange(n).wait_send()
    for e in range(1, experts):
        share_logits(e).wait_send()
        for p in range(groups):
            dispatch(e, p, group).wait_send()
    for p in range(groups):
        for r in range(chips):
            forward(p, r).wait_send()
            if r > 0:
                spread(p, order(p)[0], r ^ order(p)[0]).wait_send()

    @pl.loop(0, total)
    def _(n):
        for t in range(steps):
            for k in range(len(moves[t])):
                deliver(n, t, k).wait_send()
        for u in range(zsteps):
            for k in range(len(zmoves[u])):
                hand(n, u, k).wait_send()


def expert_layer(x, gate_w, up_w, down_w, stream, place, logits, routes_t):
    chips, experts = lax.axis_size("blk") // 2, lax.axis_size("expert")
    rows, width = x.shape[1], x.shape[2] * experts
    units = gate_w.shape[1]
    tile = 256 if units % 256 == 0 else 128
    tokens = stream.shape[0]
    tw = 128 * experts
    total = width // tw
    dma = pltpu.SemaphoreType.DMA
    low, wide = jnp.bfloat16, jnp.float32
    vmem = pl.BlockSpec(memory_space=pltpu.VMEM)
    anywhere = pl.BlockSpec(memory_space=pl.ANY)
    own_rows = tokens // experts
    slots = 2 * (units // tile)
    moved = 2 * (chips - 1)
    return pl.pallas_call(
        functools.partial(expert_kernel, chips, experts),
        out_shape=jax.ShapeDtypeStruct((own_rows, width), low),
        in_specs=[anywhere] * 8,
        out_specs=vmem,
        scratch_shapes=[
            pltpu.VMEM((2 * chips * rows, width), low),
            pltpu.VMEM((slots, width, tile), low),
            pltpu.VMEM((2, chips * rows, units), low),
            pltpu.VMEM((2, chips * rows, tw), low),
            pltpu.VMEM((total, chips * rows, tw), low),
            pltpu.VMEM((chips * rows, tw), wide),
            pltpu.VMEM((total, moved, rows, tw // 2), low),
            pltpu.VMEM((total, own_rows, tw), wide),
            pltpu.VMEM((total, experts - 1, own_rows, tw), low),
            pltpu.VMEM((total, experts - 1, own_rows, tw), low),
            pltpu.VMEM((tokens, tw), wide),
            pltpu.VMEM((tokens, 128), wide),
            pltpu.VMEM(stream.shape, wide),
            pltpu.VMEM(place.shape, low),
            pltpu.VMEM((experts,) + logits.shape, wide),
            pltpu.VMEM(routes_t.shape, jnp.int32),
            dma((slots,)),
            dma((slots, tile // 128)),
            dma((4, chips)),
            dma((4, chips)),
            dma((4, chips)),
            dma((4, chips)),
            dma((total,)),
            dma((total,)),
            dma((total, moved)),
            dma((total, moved)),
            dma((total, experts - 1)),
            dma((total, experts - 1)),
            dma((experts, 4)),
            dma((experts, 4)),
            dma((experts,)),
            dma((experts,)),
            dma((3,)),
        ],
        compiler_params=pltpu.CompilerParams(
            collective_id=1, has_side_effects=True, vmem_limit_bytes=61 * 1024 * 1024
        ),
    )(x, gate_w, up_w, down_w, stream, place, logits, routes_t)


def on_device(
    residual,
    queries,
    key_cache,
    value_cache,
    segments,
    routes,
    w_out,
    norm_gain,
    w_router,
    w_gate,
    w_up,
    w_down,
):
    experts = w_router.shape[1]
    cols = residual.shape[1]
    first_col = lax.axis_index("expert") * cols
    capacity = queries.shape[0] * TOP * 9 // (8 * experts)
    capacity = -(-capacity // 16) * 16
    router = lax.dynamic_slice_in_dim(w_router, first_col, cols, 0).T
    router = jnp.pad(router, ((0, -experts % 16), (0, 0)))
    routes_t = routes.T
    stream, chosen, logits, place = front(
        queries, key_cache, value_cache, segments[None, :], routes_t, w_out, residual, norm_gain[None, :], router, capacity
    )
    return expert_layer(chosen, w_gate[0], w_up[0], w_down[0], stream, place, logits, routes_t)


def solution(mesh):
    return jax.shard_map(
        on_device,
        mesh=mesh,
        in_specs=(
            P("blk", "expert"),
            P("blk", "expert"),
            P("blk", "expert"),
            P("blk", "expert"),
            P(),
            P("blk", None),
            P("expert", None),
            P(),
            P(),
            P("expert", None, "blk"),
            P("expert", None, "blk"),
            P("expert", "blk", None),
        ),
        out_specs=P(("blk", "expert"), None),
        check_vma=False,
    )
```

```python
import functools
import math

import jax
import jax.numpy as jnp
from jax import lax
from jax.experimental import pallas as pl
from jax.experimental.pallas import tpu as pltpu
from jax.sharding import PartitionSpec as P

HD = 128
TOP = 2

MESH = pl.DeviceIdType.MESH


def remote(src, dst, send_sem, recv_sem, target, axis="blk"):
    return pltpu.make_async_remote_copy(
        src_ref=src,
        dst_ref=dst,
        send_sem=send_sem,
        recv_sem=recv_sem,
        device_id={axis: target},
        device_id_type=MESH,
    )


def flip(index, bit):
    return index + bit * (1 - 2 * ((index // bit) % 2))


def across(index, bits):
    for bit in bits:
        index = flip(index, bit)
    return index


def log2(n):
    return n.bit_length() - 1


def parts_of(mask):
    return [1 << b for b in range(mask.bit_length()) if mask >> b & 1]


def span(order):
    found = [0]
    for bit in order:
        found += [f | bit for f in found]
    return found


def front_kernel(
    chips, experts, given, q_ref, k_ref, v_ref, seg_ref, rt_ref, w_ref, res_ref, gain_ref, router_ref,
    stream_any, chosen_any, logit_ref, mine_ref,
    stream_ref, chosen_ref, kv_in, w_in, att_in, stacked, top, total_w, acc, place, squares, res_in, seg_in, rt_in, gain_in, router_in,
    local, q_local, out_local,
    kv_send, kv_recv, kf_send, kf_recv, wz_send, wz_recv, w_send, w_recv, wf_send, wf_recv,
    a_send, a_recv, s_send, s_recv,
):
    me, group = lax.axis_index("blk"), lax.axis_index("expert")
    chip, core = me // 2, me % 2
    sibling = chip * 2 + 1 - core
    steps, zsteps = log2(chips), log2(experts)
    bits = [1 << b for b in range(steps)]
    zorder = [1 << b for b in range(zsteps)][::-1]
    parts = 2
    orders = [bits[p % steps :] + bits[: p % steps] for p in range(parts)]
    rows, cols = res_ref.shape
    kv_heads = k_ref.shape[1] // HD
    pack = q_ref.shape[1] // k_ref.shape[1]
    depth = q_ref.shape[1]
    wide, low = jnp.float32, jnp.bfloat16
    kv = (k_ref, v_ref)

    def peer(bit):
        return flip(chip, bit) * 2 + core

    def target(k):
        return (group + k) % experts

    barrier = pltpu.get_barrier_semaphore()
    pl.semaphore_signal(barrier, inc=1, device_id={"blk": sibling}, device_id_type=MESH)
    for bit in bits:
        pl.semaphore_signal(barrier, inc=1, device_id={"blk": peer(bit)}, device_id_type=MESH)
    for k in range(1, experts):
        pl.semaphore_signal(barrier, inc=1, device_id={"expert": target(k)}, device_id_type=MESH)

    def kv_from(p, r):
        return kv[p] if r == 0 else kv_in.at[p, r, 0]

    def kv_spread(p, bit, r):
        return remote(
            kv_from(p, r), kv_in.at[p, r ^ bit, 0], kv_send.at[p, r ^ bit], kv_recv.at[p, r ^ bit], peer(bit)
        )

    def kv_forward(p, r):
        return remote(kv_from(p, r), kv_in.at[p, r, 1], kf_send.at[p, r], kf_recv.at[p, r], sibling)

    piece = cols // (2 * chips)
    lanes = pl.ds(pl.multiple_of(core * piece, 128), piece)
    w_rows = pl.ds(pl.multiple_of(group * depth, depth), depth)

    def w_piece(k):
        return w_ref.at[:, pl.ds(pl.multiple_of(target(k) * cols + me * piece, 128), piece)]

    def lend(k):
        return remote(
            w_piece(k), w_in.at[0, w_rows, lanes], wz_send.at[k], wz_recv.at[k], target(k), "expert"
        )

    def w_part(p, r):
        return w_in.at[r, pl.ds(pl.multiple_of(target(p) * depth, depth), depth), lanes]

    def w_spread(p, bit, r):
        return remote(
            w_part(p, r), w_part(p, r ^ bit), w_send.at[p, r ^ bit], w_recv.at[p, r ^ bit], peer(bit)
        )

    def w_forward(p, r):
        return remote(w_part(p, r), w_part(p, r), wf_send.at[p, r], wf_recv.at[p, r], sibling)

    own = [pltpu.make_async_copy(kv[p], kv_in.at[p, 0, 0], local.at[p]) for p in range(2)]
    if given:
        own.append(pltpu.make_async_copy(w_ref, w_in.at[0], local.at[2]))
    else:
        own.append(pltpu.make_async_copy(w_piece(0), w_in.at[0, w_rows, lanes], local.at[2]))
    early = [
        pltpu.make_async_copy(seg_ref, seg_in, local.at[3]),
        pltpu.make_async_copy(rt_ref, rt_in, local.at[4]),
    ]
    late = [
        pltpu.make_async_copy(res_ref, res_in, local.at[5]),
        pltpu.make_async_copy(gain_ref.at[:, pl.ds(pl.multiple_of(group * cols, 128), cols)], gain_in, local.at[6]),
        pltpu.make_async_copy(router_ref, router_in, local.at[7]),
    ]
    for h in range(kv_heads):
        for g in range(pack):
            early.append(
                pltpu.make_async_copy(
                    q_ref.at[:, pl.ds((h * pack + g) * HD, HD)],
                    stacked.at[h, pl.ds(g * rows, rows), :],
                    q_local.at[h, g],
                )
            )
    for copy in own + early + late:
        copy.start()
    pl.semaphore_wait(barrier, steps + experts)
    for p in range(parts):
        kv_spread(p, orders[p][0], 0).start()
    if not given:
        for k in range(experts - 1, 0, -1):
            lend(k).start()
    for p in range(parts):
        kv_forward(p, 0).start()
    for t in range(1, steps):
        for p in range(parts):
            kv_spread(p, orders[p][t], 0).start()
    for copy in early:
        copy.wait()

    ids = lax.broadcasted_iota(jnp.int32, (16, rows), 0)
    routed = rt_in[0:1, :] == ids
    for j in range(1, rt_in.shape[0]):
        routed = routed | (rt_in[j : j + 1, :] == ids)
    earlier = lax.broadcasted_iota(jnp.int32, (rows, rows), 0) <= lax.broadcasted_iota(jnp.int32, (rows, rows), 1)
    counted = jnp.dot(
        jnp.where(routed, 1.0, 0.0).astype(low), jnp.where(earlier, 1.0, 0.0).astype(low), preferred_element_type=wide
    )
    index = jnp.where(routed, counted.astype(jnp.int32) - 1, -1)
    capacity = place.shape[1]
    slots = lax.broadcasted_iota(jnp.int32, (capacity, rows), 0)
    for e in range(experts):
        place[e] = jnp.where(index[e : e + 1, :] == slots, 1.0, 0.0).astype(low)
    mine_ref[...] = place[group]

    top[...] = jnp.full_like(top, -1e30)
    total_w[...] = jnp.zeros_like(total_w)
    acc[...] = jnp.zeros_like(acc)
    here = seg_in[:, pl.ds(pl.multiple_of(me * rows, 128), rows)].astype(wide)
    here = jnp.transpose(jnp.broadcast_to(here, (128, rows)))[:, :1]
    row_id = lax.broadcasted_iota(jnp.int32, (rows, rows), 0)
    col_id = lax.broadcasted_iota(jnp.int32, (rows, rows), 1)
    scale = 1.0 / math.sqrt(HD)

    def attend(h, r, c):
        block = across(chip, parts_of(r)) * 2 + (core if c == 0 else 1 - core)

        @pl.when(block <= me)
        def _():
            there = seg_in[:, pl.ds(pl.multiple_of(block * rows, 128), rows)].astype(wide)
            seen = (here == there) & (col_id + block * rows <= row_id + me * rows)
            seen = jnp.concatenate([seen.astype(jnp.int32)] * pack, axis=0) > 0
            keys = kv_in[0, r, c, :, h * HD : (h + 1) * HD]
            values = kv_in[1, r, c, :, h * HD : (h + 1) * HD]
            score = lax.dot_general(
                stacked[h], keys, (((1,), (1,)), ((), ())), preferred_element_type=wide
            ) * scale
            score = jnp.where(seen, score, -1e30)
            before = top[h]
            after = jnp.maximum(before, jnp.max(score, axis=-1, keepdims=True))
            shrink = jnp.exp(before - after)
            weight = jnp.where(seen, jnp.exp(score - after[:, :1]), 0.0)
            top[h] = after
            total_w[h] = total_w[h] * shrink + jnp.sum(weight, axis=-1, keepdims=True)
            acc[h] = acc[h] * shrink + jnp.dot(weight.astype(low), values, preferred_element_type=wide)

    for copy in own[:2]:
        copy.wait()
    for h in range(kv_heads):
        attend(h, 0, 0)
    for p in range(parts):
        kv_forward(p, 0).wait_recv()
    for h in range(kv_heads):
        attend(h, 0, 1)

    def take(spread, onward, got, p, r):
        if r not in got[p]:
            spread(p, orders[p][0], r ^ orders[p][0]).wait_recv()
            onward(p, r).start()
            got[p].add(r)

    def relay(spread, onward, got, t, skip):
        for p in range(parts):
            for r in span(orders[p][:t]):
                take(spread, onward, got, p, r)
        for k in range(skip, 1 << t):
            for p in range(parts):
                spread(p, orders[p][t], span(orders[p][:t])[k]).start()

    got = [{0} for _ in range(parts)]
    for t in range(1, steps):
        relay(kv_spread, kv_forward, got, t, 1)
    rest = sorted(range(1, chips), key=lambda r: (len(parts_of(r)), r))
    w_got = set()

    def w_take(p, r):
        if given or (p, r) in w_got:
            return
        w_got.add((p, r))
        order = orders[p % parts]
        if r > 0:
            w_spread(p, order[0], r ^ order[0]).wait_recv()
            order = order[max(order.index(b) for b in parts_of(r)) + 1 :]
        elif p > 0:
            lend(experts - p).wait_recv()
        else:
            own[2].wait()
        for bit in order:
            w_spread(p, bit, r).start()
        w_forward(p, r).start()

    w_take(0, 0)
    for r in rest:
        for p in range(parts):
            take(kv_spread, kv_forward, got, p, r)
    for p in range(1, experts):
        w_take(p, 0)
    for r in rest:
        for p in range(parts):
            kv_forward(p, r).wait_recv()
        for c in range(2):
            attend(0, r, c)

    def part(h):
        return pl.ds(h * pack * HD, pack * HD)

    def share_heads(h, bit, q):
        return remote(
            att_in.at[q, :, part(h)], att_in.at[q ^ bit, :, part(h)],
            a_send.at[h, q ^ bit], a_recv.at[h, q ^ bit], flip(group, bit), "expert",
        )

    for h in range(kv_heads):
        if h > 0:
            for r in rest:
                for c in range(2):
                    attend(h, r, c)
        done = (acc[h] / total_w[h]).astype(low)
        for g in range(pack):
            at = (h * pack + g) * HD
            att_in[0, :, at : at + HD] = done[g * rows : (g + 1) * rows, :]
        for bit in zorder:
            share_heads(h, bit, 0).start()
    if given:
        own[2].wait()
    for t in range(1, steps):
        for p in range(experts):
            for r in span(orders[p % parts][:t]):
                w_take(p, r)
    for copy in late:
        copy.wait()
    stream_ref[...] = res_in[...].astype(wide)
    z_got = {0}
    for t in range(1, zsteps):
        for q in span(zorder[:t]):
            if q not in z_got:
                z_got.add(q)
                for h in range(kv_heads):
                    share_heads(h, zorder[0], q ^ zorder[0]).wait_recv()
                    for bit in zorder[t:]:
                        share_heads(h, bit, q).start()
    if not given:
        for r in rest:
            for p in range(experts):
                w_take(p, r)
        for r in range(chips):
            for p in range(experts):
                w_forward(p, r).wait_recv()

    def project(q):
        g = across(group, parts_of(q))
        from_rows = pl.ds(pl.multiple_of(g * depth, depth), depth)
        if given:
            stream_ref[...] += jnp.dot(att_in[q], w_in[0, from_rows, :], preferred_element_type=wide)
        else:
            for r in range(chips):
                c = across(chip, parts_of(r)) * 2 * piece
                at = pl.ds(pl.multiple_of(c, 2 * piece), 2 * piece)
                stream_ref[:, at] += jnp.dot(att_in[q], w_in[r, from_rows, :], preferred_element_type=wide)

    for q in [0] + zorder + sorted(set(range(1, experts)) - set(zorder)):
        if q not in z_got:
            z_got.add(q)
            for h in range(kv_heads):
                share_heads(h, zorder[0], q ^ zorder[0]).wait_recv()
        project(q)

    def share_squares(k):
        return remote(squares.at[0], squares.at[k], s_send.at[k], s_recv.at[k], target(k), "expert")

    leaving = [pltpu.make_async_copy(stream_ref, stream_any, out_local.at[experts])]
    leaving[0].start()
    stream = stream_ref[...]
    total = jnp.sum(stream * stream, axis=-1, keepdims=True)
    squares[0] = jnp.transpose(jnp.broadcast_to(total, (rows, 128)))[:8, :]
    for k in range(1, experts):
        share_squares(k).start()
    for k in range(1, experts):
        share_squares(k).wait_recv()
    total = squares[0]
    for k in range(1, experts):
        total = total + squares[k]
    total = jnp.transpose(jnp.broadcast_to(total[:1, :], (128, rows)))[:, :1]
    inverse = lax.rsqrt(total * (1.0 / (cols * experts)) + 1e-05)
    normed = (stream_ref[...] * inverse * gain_in[...]).astype(low)
    for k in range(experts):
        chosen_ref[k] = jnp.dot(place[target(k)], normed, preferred_element_type=wide).astype(low)
        leaving.append(pltpu.make_async_copy(chosen_ref.at[k], chosen_any.at[k], out_local.at[k]))
        leaving[-1].start()
    logit_ref[...] = lax.dot_general(
        router_in[...], normed, (((1,), (1,)), ((), ())), preferred_element_type=wide
    )
    for p in range(parts):
        for r in range(chips):
            kv_forward(p, r).wait_send()
            if r > 0:
                kv_spread(p, orders[p][0], r ^ orders[p][0]).wait_send()
    for p in range(0 if given else experts):
        for r in range(chips):
            w_forward(p, r).wait_send()
            if r > 0:
                w_spread(p, bits[0], r ^ bits[0]).wait_send()
    for h in range(kv_heads):
        for q in range(1, experts):
            share_heads(h, zorder[0], q ^ zorder[0]).wait_send()
    for k in range(1, experts):
        if not given:
            lend(k).wait_send()
        share_squares(k).wait_send()
    for copy in leaving:
        copy.wait()


def front(queries, keys, values, segments, routes_t, w_out, residual, gain, router, capacity):
    chips, experts = lax.axis_size("blk") // 2, lax.axis_size("expert")
    rows, cols = residual.shape
    depth = queries.shape[1]
    kv_heads = keys.shape[1] // HD
    pack = queries.shape[1] // keys.shape[1]
    low, wide = jnp.bfloat16, jnp.float32
    vmem, dma, shape = pl.BlockSpec(memory_space=pltpu.VMEM), pltpu.SemaphoreType.DMA, jax.ShapeDtypeStruct
    given = cols % (256 * chips) != 0
    if given:
        w_out = lax.all_to_all(w_out, "expert", 1, 0, tiled=True)
    w_shape = (1, depth * experts, cols) if given else (chips, depth * experts, cols // chips)
    return pl.pallas_call(
        functools.partial(front_kernel, chips, experts, given),
        out_shape=(
            shape((rows, cols), wide),
            shape((experts, capacity, cols), low),
            shape((router.shape[0], rows), wide),
            shape((capacity, rows), low),
        ),
        in_specs=[pl.BlockSpec(memory_space=pl.ANY)] * 9,
        out_specs=(pl.BlockSpec(memory_space=pl.ANY),) * 2 + (vmem,) * 2,
        scratch_shapes=[
            pltpu.VMEM((rows, cols), wide),
            pltpu.VMEM((experts, capacity, cols), low),
            pltpu.VMEM((2, chips, 2) + keys.shape, low),
            pltpu.VMEM(w_shape, low),
            pltpu.VMEM((experts, rows, depth), low),
            pltpu.VMEM((kv_heads, pack * rows, HD), low),
            pltpu.VMEM((kv_heads, pack * rows, HD), wide),
            pltpu.VMEM((kv_heads, pack * rows, HD), wide),
            pltpu.VMEM((kv_heads, pack * rows, HD), wide),
            pltpu.VMEM((experts, capacity, rows), low),
            pltpu.VMEM((experts, 8, rows), wide),
            pltpu.VMEM((rows, cols), low),
            pltpu.VMEM(segments.shape, jnp.int32),
            pltpu.VMEM(routes_t.shape, jnp.int32),
            pltpu.VMEM((1, cols), wide),
            pltpu.VMEM(router.shape, low),
            dma((8,)),
            dma((kv_heads, pack)),
            dma((experts + 1,)),
        ]
        + [dma((2, chips))] * 4
        + [dma((experts,))] * 2
        + [dma((experts, chips))] * 4
        + [dma((kv_heads, experts))] * 2
        + [dma((experts,))] * 2,
        compiler_params=pltpu.CompilerParams(
            collective_id=0, has_side_effects=True, vmem_limit_bytes=61 * 1024 * 1024
        ),
    )(queries, keys, values, segments, routes_t, w_out, residual, gain, router)


def expert_kernel(
    chips, experts, x_ref, wg_ref, wu_ref, wd_ref, stream_any, place_any, logit_any, rt_any, o_ref,
    rows_in, weights, hidden, leaving, sib_in, keep, part_in, own_out, strips, strip_in, scatter, share,
    stream_ref, place_ref, logit_ref, rt_ref,
    w_sem, d_sem, ag_send, ag_recv, fw_send, fw_recv, sib_send, sib_recv,
    rs_send, rs_recv, z_send, z_recv, x_send, x_recv, l_send, l_recv, small,
):
    me, group = lax.axis_index("blk"), lax.axis_index("expert")
    chip, core = me // 2, me % 2
    sibling = chip * 2 + 1 - core
    rows, width = x_ref.shape[1], x_ref.shape[2] * experts
    units = wg_ref.shape[1]
    tile = weights.shape[2]
    tiles = units // tile
    slots = 2 * tiles
    steps, zsteps = log2(chips), log2(experts)
    bits = [1 << b for b in range(steps)]
    zbits = [1 << b for b in range(zsteps)]
    parts = 2
    groups = 4
    orders = [bits[p % steps :] + bits[: p % steps] for p in range(parts)]
    tw = leaving.shape[2]
    pw = tw // parts
    total = width // tw
    per_tile = tw // tile
    piece = tw // experts
    subs = width // tile
    slab = width // experts
    own_rows = o_ref.shape[0]
    low = jnp.bfloat16

    def peer(bit):
        return flip(chip, bit) * 2 + core

    barrier = pltpu.get_barrier_semaphore()
    pl.semaphore_signal(barrier, inc=1, device_id={"blk": sibling}, device_id_type=MESH)
    for bit in bits:
        pl.semaphore_signal(barrier, inc=1, device_id={"blk": peer(bit)}, device_id_type=MESH)
    for e in range(1, experts):
        pl.semaphore_signal(barrier, inc=1, device_id={"expert": (group + e) % experts}, device_id_type=MESH)

    def load(f, side):
        src = (wg_ref, wu_ref)[side]
        return pltpu.make_async_copy(
            src.at[:, pl.ds(pl.multiple_of(f * tile, 128), tile)], weights.at[2 * f + side], w_sem.at[2 * f + side]
        )

    def load_down(m, i):
        column = (m % per_tile) * (tile // piece) + i
        column = column * slab + (m // per_tile) * piece
        slot = m % slots
        return pltpu.make_async_copy(
            wd_ref.at[:, pl.ds(pl.multiple_of(column, 128), piece)],
            weights.at[slot, pl.ds(0, units), pl.ds(i * piece, piece)],
            d_sem.at[slot, i],
        )

    cuts = [0]
    for p in range(groups):
        extra = p in (2, 3, 1)[: rows // 16 % groups]
        cuts.append(cuts[-1] + 16 * (rows // 16 // groups + extra))
    early, late = [0, 1], [2, 3]
    by_distance = sorted(range(1, chips), key=lambda r: (len(parts_of(r)), r))
    near = [r for r in by_distance if len(parts_of(r)) == 1]
    far = [r for r in by_distance if r not in near]
    units_of_work = [
        [(0, early)],
        [(r, early) for r in near],
        [(r, early) for r in far] + [(0, late)],
        [(r, late) for r in near],
        [(r, late) for r in far],
    ]
    units_of_work = [work for work in units_of_work if work]
    place_of, begins, count = {}, [], 0
    for work in units_of_work:
        begins.append(count)
        for r, which in work:
            for c in range(2):
                for p in which:
                    place_of[r, c, p] = count
                    count += cuts[p + 1] - cuts[p]
    begins.append(count)

    def lot(r, c, p):
        return rows_in.at[pl.ds(place_of[r, c, p], cuts[p + 1] - cuts[p]), :]

    def slab_of(g):
        return pl.ds(pl.multiple_of(g * slab, 128), slab)

    def dispatch(k, p, g):
        take_rows = pl.ds(cuts[p], cuts[p + 1] - cuts[p])
        put_rows = pl.ds(place_of[0, 0, p], cuts[p + 1] - cuts[p])
        source, goal = x_ref.at[k, take_rows, :], rows_in.at[put_rows, slab_of(g)]
        if k == 0:
            return pltpu.make_async_copy(source, goal, x_send.at[0, p])
        return remote(source, goal, x_send.at[k, p], x_recv.at[k, p], (group + k) % experts, "expert")

    def share_logits(k):
        if k == 0:
            return pltpu.make_async_copy(logit_any, logit_ref.at[0], l_send.at[0])
        return remote(logit_any, logit_ref.at[k], l_send.at[k], l_recv.at[k], (group + k) % experts, "expert")

    def order(p):
        return bits[p % steps :] + bits[: p % steps]

    def spread(p, bit, r):
        return remote(
            lot(r, 0, p), lot(r ^ bit, 0, p), ag_send.at[p, r ^ bit], ag_recv.at[p, r ^ bit], peer(bit)
        )

    def forward(p, r):
        return remote(lot(r, 0, p), lot(r, 1, p), fw_send.at[p, r], fw_recv.at[p, r], sibling)

    got = set()

    def take(p, r):
        if (p, r) in got:
            return
        got.add((p, r))
        if r == 0:
            dispatch(0, p, group).wait()
            for e in range(1, experts):
                dispatch(e, p, (group + experts - e) % experts).wait_recv()
            onward = order(p)
        else:
            bit = order(p)[0]
            spread(p, bit, r ^ bit).wait_recv()
            onward = order(p)[max(order(p).index(b) for b in parts_of(r)) + 1 :]
        for bit in onward:
            spread(p, bit, r).start()
        forward(p, r).start()

    def begin_dispatch(p):
        for e in range(experts - 1, -1, -1):
            dispatch(e, p, group).start()

    smalls = [
        pltpu.make_async_copy(stream_any, stream_ref, small.at[0]),
        pltpu.make_async_copy(place_any, place_ref, small.at[1]),
        pltpu.make_async_copy(rt_any, rt_ref, small.at[2]),
    ]
    pl.semaphore_wait(barrier, steps + experts)
    begin_dispatch(0)
    for e in range(experts):
        share_logits(e).start()
    for copy in smalls:
        copy.start()

    @pl.loop(0, tiles)
    def _(f):
        load(f, 0).start()
        load(f, 1).start()

    take(0, 0)
    begin_dispatch(1)

    for copy in smalls:
        copy.wait()
    share_logits(0).wait()
    for e in range(1, experts):
        share_logits(e).wait_recv()
    logit = logit_ref[0]
    for e in range(1, experts):
        logit = logit + logit_ref[e]
    tokens_here = rt_ref.shape[1]
    ids = lax.broadcasted_iota(jnp.int32, logit.shape, 0)
    routed = rt_ref[0:1, :] == ids
    for j in range(1, rt_ref.shape[0]):
        routed = routed | (rt_ref[j : j + 1, :] == ids)
    score = jnp.where(routed, 1.0 / (1.0 + jnp.exp(-logit)), 0.0)
    fraction = jnp.sum(jnp.where(ids == group, score, 0.0), axis=0, keepdims=True) / jnp.sum(
        score, axis=0, keepdims=True
    )
    share[...] = jnp.transpose(jnp.broadcast_to(fraction, (128, tokens_here)))
    take(1, 0)
    begin_dispatch(2)
    begin_dispatch(3)

    def up_tiles(u, begin, end):
        size = begins[u + 1] - begins[u]

        def body(f):
            if u == 0:
                load(f, 0).wait()
                load(f, 1).wait()
            tokens = rows_in[begins[u] : begins[u + 1], :]
            gate = jnp.dot(tokens, weights[2 * f], preferred_element_type=jnp.float32)
            up = jnp.dot(tokens, weights[2 * f + 1], preferred_element_type=jnp.float32)
            act = (gate / (1.0 + jnp.exp(-gate)) * up).astype(low)
            at = pl.ds(pl.multiple_of(f * tile, 128), tile)
            for r, which in units_of_work[u]:
                for c in range(2):
                    start = place_of[r, c, which[0]] - begins[u]
                    length = cuts[which[-1] + 1] - cuts[which[0]]
                    to = r * rows + cuts[which[0]]
                    hidden[c, to : to + length, at] = act[start : start + length]
            if u == len(units_of_work) - 1:
                for side in range(2):
                    m = 2 * f + side

                    @pl.when(m < subs)
                    def _():
                        for i in range(tile // piece):
                            load_down(m, i).start()

        pl.loop(begin, end, unroll=1)(body)

    middle = tiles // 2
    for u, work in enumerate(units_of_work):
        for r, which in work:
            for p in which:
                take(p, r)
        for r, which in work:
            for p in which:
                forward(p, r).wait_recv()
        up_tiles(u, 0, middle)
        if u == 1:
            take(2, 0)
            take(3, 0)
        if u == 2:
            for r in near:
                take(2, r)
        up_tiles(u, middle, tiles)

    moves = []
    for t in range(steps):
        step = []
        for p in range(parts):
            for i, left in enumerate(span(orders[p][t + 1 :])):
                step.append((p, left | orders[p][t], left, i))
        moves.append(step)
    base = [sum(len(s) for s in moves[:t]) for t in range(steps)]
    zmoves = [[(left | zbits[u], left) for left in span(zbits[u + 1 :])] for u in range(zsteps)]
    zbase = [sum(len(s) for s in zmoves[:u]) for u in range(zsteps)]

    def exchange(n):
        return remote(leaving.at[n % 2], sib_in.at[n], sib_send.at[n], sib_recv.at[n], sibling)

    def block(r):
        return pl.ds(r * rows, rows)

    def deliver(n, t, k):
        p, sent, _, _ = moves[t][k]
        at = base[t] + k
        return remote(
            sib_in.at[n, block(sent), pl.ds(p * pw, pw)], part_in.at[n, at],
            rs_send.at[n, at], rs_recv.at[n, at], peer(orders[p][t]),
        )

    def hand(n, u, k):
        sent, _ = zmoves[u][k]
        at = zbase[u] + k
        return remote(
            strips.at[n, sent - 1], strip_in.at[n, at], z_send.at[n, at], z_recv.at[n, at],
            flip(group, zbits[u]), "expert",
        )

    def down(c, n, i):
        slot = (n * per_tile + i) % slots
        return jnp.dot(hidden[c], weights[slot, :units, :], preferred_element_type=jnp.float32)

    def leave(n):
        for i in range(per_tile):
            for j in range(tile // piece):
                load_down(n * per_tile + i, j).wait()

        @pl.when(n >= 2)
        def _():
            exchange(n - 2).wait_send()

        for i in range(per_tile):
            leaving[n % 2, :, i * tile : (i + 1) * tile] = down(1, n, i).astype(low)
        exchange(n).start()

    def stay(n):
        for i in range(per_tile):
            keep[:, i * tile : (i + 1) * tile] = down(0, n, i)
        for i in range(per_tile):
            m = n * per_tile + i + slots

            @pl.when(m < subs)
            def _():
                for j in range(tile // piece):
                    load_down(m, j).start()

    def join(n):
        exchange(n).wait_recv()
        sib_in[n] = (keep[...] + sib_in[n].astype(jnp.float32)).astype(low)
        for k in range(len(moves[0])):
            deliver(n, 0, k).start()

    def gather_step(n, t):
        for k, (p, _, left, _) in enumerate(moves[t]):
            deliver(n, t, k).wait_recv()
            at = (block(left), pl.ds(p * pw, pw))
            mine = sib_in[n, at[0], at[1]].astype(jnp.float32)
            sib_in[n, at[0], at[1]] = (mine + part_in[n, base[t] + k].astype(jnp.float32)).astype(low)
        if t + 1 < steps:
            for k in range(len(moves[t + 1])):
                deliver(n, t + 1, k).start()
        else:
            mix = share[:, :1] * lax.dot_general(
                place_ref[...], sib_in[n, :rows, :], (((0,), (0,)), ((), ())), preferred_element_type=jnp.float32
            )
            column = pl.ds(pl.multiple_of(n * piece, 128), piece)
            scatter[...] = mix
            mine = pl.ds(pl.multiple_of(group * piece, 128), piece)
            scatter[:, mine] += stream_ref[:, column]
            for q in range(experts):
                start = across(group, parts_of(q)) * own_rows
                strip = scatter[pl.ds(pl.multiple_of(start, own_rows), own_rows), :]
                if q == 0:
                    own_out[n] = strip
                else:
                    strips[n, q - 1] = strip.astype(low)
            for k in range(len(zmoves[0])):
                hand(n, 0, k).start()

    def combine_step(n, u):
        for k, (_, left) in enumerate(zmoves[u]):
            hand(n, u, k).wait_recv()
            theirs = strip_in[n, zbase[u] + k].astype(jnp.float32)
            if left == 0:
                own_out[n] += theirs
            else:
                strips[n, left - 1] = (strips[n, left - 1].astype(jnp.float32) + theirs).astype(low)
        if u + 1 < zsteps:
            for k in range(len(zmoves[u + 1])):
                hand(n, u + 1, k).start()
        else:
            column = n * piece
            for g in range(experts):
                at = pl.ds(pl.multiple_of(g * slab + column, 128), piece)
                o_ref[:, at] = own_out[n, :, g * piece : (g + 1) * piece].astype(o_ref.dtype)

    lag = 1 + steps + zsteps

    @pl.loop(0, total + lag)
    def _(n):
        @pl.when(n < total)
        def _():
            leave(n)

        @pl.when((n >= 1) & (n - 1 < total))
        def _():
            join(n - 1)

        @pl.when(n < total)
        def _():
            stay(n)

        for t in range(steps):
            @pl.when((n >= 2 + t) & (n - 2 - t < total))
            def _():
                gather_step(n - 2 - t, t)

        for u in range(zsteps):
            @pl.when((n >= 2 + steps + u) & (n - 2 - steps - u < total))
            def _():
                combine_step(n - 2 - steps - u, u)

    for n in range(max(0, total - 2), total):
        exchange(n).wait_send()
    for e in range(1, experts):
        share_logits(e).wait_send()
        for p in range(groups):
            dispatch(e, p, group).wait_send()
    for p in range(groups):
        for r in range(chips):
            forward(p, r).wait_send()
            if r > 0:
                spread(p, order(p)[0], r ^ order(p)[0]).wait_send()

    @pl.loop(0, total)
    def _(n):
        for t in range(steps):
            for k in range(len(moves[t])):
                deliver(n, t, k).wait_send()
        for u in range(zsteps):
            for k in range(len(zmoves[u])):
                hand(n, u, k).wait_send()


def expert_layer(x, gate_w, up_w, down_w, stream, place, logits, routes_t):
    chips, experts = lax.axis_size("blk") // 2, lax.axis_size("expert")
    rows, width = x.shape[1], x.shape[2] * experts
    units = gate_w.shape[1]
    tile = 256 if units % 256 == 0 else 128
    tokens = stream.shape[0]
    tw = 128 * experts
    total = width // tw
    dma = pltpu.SemaphoreType.DMA
    low, wide = jnp.bfloat16, jnp.float32
    vmem = pl.BlockSpec(memory_space=pltpu.VMEM)
    anywhere = pl.BlockSpec(memory_space=pl.ANY)
    own_rows = tokens // experts
    slots = 2 * (units // tile)
    moved = 2 * (chips - 1)
    return pl.pallas_call(
        functools.partial(expert_kernel, chips, experts),
        out_shape=jax.ShapeDtypeStruct((own_rows, width), low),
        in_specs=[anywhere] * 8,
        out_specs=vmem,
        scratch_shapes=[
            pltpu.VMEM((2 * chips * rows, width), low),
            pltpu.VMEM((slots, width, tile), low),
            pltpu.VMEM((2, chips * rows, units), low),
            pltpu.VMEM((2, chips * rows, tw), low),
            pltpu.VMEM((total, chips * rows, tw), low),
            pltpu.VMEM((chips * rows, tw), wide),
            pltpu.VMEM((total, moved, rows, tw // 2), low),
            pltpu.VMEM((total, own_rows, tw), wide),
            pltpu.VMEM((total, experts - 1, own_rows, tw), low),
            pltpu.VMEM((total, experts - 1, own_rows, tw), low),
            pltpu.VMEM((tokens, tw), wide),
            pltpu.VMEM((tokens, 128), wide),
            pltpu.VMEM(stream.shape, wide),
            pltpu.VMEM(place.shape, low),
            pltpu.VMEM((experts,) + logits.shape, wide),
            pltpu.VMEM(routes_t.shape, jnp.int32),
            dma((slots,)),
            dma((slots, tile // 128)),
            dma((4, chips)),
            dma((4, chips)),
            dma((4, chips)),
            dma((4, chips)),
            dma((total,)),
            dma((total,)),
            dma((total, moved)),
            dma((total, moved)),
            dma((total, experts - 1)),
            dma((total, experts - 1)),
            dma((experts, 4)),
            dma((experts, 4)),
            dma((experts,)),
            dma((experts,)),
            dma((3,)),
        ],
        compiler_params=pltpu.CompilerParams(
            collective_id=1, has_side_effects=True, vmem_limit_bytes=61 * 1024 * 1024
        ),
    )(x, gate_w, up_w, down_w, stream, place, logits, routes_t)


def on_device(
    residual,
    queries,
    key_cache,
    value_cache,
    segments,
    routes,
    w_out,
    norm_gain,
    w_router,
    w_gate,
    w_up,
    w_down,
):
    experts = w_router.shape[1]
    cols = residual.shape[1]
    first_col = lax.axis_index("expert") * cols
    capacity = queries.shape[0] * TOP * 9 // (8 * experts)
    capacity = -(-capacity // 16) * 16
    router = lax.dynamic_slice_in_dim(w_router, first_col, cols, 0).T
    router = jnp.pad(router, ((0, -experts % 16), (0, 0)))
    routes_t = routes.T
    stream, chosen, logits, place = front(
        queries, key_cache, value_cache, segments[None, :], routes_t, w_out, residual, norm_gain[None, :], router, capacity
    )
    return expert_layer(chosen, w_gate[0], w_up[0], w_down[0], stream, place, logits, routes_t)


def solution(mesh):
    return jax.shard_map(
        on_device,
        mesh=mesh,
        in_specs=(
            P("blk", "expert"),
            P("blk", "expert"),
            P("blk", "expert"),
            P("blk", "expert"),
            P(),
            P("blk", None),
            P("expert", None),
            P(),
            P(),
            P("expert", None, "blk"),
            P("expert", None, "blk"),
            P("expert", "blk", None),
        ),
        out_specs=P(("blk", "expert"), None),
        check_vma=False,
    )
```

```python
import functools
import math

import jax
import jax.numpy as jnp
from jax import lax
from jax.experimental import pallas as pl
from jax.experimental.pallas import tpu as pltpu
from jax.sharding import PartitionSpec as P

HD = 128
TOP = 2

MESH = pl.DeviceIdType.MESH


def remote(src, dst, send_sem, recv_sem, target, axis="blk"):
    return pltpu.make_async_remote_copy(
        src_ref=src,
        dst_ref=dst,
        send_sem=send_sem,
        recv_sem=recv_sem,
        device_id={axis: target},
        device_id_type=MESH,
    )


def flip(index, bit):
    return index + bit * (1 - 2 * ((index // bit) % 2))


def across(index, bits):
    for bit in bits:
        index = flip(index, bit)
    return index


def log2(n):
    return n.bit_length() - 1


def parts_of(mask):
    return [1 << b for b in range(mask.bit_length()) if mask >> b & 1]


def span(order):
    found = [0]
    for bit in order:
        found += [f | bit for f in found]
    return found


def front_kernel(
    chips, experts, given, q_ref, k_ref, v_ref, seg_ref, rt_ref, w_ref, res_ref, gain_ref, router_ref,
    stream_any, chosen_any, logit_ref, mine_ref,
    stream_ref, chosen_ref, kv_in, w_in, att_in, stacked, top, total_w, acc, place, squares, res_in, seg_in, rt_in, gain_in, router_in,
    local, q_local, out_local,
    kv_send, kv_recv, kf_send, kf_recv, wz_send, wz_recv, w_send, w_recv, wf_send, wf_recv,
    a_send, a_recv, s_send, s_recv,
):
    me, group = lax.axis_index("blk"), lax.axis_index("expert")
    chip, core = me // 2, me % 2
    sibling = chip * 2 + 1 - core
    steps, zsteps = log2(chips), log2(experts)
    bits = [1 << b for b in range(steps)]
    zorder = [1 << b for b in range(zsteps)][::-1]
    parts = 2
    orders = [bits[p % steps :] + bits[: p % steps] for p in range(parts)]
    rows, cols = res_ref.shape
    kv_heads = k_ref.shape[1] // HD
    pack = q_ref.shape[1] // k_ref.shape[1]
    depth = q_ref.shape[1]
    wide, low = jnp.float32, jnp.bfloat16
    kv = (k_ref, v_ref)

    def peer(bit):
        return flip(chip, bit) * 2 + core

    def target(k):
        return (group + k) % experts

    barrier = pltpu.get_barrier_semaphore()
    pl.semaphore_signal(barrier, inc=1, device_id={"blk": sibling}, device_id_type=MESH)
    for bit in bits:
        pl.semaphore_signal(barrier, inc=1, device_id={"blk": peer(bit)}, device_id_type=MESH)
    for k in range(1, experts):
        pl.semaphore_signal(barrier, inc=1, device_id={"expert": target(k)}, device_id_type=MESH)

    def kv_from(p, r):
        return kv[p] if r == 0 else kv_in.at[p, r, 0]

    def kv_spread(p, bit, r):
        return remote(
            kv_from(p, r), kv_in.at[p, r ^ bit, 0], kv_send.at[p, r ^ bit], kv_recv.at[p, r ^ bit], peer(bit)
        )

    def kv_forward(p, r):
        return remote(kv_from(p, r), kv_in.at[p, r, 1], kf_send.at[p, r], kf_recv.at[p, r], sibling)

    piece = cols // (2 * chips)
    lanes = pl.ds(pl.multiple_of(core * piece, 128), piece)
    w_rows = pl.ds(pl.multiple_of(group * depth, depth), depth)

    def w_piece(k):
        return w_ref.at[:, pl.ds(pl.multiple_of(target(k) * cols + me * piece, 128), piece)]

    def lend(k):
        return remote(
            w_piece(k), w_in.at[0, w_rows, lanes], wz_send.at[k], wz_recv.at[k], target(k), "expert"
        )

    def w_part(p, r):
        return w_in.at[r, pl.ds(pl.multiple_of(target(p) * depth, depth), depth), lanes]

    def w_spread(p, bit, r):
        return remote(
            w_part(p, r), w_part(p, r ^ bit), w_send.at[p, r ^ bit], w_recv.at[p, r ^ bit], peer(bit)
        )

    def w_forward(p, r):
        return remote(w_part(p, r), w_part(p, r), wf_send.at[p, r], wf_recv.at[p, r], sibling)

    own = [pltpu.make_async_copy(kv[p], kv_in.at[p, 0, 0], local.at[p]) for p in range(2)]
    if given:
        own.append(pltpu.make_async_copy(w_ref, w_in.at[0], local.at[2]))
    else:
        own.append(pltpu.make_async_copy(w_piece(0), w_in.at[0, w_rows, lanes], local.at[2]))
    early = [
        pltpu.make_async_copy(seg_ref, seg_in, local.at[3]),
        pltpu.make_async_copy(rt_ref, rt_in, local.at[4]),
    ]
    late = [
        pltpu.make_async_copy(res_ref, res_in, local.at[5]),
        pltpu.make_async_copy(gain_ref.at[:, pl.ds(pl.multiple_of(group * cols, 128), cols)], gain_in, local.at[6]),
        pltpu.make_async_copy(router_ref, router_in, local.at[7]),
    ]
    for h in range(kv_heads):
        for g in range(pack):
            early.append(
                pltpu.make_async_copy(
                    q_ref.at[:, pl.ds((h * pack + g) * HD, HD)],
                    stacked.at[h, pl.ds(g * rows, rows), :],
                    q_local.at[h, g],
                )
            )
    for copy in own + early + late:
        copy.start()
    pl.semaphore_wait(barrier, steps + experts)
    for p in range(parts):
        kv_spread(p, orders[p][0], 0).start()
    if not given:
        for k in range(experts - 1, 0, -1):
            lend(k).start()
    for p in range(parts):
        kv_forward(p, 0).start()
    for t in range(1, steps):
        for p in range(parts):
            kv_spread(p, orders[p][t], 0).start()
    for copy in early:
        copy.wait()

    ids = lax.broadcasted_iota(jnp.int32, (16, rows), 0)
    routed = rt_in[0:1, :] == ids
    for j in range(1, rt_in.shape[0]):
        routed = routed | (rt_in[j : j + 1, :] == ids)
    earlier = lax.broadcasted_iota(jnp.int32, (rows, rows), 0) <= lax.broadcasted_iota(jnp.int32, (rows, rows), 1)
    counted = jnp.dot(
        jnp.where(routed, 1.0, 0.0).astype(low), jnp.where(earlier, 1.0, 0.0).astype(low), preferred_element_type=wide
    )
    index = jnp.where(routed, counted.astype(jnp.int32) - 1, -1)
    capacity = place.shape[1]
    slots = lax.broadcasted_iota(jnp.int32, (capacity, rows), 0)
    for e in range(experts):
        place[e] = jnp.where(index[e : e + 1, :] == slots, 1.0, 0.0).astype(low)
    mine_ref[...] = place[group]

    top[...] = jnp.full_like(top, -1e30)
    total_w[...] = jnp.zeros_like(total_w)
    acc[...] = jnp.zeros_like(acc)
    here = seg_in[:, pl.ds(pl.multiple_of(me * rows, 128), rows)].astype(wide)
    here = jnp.transpose(jnp.broadcast_to(here, (128, rows)))[:, :1]
    row_id = lax.broadcasted_iota(jnp.int32, (rows, rows), 0)
    col_id = lax.broadcasted_iota(jnp.int32, (rows, rows), 1)
    scale = 1.0 / math.sqrt(HD)

    def attend(h, r, c):
        block = across(chip, parts_of(r)) * 2 + (core if c == 0 else 1 - core)

        @pl.when(block <= me)
        def _():
            there = seg_in[:, pl.ds(pl.multiple_of(block * rows, 128), rows)].astype(wide)
            seen = (here == there) & (col_id + block * rows <= row_id + me * rows)
            seen = jnp.concatenate([seen.astype(jnp.int32)] * pack, axis=0) > 0
            keys = kv_in[0, r, c, :, h * HD : (h + 1) * HD]
            values = kv_in[1, r, c, :, h * HD : (h + 1) * HD]
            score = lax.dot_general(
                stacked[h], keys, (((1,), (1,)), ((), ())), preferred_element_type=wide
            ) * scale
            score = jnp.where(seen, score, -1e30)
            before = top[h]
            after = jnp.maximum(before, jnp.max(score, axis=-1, keepdims=True))
            shrink = jnp.exp(before - after)
            weight = jnp.where(seen, jnp.exp(score - after[:, :1]), 0.0)
            top[h] = after
            total_w[h] = total_w[h] * shrink + jnp.sum(weight, axis=-1, keepdims=True)
            acc[h] = acc[h] * shrink + jnp.dot(weight.astype(low), values, preferred_element_type=wide)

    for copy in own[:2]:
        copy.wait()
    for h in range(kv_heads):
        attend(h, 0, 0)
    for p in range(parts):
        kv_forward(p, 0).wait_recv()
    for h in range(kv_heads):
        attend(h, 0, 1)

    def take(spread, onward, got, p, r):
        if r not in got[p]:
            spread(p, orders[p][0], r ^ orders[p][0]).wait_recv()
            onward(p, r).start()
            got[p].add(r)

    def relay(spread, onward, got, t, skip):
        for p in range(parts):
            for r in span(orders[p][:t]):
                take(spread, onward, got, p, r)
        for k in range(skip, 1 << t):
            for p in range(parts):
                spread(p, orders[p][t], span(orders[p][:t])[k]).start()

    got = [{0} for _ in range(parts)]
    for t in range(1, steps):
        relay(kv_spread, kv_forward, got, t, 1)
    rest = sorted(range(1, chips), key=lambda r: (len(parts_of(r)), r))
    w_got = set()

    def w_take(p, r):
        if given or (p, r) in w_got:
            return
        w_got.add((p, r))
        order = orders[p % parts]
        if r > 0:
            w_spread(p, order[0], r ^ order[0]).wait_recv()
            order = order[max(order.index(b) for b in parts_of(r)) + 1 :]
        elif p > 0:
            lend(experts - p).wait_recv()
        else:
            own[2].wait()
        for bit in order:
            w_spread(p, bit, r).start()
        w_forward(p, r).start()

    w_take(0, 0)
    for r in rest:
        for p in range(parts):
            take(kv_spread, kv_forward, got, p, r)
    for p in range(1, experts):
        w_take(p, 0)
    for r in rest:
        for p in range(parts):
            kv_forward(p, r).wait_recv()
        for c in range(2):
            attend(0, r, c)

    def part(h):
        return pl.ds(h * pack * HD, pack * HD)

    def share_heads(h, bit, q):
        return remote(
            att_in.at[q, :, part(h)], att_in.at[q ^ bit, :, part(h)],
            a_send.at[h, q ^ bit], a_recv.at[h, q ^ bit], flip(group, bit), "expert",
        )

    for h in range(kv_heads):
        if h > 0:
            for r in rest:
                for c in range(2):
                    attend(h, r, c)
        done = (acc[h] / total_w[h]).astype(low)
        for g in range(pack):
            at = (h * pack + g) * HD
            att_in[0, :, at : at + HD] = done[g * rows : (g + 1) * rows, :]
        for bit in zorder:
            share_heads(h, bit, 0).start()
    if given:
        own[2].wait()
    for t in range(1, steps):
        for p in range(experts):
            for r in span(orders[p % parts][:t]):
                w_take(p, r)
    for copy in late:
        copy.wait()
    stream_ref[...] = res_in[...].astype(wide)
    z_got = {0}
    for t in range(1, zsteps):
        for q in span(zorder[:t]):
            if q not in z_got:
                z_got.add(q)
                for h in range(kv_heads):
                    share_heads(h, zorder[0], q ^ zorder[0]).wait_recv()
                    for bit in zorder[t:]:
                        share_heads(h, bit, q).start()
    if not given:
        for r in rest:
            for p in range(experts):
                w_take(p, r)
        for r in range(chips):
            for p in range(experts):
                w_forward(p, r).wait_recv()

    def project(q):
        g = across(group, parts_of(q))
        from_rows = pl.ds(pl.multiple_of(g * depth, depth), depth)
        if given:
            stream_ref[...] += jnp.dot(att_in[q], w_in[0, from_rows, :], preferred_element_type=wide)
        else:
            for r in range(chips):
                c = across(chip, parts_of(r)) * 2 * piece
                at = pl.ds(pl.multiple_of(c, 2 * piece), 2 * piece)
                stream_ref[:, at] += jnp.dot(att_in[q], w_in[r, from_rows, :], preferred_element_type=wide)

    for q in [0] + zorder + sorted(set(range(1, experts)) - set(zorder)):
        if q not in z_got:
            z_got.add(q)
            for h in range(kv_heads):
                share_heads(h, zorder[0], q ^ zorder[0]).wait_recv()
        project(q)

    def share_squares(k):
        return remote(squares.at[0], squares.at[k], s_send.at[k], s_recv.at[k], target(k), "expert")

    leaving = [pltpu.make_async_copy(stream_ref, stream_any, out_local.at[experts])]
    leaving[0].start()
    stream = stream_ref[...]
    total = jnp.sum(stream * stream, axis=-1, keepdims=True)
    squares[0] = jnp.transpose(jnp.broadcast_to(total, (rows, 128)))[:8, :]
    for k in range(1, experts):
        share_squares(k).start()
    for k in range(1, experts):
        share_squares(k).wait_recv()
    total = squares[0]
    for k in range(1, experts):
        total = total + squares[k]
    total = jnp.transpose(jnp.broadcast_to(total[:1, :], (128, rows)))[:, :1]
    inverse = lax.rsqrt(total * (1.0 / (cols * experts)) + 1e-05)
    normed = (stream_ref[...] * inverse * gain_in[...]).astype(low)
    for k in range(experts):
        chosen_ref[k] = jnp.dot(place[target(k)], normed, preferred_element_type=wide).astype(low)
        leaving.append(pltpu.make_async_copy(chosen_ref.at[k], chosen_any.at[k], out_local.at[k]))
        leaving[-1].start()
    logit_ref[...] = lax.dot_general(
        router_in[...], normed, (((1,), (1,)), ((), ())), preferred_element_type=wide
    )
    for p in range(parts):
        for r in range(chips):
            kv_forward(p, r).wait_send()
            if r > 0:
                kv_spread(p, orders[p][0], r ^ orders[p][0]).wait_send()
    for p in range(0 if given else experts):
        for r in range(chips):
            w_forward(p, r).wait_send()
            if r > 0:
                w_spread(p, bits[0], r ^ bits[0]).wait_send()
    for h in range(kv_heads):
        for q in range(1, experts):
            share_heads(h, zorder[0], q ^ zorder[0]).wait_send()
    for k in range(1, experts):
        if not given:
            lend(k).wait_send()
        share_squares(k).wait_send()
    for copy in leaving:
        copy.wait()


def front(queries, keys, values, segments, routes_t, w_out, residual, gain, router, capacity):
    chips, experts = lax.axis_size("blk") // 2, lax.axis_size("expert")
    rows, cols = residual.shape
    depth = queries.shape[1]
    kv_heads = keys.shape[1] // HD
    pack = queries.shape[1] // keys.shape[1]
    low, wide = jnp.bfloat16, jnp.float32
    vmem, dma, shape = pl.BlockSpec(memory_space=pltpu.VMEM), pltpu.SemaphoreType.DMA, jax.ShapeDtypeStruct
    given = cols % (256 * chips) != 0
    if given:
        w_out = lax.all_to_all(w_out, "expert", 1, 0, tiled=True)
    w_shape = (1, depth * experts, cols) if given else (chips, depth * experts, cols // chips)
    return pl.pallas_call(
        functools.partial(front_kernel, chips, experts, given),
        out_shape=(
            shape((rows, cols), wide),
            shape((experts, capacity, cols), low),
            shape((router.shape[0], rows), wide),
            shape((capacity, rows), low),
        ),
        in_specs=[pl.BlockSpec(memory_space=pl.ANY)] * 9,
        out_specs=(pl.BlockSpec(memory_space=pl.ANY),) * 2 + (vmem,) * 2,
        scratch_shapes=[
            pltpu.VMEM((rows, cols), wide),
            pltpu.VMEM((experts, capacity, cols), low),
            pltpu.VMEM((2, chips, 2) + keys.shape, low),
            pltpu.VMEM(w_shape, low),
            pltpu.VMEM((experts, rows, depth), low),
            pltpu.VMEM((kv_heads, pack * rows, HD), low),
            pltpu.VMEM((kv_heads, pack * rows, HD), wide),
            pltpu.VMEM((kv_heads, pack * rows, HD), wide),
            pltpu.VMEM((kv_heads, pack * rows, HD), wide),
            pltpu.VMEM((experts, capacity, rows), low),
            pltpu.VMEM((experts, 8, rows), wide),
            pltpu.VMEM((rows, cols), low),
            pltpu.VMEM(segments.shape, jnp.int32),
            pltpu.VMEM(routes_t.shape, jnp.int32),
            pltpu.VMEM((1, cols), wide),
            pltpu.VMEM(router.shape, low),
            dma((8,)),
            dma((kv_heads, pack)),
            dma((experts + 1,)),
        ]
        + [dma((2, chips))] * 4
        + [dma((experts,))] * 2
        + [dma((experts, chips))] * 4
        + [dma((kv_heads, experts))] * 2
        + [dma((experts,))] * 2,
        compiler_params=pltpu.CompilerParams(
            collective_id=0, has_side_effects=True, vmem_limit_bytes=61 * 1024 * 1024
        ),
    )(queries, keys, values, segments, routes_t, w_out, residual, gain, router)


def expert_kernel(
    chips, experts, x_ref, wg_ref, wu_ref, wd_ref, stream_any, place_any, logit_any, rt_any, o_ref,
    rows_in, weights, hidden, leaving, sib_in, keep, part_in, own_out, strips, strip_in, scatter, share,
    stream_ref, place_ref, logit_ref, rt_ref,
    w_sem, d_sem, ag_send, ag_recv, fw_send, fw_recv, sib_send, sib_recv,
    rs_send, rs_recv, z_send, z_recv, x_send, x_recv, l_send, l_recv, small,
):
    me, group = lax.axis_index("blk"), lax.axis_index("expert")
    chip, core = me // 2, me % 2
    sibling = chip * 2 + 1 - core
    rows, width = x_ref.shape[1], x_ref.shape[2] * experts
    units = wg_ref.shape[1]
    tile = weights.shape[2]
    tiles = units // tile
    slots = 2 * tiles
    steps, zsteps = log2(chips), log2(experts)
    bits = [1 << b for b in range(steps)]
    zbits = [1 << b for b in range(zsteps)]
    parts = 2
    groups = 4
    orders = [bits[p % steps :] + bits[: p % steps] for p in range(parts)]
    tw = leaving.shape[2]
    pw = tw // parts
    total = width // tw
    per_tile = tw // tile
    piece = tw // experts
    subs = width // tile
    slab = width // experts
    own_rows = o_ref.shape[0]
    low = jnp.bfloat16

    def peer(bit):
        return flip(chip, bit) * 2 + core

    barrier = pltpu.get_barrier_semaphore()
    pl.semaphore_signal(barrier, inc=1, device_id={"blk": sibling}, device_id_type=MESH)
    for bit in bits:
        pl.semaphore_signal(barrier, inc=1, device_id={"blk": peer(bit)}, device_id_type=MESH)
    for e in range(1, experts):
        pl.semaphore_signal(barrier, inc=1, device_id={"expert": (group + e) % experts}, device_id_type=MESH)

    def load(f, side):
        src = (wg_ref, wu_ref)[side]
        return pltpu.make_async_copy(
            src.at[:, pl.ds(pl.multiple_of(f * tile, 128), tile)], weights.at[2 * f + side], w_sem.at[2 * f + side]
        )

    def load_down(m, i):
        column = (m % per_tile) * (tile // piece) + i
        column = column * slab + (m // per_tile) * piece
        slot = m % slots
        return pltpu.make_async_copy(
            wd_ref.at[:, pl.ds(pl.multiple_of(column, 128), piece)],
            weights.at[slot, pl.ds(0, units), pl.ds(i * piece, piece)],
            d_sem.at[slot, i],
        )

    cuts = [0]
    for p in range(groups):
        extra = p in (2, 3, 1)[: rows // 16 % groups]
        cuts.append(cuts[-1] + 16 * (rows // 16 // groups + extra))
    early, late = [0, 1], [2, 3]
    by_distance = sorted(range(1, chips), key=lambda r: (len(parts_of(r)), r))
    near = [r for r in by_distance if len(parts_of(r)) == 1]
    far = [r for r in by_distance if r not in near]
    units_of_work = [
        [(0, early)],
        [(r, early) for r in near],
        [(r, early) for r in far] + [(0, late)],
        [(r, late) for r in near],
        [(r, late) for r in far],
    ]
    units_of_work = [work for work in units_of_work if work]
    place_of, begins, count = {}, [], 0
    for work in units_of_work:
        begins.append(count)
        for r, which in work:
            for c in range(2):
                for p in which:
                    place_of[r, c, p] = count
                    count += cuts[p + 1] - cuts[p]
    begins.append(count)

    def lot(r, c, p):
        return rows_in.at[pl.ds(place_of[r, c, p], cuts[p + 1] - cuts[p]), :]

    def slab_of(g):
        return pl.ds(pl.multiple_of(g * slab, 128), slab)

    def dispatch(k, p, g):
        take_rows = pl.ds(cuts[p], cuts[p + 1] - cuts[p])
        put_rows = pl.ds(place_of[0, 0, p], cuts[p + 1] - cuts[p])
        source, goal = x_ref.at[k, take_rows, :], rows_in.at[put_rows, slab_of(g)]
        if k == 0:
            return pltpu.make_async_copy(source, goal, x_send.at[0, p])
        return remote(source, goal, x_send.at[k, p], x_recv.at[k, p], (group + k) % experts, "expert")

    def share_logits(k):
        if k == 0:
            return pltpu.make_async_copy(logit_any, logit_ref.at[0], l_send.at[0])
        return remote(logit_any, logit_ref.at[k], l_send.at[k], l_recv.at[k], (group + k) % experts, "expert")

    def order(p):
        return bits[p % steps :] + bits[: p % steps]

    def spread(p, bit, r):
        return remote(
            lot(r, 0, p), lot(r ^ bit, 0, p), ag_send.at[p, r ^ bit], ag_recv.at[p, r ^ bit], peer(bit)
        )

    def forward(p, r):
        return remote(lot(r, 0, p), lot(r, 1, p), fw_send.at[p, r], fw_recv.at[p, r], sibling)

    got = set()

    def take(p, r):
        if (p, r) in got:
            return
        got.add((p, r))
        if r == 0:
            dispatch(0, p, group).wait()
            for e in range(1, experts):
                dispatch(e, p, (group + experts - e) % experts).wait_recv()
            onward = order(p)
        else:
            bit = order(p)[0]
            spread(p, bit, r ^ bit).wait_recv()
            onward = order(p)[max(order(p).index(b) for b in parts_of(r)) + 1 :]
        for bit in onward:
            spread(p, bit, r).start()
        forward(p, r).start()

    def begin_dispatch(p):
        for e in range(experts - 1, -1, -1):
            dispatch(e, p, group).start()

    smalls = [
        pltpu.make_async_copy(stream_any, stream_ref, small.at[0]),
        pltpu.make_async_copy(place_any, place_ref, small.at[1]),
        pltpu.make_async_copy(rt_any, rt_ref, small.at[2]),
    ]
    pl.semaphore_wait(barrier, steps + experts)
    begin_dispatch(0)
    for e in range(experts):
        share_logits(e).start()
    for copy in smalls:
        copy.start()

    @pl.loop(0, tiles)
    def _(f):
        load(f, 0).start()
        load(f, 1).start()

    take(0, 0)
    begin_dispatch(1)

    for copy in smalls:
        copy.wait()
    share_logits(0).wait()
    for e in range(1, experts):
        share_logits(e).wait_recv()
    logit = logit_ref[0]
    for e in range(1, experts):
        logit = logit + logit_ref[e]
    tokens_here = rt_ref.shape[1]
    ids = lax.broadcasted_iota(jnp.int32, logit.shape, 0)
    routed = rt_ref[0:1, :] == ids
    for j in range(1, rt_ref.shape[0]):
        routed = routed | (rt_ref[j : j + 1, :] == ids)
    score = jnp.where(routed, 1.0 / (1.0 + jnp.exp(-logit)), 0.0)
    fraction = jnp.sum(jnp.where(ids == group, score, 0.0), axis=0, keepdims=True) / jnp.sum(
        score, axis=0, keepdims=True
    )
    share[...] = jnp.transpose(jnp.broadcast_to(fraction, (128, tokens_here)))
    take(1, 0)
    begin_dispatch(2)
    begin_dispatch(3)

    def up_tiles(u, begin, end):
        size = begins[u + 1] - begins[u]

        def body(f):
            if u == 0:
                load(f, 0).wait()
                load(f, 1).wait()
            tokens = rows_in[begins[u] : begins[u + 1], :]
            gate = jnp.dot(tokens, weights[2 * f], preferred_element_type=jnp.float32)
            up = jnp.dot(tokens, weights[2 * f + 1], preferred_element_type=jnp.float32)
            act = (gate / (1.0 + jnp.exp(-gate)) * up).astype(low)
            at = pl.ds(pl.multiple_of(f * tile, 128), tile)
            for r, which in units_of_work[u]:
                for c in range(2):
                    start = place_of[r, c, which[0]] - begins[u]
                    length = cuts[which[-1] + 1] - cuts[which[0]]
                    to = r * rows + cuts[which[0]]
                    hidden[c, to : to + length, at] = act[start : start + length]
            if u == len(units_of_work) - 1:
                for side in range(2):
                    m = 2 * f + side

                    @pl.when(m < subs)
                    def _():
                        for i in range(tile // piece):
                            load_down(m, i).start()

        pl.loop(begin, end, unroll=1)(body)

    middle = tiles // 2
    for u, work in enumerate(units_of_work):
        for r, which in work:
            for p in which:
                take(p, r)
        for r, which in work:
            for p in which:
                forward(p, r).wait_recv()
        up_tiles(u, 0, middle)
        if u == 1:
            take(2, 0)
            take(3, 0)
        if u == 2:
            for r in near:
                take(2, r)
        if u == 3:
            for r in far:
                take(2, r)
        up_tiles(u, middle, tiles)

    moves = []
    for t in range(steps):
        step = []
        for p in range(parts):
            for i, left in enumerate(span(orders[p][t + 1 :])):
                step.append((p, left | orders[p][t], left, i))
        moves.append(step)
    base = [sum(len(s) for s in moves[:t]) for t in range(steps)]
    zmoves = [[(left | zbits[u], left) for left in span(zbits[u + 1 :])] for u in range(zsteps)]
    zbase = [sum(len(s) for s in zmoves[:u]) for u in range(zsteps)]

    def exchange(n):
        return remote(leaving.at[n % 2], sib_in.at[n], sib_send.at[n], sib_recv.at[n], sibling)

    def block(r):
        return pl.ds(r * rows, rows)

    def deliver(n, t, k):
        p, sent, _, _ = moves[t][k]
        at = base[t] + k
        return remote(
            sib_in.at[n, block(sent), pl.ds(p * pw, pw)], part_in.at[n, at],
            rs_send.at[n, at], rs_recv.at[n, at], peer(orders[p][t]),
        )

    def hand(n, u, k):
        sent, _ = zmoves[u][k]
        at = zbase[u] + k
        return remote(
            strips.at[n, sent - 1], strip_in.at[n, at], z_send.at[n, at], z_recv.at[n, at],
            flip(group, zbits[u]), "expert",
        )

    def down(c, n, i):
        slot = (n * per_tile + i) % slots
        return jnp.dot(hidden[c], weights[slot, :units, :], preferred_element_type=jnp.float32)

    def leave(n):
        for i in range(per_tile):
            for j in range(tile // piece):
                load_down(n * per_tile + i, j).wait()

        @pl.when(n >= 2)
        def _():
            exchange(n - 2).wait_send()

        for i in range(per_tile):
            leaving[n % 2, :, i * tile : (i + 1) * tile] = down(1, n, i).astype(low)
        exchange(n).start()

    def stay(n):
        for i in range(per_tile):
            keep[:, i * tile : (i + 1) * tile] = down(0, n, i)
        for i in range(per_tile):
            m = n * per_tile + i + slots

            @pl.when(m < subs)
            def _():
                for j in range(tile // piece):
                    load_down(m, j).start()

    def join(n):
        exchange(n).wait_recv()
        sib_in[n] = (keep[...] + sib_in[n].astype(jnp.float32)).astype(low)
        for k in range(len(moves[0])):
            deliver(n, 0, k).start()

    def gather_step(n, t):
        for k, (p, _, left, _) in enumerate(moves[t]):
            deliver(n, t, k).wait_recv()
            at = (block(left), pl.ds(p * pw, pw))
            mine = sib_in[n, at[0], at[1]].astype(jnp.float32)
            sib_in[n, at[0], at[1]] = (mine + part_in[n, base[t] + k].astype(jnp.float32)).astype(low)
        if t + 1 < steps:
            for k in range(len(moves[t + 1])):
                deliver(n, t + 1, k).start()
        else:
            mix = share[:, :1] * lax.dot_general(
                place_ref[...], sib_in[n, :rows, :], (((0,), (0,)), ((), ())), preferred_element_type=jnp.float32
            )
            column = pl.ds(pl.multiple_of(n * piece, 128), piece)
            scatter[...] = mix
            mine = pl.ds(pl.multiple_of(group * piece, 128), piece)
            scatter[:, mine] += stream_ref[:, column]
            for q in range(experts):
                start = across(group, parts_of(q)) * own_rows
                strip = scatter[pl.ds(pl.multiple_of(start, own_rows), own_rows), :]
                if q == 0:
                    own_out[n] = strip
                else:
                    strips[n, q - 1] = strip.astype(low)
            for k in range(len(zmoves[0])):
                hand(n, 0, k).start()

    def combine_step(n, u):
        for k, (_, left) in enumerate(zmoves[u]):
            hand(n, u, k).wait_recv()
            theirs = strip_in[n, zbase[u] + k].astype(jnp.float32)
            if left == 0:
                own_out[n] += theirs
            else:
                strips[n, left - 1] = (strips[n, left - 1].astype(jnp.float32) + theirs).astype(low)
        if u + 1 < zsteps:
            for k in range(len(zmoves[u + 1])):
                hand(n, u + 1, k).start()
        else:
            column = n * piece
            for g in range(experts):
                at = pl.ds(pl.multiple_of(g * slab + column, 128), piece)
                o_ref[:, at] = own_out[n, :, g * piece : (g + 1) * piece].astype(o_ref.dtype)

    lag = steps + zsteps

    @pl.loop(0, total + lag)
    def _(n):
        @pl.when(n < total)
        def _():
            leave(n)

            stay(n)
            join(n)

        for t in range(steps):
            @pl.when((n >= 1 + t) & (n - 1 - t < total))
            def _():
                gather_step(n - 1 - t, t)

        for u in range(zsteps):
            @pl.when((n >= 1 + steps + u) & (n - 1 - steps - u < total))
            def _():
                combine_step(n - 1 - steps - u, u)

    for n in range(max(0, total - 2), total):
        exchange(n).wait_send()
    for e in range(1, experts):
        share_logits(e).wait_send()
        for p in range(groups):
            dispatch(e, p, group).wait_send()
    for p in range(groups):
        for r in range(chips):
            forward(p, r).wait_send()
            if r > 0:
                spread(p, order(p)[0], r ^ order(p)[0]).wait_send()

    @pl.loop(0, total)
    def _(n):
        for t in range(steps):
            for k in range(len(moves[t])):
                deliver(n, t, k).wait_send()
        for u in range(zsteps):
            for k in range(len(zmoves[u])):
                hand(n, u, k).wait_send()


def expert_layer(x, gate_w, up_w, down_w, stream, place, logits, routes_t):
    chips, experts = lax.axis_size("blk") // 2, lax.axis_size("expert")
    rows, width = x.shape[1], x.shape[2] * experts
    units = gate_w.shape[1]
    tile = 256 if units % 256 == 0 else 128
    tokens = stream.shape[0]
    tw = 128 * experts
    total = width // tw
    dma = pltpu.SemaphoreType.DMA
    low, wide = jnp.bfloat16, jnp.float32
    vmem = pl.BlockSpec(memory_space=pltpu.VMEM)
    anywhere = pl.BlockSpec(memory_space=pl.ANY)
    own_rows = tokens // experts
    slots = 2 * (units // tile)
    moved = 2 * (chips - 1)
    return pl.pallas_call(
        functools.partial(expert_kernel, chips, experts),
        out_shape=jax.ShapeDtypeStruct((own_rows, width), low),
        in_specs=[anywhere] * 8,
        out_specs=vmem,
        scratch_shapes=[
            pltpu.VMEM((2 * chips * rows, width), low),
            pltpu.VMEM((slots, width, tile), low),
            pltpu.VMEM((2, chips * rows, units), low),
            pltpu.VMEM((2, chips * rows, tw), low),
            pltpu.VMEM((total, chips * rows, tw), low),
            pltpu.VMEM((chips * rows, tw), wide),
            pltpu.VMEM((total, moved, rows, tw // 2), low),
            pltpu.VMEM((total, own_rows, tw), wide),
            pltpu.VMEM((total, experts - 1, own_rows, tw), low),
            pltpu.VMEM((total, experts - 1, own_rows, tw), low),
            pltpu.VMEM((tokens, tw), wide),
            pltpu.VMEM((tokens, 128), wide),
            pltpu.VMEM(stream.shape, wide),
            pltpu.VMEM(place.shape, low),
            pltpu.VMEM((experts,) + logits.shape, wide),
            pltpu.VMEM(routes_t.shape, jnp.int32),
            dma((slots,)),
            dma((slots, tile // 128)),
            dma((4, chips)),
            dma((4, chips)),
            dma((4, chips)),
            dma((4, chips)),
            dma((total,)),
            dma((total,)),
            dma((total, moved)),
            dma((total, moved)),
            dma((total, experts - 1)),
            dma((total, experts - 1)),
            dma((experts, 4)),
            dma((experts, 4)),
            dma((experts,)),
            dma((experts,)),
            dma((3,)),
        ],
        compiler_params=pltpu.CompilerParams(
            collective_id=1, has_side_effects=True, vmem_limit_bytes=61 * 1024 * 1024
        ),
    )(x, gate_w, up_w, down_w, stream, place, logits, routes_t)


def on_device(
    residual,
    queries,
    key_cache,
    value_cache,
    segments,
    routes,
    w_out,
    norm_gain,
    w_router,
    w_gate,
    w_up,
    w_down,
):
    experts = w_router.shape[1]
    cols = residual.shape[1]
    first_col = lax.axis_index("expert") * cols
    capacity = queries.shape[0] * TOP * 9 // (8 * experts)
    capacity = -(-capacity // 16) * 16
    router = lax.dynamic_slice_in_dim(w_router, first_col, cols, 0).T
    router = jnp.pad(router, ((0, -experts % 16), (0, 0)))
    routes_t = routes.T
    stream, chosen, logits, place = front(
        queries, key_cache, value_cache, segments[None, :], routes_t, w_out, residual, norm_gain[None, :], router, capacity
    )
    return expert_layer(chosen, w_gate[0], w_up[0], w_down[0], stream, place, logits, routes_t)


def solution(mesh):
    return jax.shard_map(
        on_device,
        mesh=mesh,
        in_specs=(
            P("blk", "expert"),
            P("blk", "expert"),
            P("blk", "expert"),
            P("blk", "expert"),
            P(),
            P("blk", None),
            P("expert", None),
            P(),
            P(),
            P("expert", None, "blk"),
            P("expert", None, "blk"),
            P("expert", "blk", None),
        ),
        out_specs=P(("blk", "expert"), None),
        check_vma=False,
    )
```
